32 devices in a mesh: dp: 8 (over z, x), seq: 4 (over y, core).
Axes of the slice: x: 2, y: 2, z: 4, core: 2. Of those that a mesh axis runs over, the one named last changes fastest.
Arguments:
- tokens: bfloat16 [2, 8, 2048, 768], P(None, 'dp', 'seq'), may hold values from -6 to 6
- qkv_weight: bfloat16 [768, 2304], P(('dp', 'seq')), may hold values from -0.21875 to 0.21875
- query_bias: bfloat16 [768], P(('dp', 'seq')), may hold values from -1.796875 to 1.796875
- value_bias: bfloat16 [768], P(('dp', 'seq')), may hold values from -1.796875 to 1.796875
- proj_weight: bfloat16 [768, 768], P(('dp', 'seq')), may hold values from -0.875 to 0.875
- proj_bias: bfloat16 [768], P(('dp', 'seq')), may hold values from -1.796875 to 1.796875
- attn_gain: bfloat16 [768], P(('dp', 'seq')), may hold values from 0.5 to 1.5
- attn_shift: bfloat16 [768], P(('dp', 'seq')), may hold values from -1.796875 to 1.796875
- inner_weight: bfloat16 [768, 3072], P(('dp', 'seq')), may hold values from -0.21875 to 0.21875
- inner_bias: bfloat16 [3072], P(('dp', 'seq')), may hold values from -1.796875 to 1.796875
- down_weight: bfloat16 [3072, 768], P(('dp', 'seq')), may hold values from -0.109375 to 0.109375
- down_bias: bfloat16 [768], P(('dp', 'seq')), may hold values from -1.796875 to 1.796875
- ffn_gain: bfloat16 [768], P(('dp', 'seq')), may hold values from 0.5 to 1.5
- ffn_shift: bfloat16 [768], P(('dp', 'seq')), may hold values from -1.796875 to 1.796875
- seg_ids: int32 [2, 8, 2048], P(None, 'dp'), may hold values from 0 to 3, never falling along the last dimension, each value on 1 to 1024 neighbouring positions
- rand_blocks: int32 [2, 8, 12, 32, 3], P(None, 'dp', 'seq'), may hold values from 0 to 31
- glob_blocks: int32 [2, 8, 2], P(None, 'dp'), may hold values from 0 to 31, as said below
- d_out: bfloat16 [2, 8, 2048, 768], P(None, 'dp', 'seq'), may hold values from -6 to 6
Outputs:
- layer_out: bfloat16 [2, 8, 2048, 768], P(None, 'dp', 'seq')
- grad_input: bfloat16 [2, 8, 2048, 768], P(None, 'dp', 'seq')
- grad_qkv_weight: float32 [768, 2304], P(('dp', 'seq'))
- grad_query_bias: float32 [768], P(('dp', 'seq'))
- grad_value_bias: float32 [768], P(('dp', 'seq'))
- grad_proj_weight: float32 [768, 768], P(('dp', 'seq'))
- grad_proj_bias: float32 [768], P(('dp', 'seq'))
- grad_attn_gain: float32 [768], P(('dp', 'seq'))
- grad_attn_shift: float32 [768], P(('dp', 'seq'))
- grad_inner_weight: float32 [768, 3072], P(('dp', 'seq'))
- grad_inner_bias: float32 [3072], P(('dp', 'seq'))
- grad_down_weight: float32 [3072, 768], P(('dp', 'seq'))
- grad_down_bias: float32 [768], P(('dp', 'seq'))
- grad_ffn_gain: float32 [768], P(('dp', 'seq'))
- grad_ffn_shift: float32 [768], P(('dp', 'seq'))
The draws below stay inside these ranges and needn't reach their ends.
Inputs may be any that keep to these rules, and one draw needn't show every extreme that they name: `seg_ids`: document numbers never fall along a sequence; each document holds at most 1024 tokens, and one holds exactly that many. `rand_blocks`: block numbers of the whole sequence. `glob_blocks`: the two global blocks of a sequence are different.
All inputs are finite; a program needn't handle non-finite values.
Results may differ from the reference program's by a relative error of at most 0.015.
Values may be sent and summed in bfloat16 or wider, within the bound.
No kernel may reach another device: no remote copies, remote signals or barrier semaphores. Data moves between devices by JAX's collectives and lax.ppermute only.
A program may use at most 256 MiB of HBM per device.

```python
import math
import jax
import jax.numpy as jnp
import numpy as np
from jax import lax

D = 768
H = 12
HD = 64
FF = 3072
BLOCK = 64
RAND = 3
MICRO = 2
DOCS = 4
LENGTH = 2048
SEQS = 8
NB = 32


def draw_glob_blocks(key, part):
    first_key, second_key = jax.random.split(jax.random.fold_in(key, 7))
    block_total = LENGTH // BLOCK
    leading = jax.random.randint(first_key, (MICRO, SEQS, 1), 0, block_total)
    offset = jax.random.randint(second_key, (MICRO, SEQS, 1), 1, block_total)
    return jnp.concatenate([leading, (leading + offset) % block_total], axis=2).astype(jnp.int32)


def plant(array, stream_key, low, largest):
    shape = array.shape
    index_at = [jax.random.randint(jax.random.fold_in(stream_key, axis), (), 0, shape[axis]) for axis in range(len(shape))]
    array = array.at[tuple(index_at)].set(low)
    longest = shape.index(max(shape))
    index_at[longest] = (index_at[longest] + 1) % shape[longest]
    return array.at[tuple(index_at)].set(largest)


def strengthened(entries, own_key, source, target, parts, factor):
    def block_of(dim):
        return (jnp.arange(entries.shape[dim]) // (entries.shape[dim] // parts)).reshape((-1,) + (1,) * (entries.ndim - 1 - dim))

    one_side = jax.random.permutation(own_key, parts)[block_of(target)]
    far = (block_of(target) + parts // 2) % parts
    return jnp.where((block_of(source) == one_side) | (block_of(source) == far), factor * entries, entries)


def block_scale(rng, extent, cuts, least, top_value):
    level, own = 1.0, jax.random.fold_in(rng, 6)
    for dim, blocks in cuts:
        heights = jnp.exp(jax.random.uniform(jax.random.fold_in(own, dim), (blocks,), jnp.float32, least / len(cuts), top_value / len(cuts)))
        level = level * jnp.repeat(heights, extent[dim] // blocks).reshape([-1 if axis == dim else 1 for axis in range(len(extent))])
    return level


def profile(count, total, reach, skew):
    portions = [(1 << 20) // math.isqrt(grade ** skew) + 1 for grade in range(2, count + 1)]
    surplus, holding = total - reach - (count - 1), [1] * (count - 1)
    while surplus > 0:
        candidates = [i for i in range(count - 1) if holding[i] < reach]
        pool, remaining = sum([portions[i] for i in candidates]), surplus
        for i in candidates:
            addition = min(reach - holding[i], max(1, remaining * portions[i] // pool), surplus)
            holding[i] = holding[i] + addition
            surplus = surplus - addition
    return np.array([reach] + holding)


def uneven_parts(stream_key, amount, total, limit, skew):
    if amount == 2:
        one = jax.random.randint(stream_key, (), max(1, total - limit), min(limit, total - 1) + 1)
        return jnp.stack([one, total - one])
    sizes = jnp.asarray(profile(amount, total, limit, skew), jnp.int32)
    twos = (amount - 1) // 2
    giver, sink = sizes[1:1 + 2 * twos:2], sizes[2:2 + 2 * twos:2]
    slack = jnp.minimum(giver - 1, limit - sink)
    passed = jax.random.randint(jax.random.fold_in(stream_key, 1), (twos,), 0, 1 << 20) % (slack + 1)
    sizes = sizes.at[1:1 + 2 * twos:2].set(giver - passed).at[2:2 + 2 * twos:2].set(sink + passed)
    return sizes[jax.random.permutation(jax.random.fold_in(stream_key, 2), amount)]


def gaussian(own_key, extent, width, bound, pieces=(), kind=jnp.bfloat16):
    level = block_scale(own_key, extent, pieces, -0.22, 0.18) if pieces else 1.0
    entries = jax.random.normal(own_key, extent, jnp.float32) * width * level
    return jnp.minimum(jnp.maximum(entries, -bound), bound).astype(kind)


def bell_draw_with(key, dims, spread, bound, cuts, heavy, kind=jnp.bfloat16):
    entries = spread * jax.random.normal(key, dims, jnp.float32)
    if cuts:
        entries = entries * block_scale(key, dims, cuts, -0.22, 0.18)
    return jnp.clip(strengthened(entries, jax.random.fold_in(key, 3), *heavy), -bound, bound).astype(kind)


def setup_inputs(seed: int = 0) -> dict:
    key_list = jax.random.split(jax.random.key(seed), 19)
    tokens = bell_draw_with(key_list[0], (MICRO, SEQS, LENGTH, D), 1.0, 6.0, ((1, 8), (2, 4)), (1, 3, 8, 2.0))
    qkv_weight = gaussian(key_list[1], (D, 3 * D), D ** -0.5, 0.21875, ((0, 32),))
    query_bias = gaussian(key_list[2], (D,), 0.3, 1.796875, ((0, 32),))
    value_bias = gaussian(key_list[3], (D,), 0.3, 1.796875, ((0, 32),))
    proj_weight = gaussian(key_list[4], (D, D), (D // 16) ** -0.5, 0.875, ((0, 32),))
    proj_bias = gaussian(key_list[5], (D,), 0.3, 1.796875, ((0, 32),))
    attn_gain = jnp.clip(1.0 + 0.1 * jax.random.normal(key_list[6], (D,), jnp.float32), 0.5, 1.5).astype(jnp.bfloat16)
    attn_shift = gaussian(key_list[7], (D,), 0.3, 1.796875, ((0, 32),))
    inner_weight = gaussian(key_list[8], (D, FF), D ** -0.5, 0.21875, ((0, 32),))
    inner_bias = gaussian(key_list[9], (FF,), 0.3, 1.796875, ((0, 32),))
    down_weight = gaussian(key_list[10], (FF, D), FF ** -0.5, 0.109375, ((0, 32),))
    down_bias = gaussian(key_list[11], (D,), 0.3, 1.796875, ((0, 32),))
    ffn_gain = jnp.clip(1.0 + 0.1 * jax.random.normal(key_list[12], (D,), jnp.float32), 0.5, 1.5).astype(jnp.bfloat16)
    ffn_shift = gaussian(key_list[13], (D,), 0.3, 1.796875, ((0, 32),))
    seg_ids = jax.vmap(lambda own: jnp.searchsorted(jnp.cumsum(uneven_parts(own, DOCS, LENGTH, LENGTH // 2, 2)), jnp.arange(LENGTH), side="right"))(jax.random.split(key_list[14], MICRO * SEQS)).reshape((MICRO, SEQS, LENGTH)).astype(jnp.int32)
    rand_blocks = plant(jax.random.randint(key_list[15], (MICRO, SEQS, H, NB, RAND), 0, NB), jax.random.fold_in(key_list[15], 1), 0, NB - 1).astype(jnp.int32)
    glob_blocks = draw_glob_blocks(jax.random.fold_in(key_list[18], 71), 0)
    d_out = bell_draw_with(key_list[17], (MICRO, SEQS, LENGTH, D), 1.0, 6.0, ((1, 8), (2, 4)), (1, 3, 8, 2.0))
    return dict(tokens=tokens, qkv_weight=qkv_weight, query_bias=query_bias, value_bias=value_bias, proj_weight=proj_weight, proj_bias=proj_bias, attn_gain=attn_gain, attn_shift=attn_shift, inner_weight=inner_weight, inner_bias=inner_bias, down_weight=down_weight, down_bias=down_bias, ffn_gain=ffn_gain, ffn_shift=ffn_shift, seg_ids=seg_ids, rand_blocks=rand_blocks, glob_blocks=glob_blocks, d_out=d_out)


EPSILON = 1e-06

@jax.custom_vjp
def low(v):
    return lax.optimization_barrier(v.astype(jnp.bfloat16)).astype(jnp.float32)

@jax.custom_vjp
def low_back(v):
    return v

def low_keep(v):
    return (low(v), None)

def low_pass(kept, grad):
    return (grad,)

def back_keep(v):
    return (v, None)

def back_low(kept, grad):
    return (low(grad),)
low.defvjp(low_keep, low_pass)
low_back.defvjp(back_keep, back_low)

def product(left, right):
    return jnp.dot(left, right, precision=lax.Precision.HIGHEST, preferred_element_type=jnp.float32)

def layer_norm(value, gain, shift):
    centred = value - lax.optimization_barrier(jnp.mean(value, axis=-1, keepdims=True))
    normed = centred * lax.rsqrt(lax.optimization_barrier(jnp.mean(centred * centred, axis=-1, keepdims=True)) + EPSILON)
    return normed * gain + shift

def attention(queries, key_rows, value_rows, segment, table, globals_pair):
    length = queries.shape[0]
    block_count = length // BLOCK
    blocks = jnp.arange(block_count, dtype=jnp.int32)
    nearby = jnp.abs(blocks[:, None] - blocks[None, :]) <= 1
    global_keys = (blocks[None, :] == globals_pair[0]) | (blocks[None, :] == globals_pair[1])
    global_rows = (blocks[:, None] == globals_pair[0]) | (blocks[:, None] == globals_pair[1])
    picked = jnp.any(table[:, :, :, None] == blocks[None, None, None, :], axis=2)
    allowed = (nearby | global_keys | global_rows)[None] | picked
    rows = min(512, length)
    step_count = length // rows
    token_block = jnp.arange(length, dtype=jnp.int32) // BLOCK
    score_scale = HD ** (-0.5)

    def one_head(head_q, head_k, head_v, allow):

        def part(number):
            first = (number * rows).astype(jnp.int32)
            query_rows = lax.dynamic_slice_in_dim(head_q, first, rows, 0)
            query_segs = lax.dynamic_slice_in_dim(segment, first, rows, 0)
            query_blocks = lax.dynamic_slice_in_dim(token_block, first, rows, 0)
            visible = allow[query_blocks][:, token_block] & (query_segs[:, None] == segment[None, :])
            scores = low_back(product(query_rows, head_k.T) * score_scale)
            scores = jnp.where(visible, scores, -1e+30)
            weights = jax.nn.softmax(scores, axis=-1)
            return product(low(weights), head_v)
        return lax.map(jax.checkpoint(part), jnp.arange(step_count, dtype=jnp.int32)).reshape(length, -1)
    result = jax.vmap(one_head, in_axes=(1, 1, 1, 0))(queries, key_rows, value_rows, allowed)
    return result.transpose(1, 0, 2).reshape(length, -1)

def layer(params, tokens, segment, table, globals_pair):
    qkv_weight, query_bias, value_bias, proj_weight, proj_bias, attn_gain, attn_shift, inner_weight, inner_bias, down_weight, down_bias, ffn_gain, ffn_shift = params
    length = tokens.shape[0]
    bias_all = jnp.concatenate([query_bias, jnp.zeros_like(query_bias), value_bias])
    qkv = low(low_back(product(low(tokens), qkv_weight) + bias_all))
    queries = qkv[:, :D].reshape(length, H, HD)
    key_rows = qkv[:, D:2 * D].reshape(length, H, HD)
    value_rows = qkv[:, 2 * D:].reshape(length, H, HD)
    context = attention(queries, key_rows, value_rows, segment, table, globals_pair)
    context = low(low_back(context))
    attn = low_back(product(context, proj_weight) + proj_bias)
    first_out = layer_norm(tokens + attn, attn_gain, attn_shift)
    pre = low_back(product(low(first_out), inner_weight) + inner_bias)
    hidden = low(jax.nn.gelu(pre, approximate=False))
    ffn = low_back(product(hidden, down_weight) + down_bias)
    return layer_norm(first_out + ffn, ffn_gain, ffn_shift)

def reference(tokens, qkv_weight, query_bias, value_bias, proj_weight, proj_bias, attn_gain, attn_shift, inner_weight, inner_bias, down_weight, down_bias, ffn_gain, ffn_shift, seg_ids, rand_blocks, glob_blocks, d_out):
    params = tuple((item.astype(jnp.float32) for item in (qkv_weight, query_bias, value_bias, proj_weight, proj_bias, attn_gain, attn_shift, inner_weight, inner_bias, down_weight, down_bias, ffn_gain, ffn_shift)))
    total = MICRO * SEQS
    inputs = tokens.astype(jnp.float32).reshape(total, LENGTH, D)
    cotangents = d_out.astype(jnp.float32).reshape(total, LENGTH, D)
    segments = seg_ids.reshape(total, LENGTH)
    tables = rand_blocks.reshape(total, H, NB, RAND)
    globals_all = glob_blocks.reshape(total, 2)

    def step(carry, item):
        source, segment, table, globals_pair, cotangent = item
        output, pull = jax.vjp(lambda weights, value: layer(weights, value, segment, table, globals_pair), params, source)
        weight_grads, input_grad = pull(cotangent)
        carry = jax.tree.map(jnp.add, carry, weight_grads)
        return (carry, (output.astype(jnp.bfloat16), input_grad.astype(jnp.bfloat16)))
    zeros = tuple((jnp.zeros_like(item) for item in params))
    grads, (outputs, input_grads) = lax.scan(step, zeros, (inputs, segments, tables, globals_all, cotangents))
    shape = (MICRO, SEQS, LENGTH, D)
    return (outputs.reshape(shape), input_grads.reshape(shape), grads[0], grads[1], grads[2], grads[3], grads[4], grads[5], grads[6], grads[7], grads[8], grads[9], grads[10], grads[11], grads[12])
```

```python
import jax
import jax.numpy as jnp
from jax import lax
from jax.experimental import pallas as pl
from jax.experimental.pallas import tpu as pltpu
from jax.sharding import PartitionSpec as P

HD = 64
BLOCK = 64
EPSILON = 1e-06
BIG = float(2.0**100)
LOWEST = -3.0e38
TQ = 256
TK = 512
CHIPS = 16
TILE = 256
BF = jnp.bfloat16
F32 = jnp.float32
VMEM_LIMIT = 60 << 20


def nn(left, right):
    return lax.dot_general(left, right, (((1,), (0,)), ((), ())), preferred_element_type=F32)


def nt(left, right):
    return lax.dot_general(left, right, (((1,), (1,)), ((), ())), preferred_element_type=F32)


def tn(left, right):
    return lax.dot_general(left, right, (((0,), (0,)), ((), ())), preferred_element_type=F32)


def smem():
    return pl.BlockSpec(memory_space=pltpu.SMEM)


def anywhere():
    return pl.BlockSpec(memory_space=pl.ANY)


def shape(dims, kind):
    return jax.ShapeDtypeStruct(dims, kind)


def swap(value, dim):
    bit = 1 if dim == "core" else 2
    return lax.ppermute(value, "seq", [(s, s ^ bit) for s in range(4)])


DIMS = {"x": (1, 2), "z": (2, 4)}


def shift(value, dim, by):
    stride, size = DIMS[dim]
    pairs = []
    for d in range(lax.axis_size("dp")):
        at = d // stride % size
        pairs.append((d, d + ((at + by) % size - at) * stride))
    return lax.ppermute(value, "dp", pairs)


def extent(dim):
    return 2 if dim == "y" else DIMS[dim][1]


def others(value, dim):
    if dim == "y":
        return [swap(value, "y")]
    return [shift(value, dim, by) for by in range(1, extent(dim))]


def gather(chunk, order):
    current = chunk[None]
    for dim in order[:-1]:
        current = jnp.concatenate([current] + others(current, dim), axis=0)
    return [current] + others(current, order[-1])


def scatter_sum(pieces, order):
    for step, dim in enumerate(order):
        total = pieces[0].astype(F32)
        for r in range(1, extent(dim)):
            if dim == "y":
                came = swap(pieces[r], "y")
            else:
                came = shift(pieces[r], dim, extent(dim) - r)
            total = total + came.astype(F32)
        if step + 1 < len(order):
            ways = extent(order[step + 1])
            total = total.astype(BF).reshape((ways, -1) + total.shape[1:])
            pieces = [total[r] for r in range(ways)]
    return total[0]


def chip_at(order, piece, index, here):
    rel = {order[-1]: piece}
    for dim in order[:-1]:
        rel[dim] = index % extent(dim)
        index //= extent(dim)
    z = lax.rem(here["z"] - rel["z"] + 4, 4)
    x = lax.rem(here["x"] + rel["x"], 2)
    y = lax.rem(here["y"] + rel["y"], 2)
    return z * 4 + x * 2 + y


def placed(meta):
    return {"c": meta[0], "x": meta[1], "y": meta[2], "z": meta[3]}


class Plan:
    def __init__(self, parts):
        self.parts = parts

    def counts(self):
        return [1 if order is None else extent(order[-1]) for _, _, order in self.parts]

    def entries(self):
        return sum(
            CHIPS for _ in self.parts
        )

    def walk(self, here):
        number = 0
        for (first, end, order), count in zip(self.parts, self.counts()):
            for p in range(count):
                for m in range(CHIPS // count):
                    chip = m if order is None else chip_at(order, p, m, here)
                    yield number + p, m, chip, first, end
            number += count


def qkv_kernel(plan, pieces_n, *refs):
    meta = refs[0]
    pieces = refs[1 : 1 + pieces_n]
    x_ref, bias_ref, out_ref, w_ref, sems = refs[1 + pieces_n :]
    here = placed(meta)
    width = w_ref.shape[2]
    depth = w_ref.shape[1] // 3

    @pl.when(pl.program_id(0) == 0)
    def _():
        copies = []
        for i, (p, m, chip, first, end) in enumerate(plan.walk(here)):
            copies.append(
                pltpu.make_async_copy(pieces[p].at[m], w_ref.at[chip, first:end, :], sems.at[i])
            )
        for copy in copies:
            copy.start()
        for copy in copies:
            copy.wait()

    x = x_ref[...]
    for w in range(3):
        weight = w_ref[:, depth * w : depth * w + depth, :].reshape(CHIPS * depth, width)
        cols = slice(width * w, width * w + width)
        out_ref[:, cols] = (nn(x, weight) + bias_ref[0:1, cols]).astype(BF)


def project_qkv(plan, meta, pieces, x_full, bias):
    rows, model = x_full.shape
    wide = bias.shape[1]
    width, depth = wide // 3, model // CHIPS
    tile = 512
    return pl.pallas_call(
        lambda *refs: qkv_kernel(plan, len(pieces), *refs),
        grid=(rows // tile,),
        in_specs=[smem()]
        + [anywhere()] * len(pieces)
        + [pl.BlockSpec((tile, model), lambda i: (i, 0)), pl.BlockSpec((1, wide), lambda i: (0, 0))],
        out_specs=[
            pl.BlockSpec((tile, wide), lambda i: (i, 0)),
            pl.BlockSpec((CHIPS, 3 * depth, width), lambda i: (0, 0, 0)),
        ],
        out_shape=[shape((rows, wide), BF), shape((CHIPS, 3 * depth, width), BF)],
        scratch_shapes=[pltpu.SemaphoreType.DMA((plan.entries(),))],
        compiler_params=pltpu.CompilerParams(vmem_limit_bytes=VMEM_LIMIT),
        cost_estimate=pl.CostEstimate(
            flops=2 * rows * model * wide, bytes_accessed=2 * rows * (model + wide), transcendentals=0
        ),
        name="project_qkv",
    )(meta, *pieces, x_full, bias)


def fill_features(seg_ref, rand_ref, first_global, second_global, key_ref, query_ref):
    heads, _, length = key_ref.shape
    blocks = length // BLOCK
    at = lax.broadcasted_iota(jnp.int32, (blocks, length), 1) // BLOCK
    row = lax.broadcasted_iota(jnp.int32, (blocks, length), 0)
    seen = jnp.abs(at - row) <= 1
    for chosen in (first_global, second_global):
        seen = seen | (at == chosen) | (row == chosen)
    same = lax.broadcasted_iota(jnp.int32, (HD - blocks, length), 0) == seg_ref[...]
    for h in range(heads):
        picked = seen
        for r in range(rand_ref.shape[2]):
            picked = picked | (at == rand_ref[h, :, r : r + 1])
        key_ref[h, 0:blocks, :] = jnp.where(picked, 0.0, 1.0).astype(BF)
        key_ref[h, blocks:HD, :] = jnp.where(same, 0.0, 1.0).astype(BF)
    query_ref[0:blocks, :] = jnp.where(at == row, -BIG, 0.0).astype(BF)
    query_ref[blocks:HD, :] = jnp.where(same, -BIG, 0.0).astype(BF)


def widen_pair(p, q_ref, k_ref, key_feat, query_feat, key_wide, query_wide):
    cols = slice(128 * p, 128 * p + 128)
    scaled = q_ref[:, cols] * BF(HD**-0.5)
    queries, keys = scaled.T, k_ref[:, cols].T
    a, b = 2 * p, 2 * p + 1
    query_wide[a, 0:HD, :] = queries[0:HD]
    query_wide[a, HD:128, :] = query_feat[...]
    query_wide[b, 0:HD, :] = query_feat[...]
    query_wide[b, HD:128, :] = queries[HD:128]
    key_wide[a] = jnp.concatenate([keys[0:HD], key_feat[a]], axis=0).T
    key_wide[b] = jnp.concatenate([key_feat[b], keys[HD:128]], axis=0).T
    return scaled, keys


def attend_kernel(meta, lo_ref, n_ref, glob_ref, q_ref, k_ref, v_ref, seg_ref, rand_ref, out_ref, lse_ref,
                  key_feat, query_feat, key_wide, query_wide, values, turned, store):
    heads, length = lse_ref.shape
    fill_features(seg_ref, rand_ref, glob_ref[0], glob_ref[1], key_feat, query_feat)
    for p in range(heads // 2):
        widen_pair(p, q_ref, k_ref, key_feat, query_feat, key_wide, query_wide)
        values[128 * p : 128 * p + 128, :] = v_ref[:, 128 * p : 128 * p + 128].T

    def tile(i, _):
        qs = pl.ds(pl.multiple_of(i * TQ, TQ), TQ)
        start = lo_ref[i]

        def scan(j, tops):
            ks = pl.ds(pl.multiple_of(start + j * TK, 128), TK)
            to = pl.ds(pl.multiple_of(j * TK, TK), TK)
            raised = []
            for h in range(heads):
                scores = nn(key_wide[h, ks, :], query_wide[h, :, qs])
                store[h, to, :] = scores
                raised.append(jnp.maximum(tops[h], jnp.max(scores.reshape(TK // 8, 8, TQ), axis=0)))
            return tuple(raised)

        tops = lax.fori_loop(0, n_ref[i], scan, (jnp.full((8, TQ), LOWEST, F32),) * heads)
        tops = [jnp.max(top, axis=0, keepdims=True) for top in tops]

        def collect(j, carry):
            ks = pl.ds(pl.multiple_of(start + j * TK, 128), TK)
            at = pl.ds(pl.multiple_of(j * TK, TK), TK)
            new = []
            for h in range(heads):
                total, summed = carry[h]
                expo = jnp.exp(store[h, at, :] - tops[h])
                total = total + jnp.sum(expo.reshape(TK // 8, 8, TQ), axis=0)
                summed = summed + nn(values[HD * h : HD * h + HD, ks], expo.astype(BF))
                new.append((total, summed))
            return tuple(new)

        none = (jnp.zeros((8, TQ), F32), jnp.zeros((HD, TQ), F32))
        found = lax.fori_loop(0, n_ref[i], collect, (none,) * heads)
        for h in range(heads):
            total, summed = found[h]
            total = jnp.sum(total, axis=0, keepdims=True)
            turned[HD * h : HD * h + HD, qs] = (summed / total).astype(BF)
            lse_ref[h : h + 1, qs] = tops[h] + jnp.log(total)
        return 0

    lax.fori_loop(0, length // TQ, tile, 0)
    quarter = length // 4
    for p in range(heads // 2):
        result = turned[128 * p : 128 * p + 128, :].T
        for n in range(4):
            rel = lax.rem(meta[0] + n, 2)
            out_ref[rel, quarter * (n // 2) : quarter * (n // 2) + quarter, 128 * p : 128 * p + 128] = result[
                quarter * n : quarter * n + quarter
            ]


def whole(dims):
    return pl.BlockSpec(dims, lambda *_: (0,) * len(dims))


def attend(meta, qkv, seg_row, table, globs, lo, n):
    length = qkv.shape[0]
    heads, blocks = table.shape[:2]
    wide = heads * HD
    third = lambda w: pl.BlockSpec((length, wide), lambda i: (0, w))
    return pl.pallas_call(
        attend_kernel,
        grid=(1,),
        in_specs=[smem()] * 4 + [third(0), third(1), third(2), whole((1, length)), whole((heads, blocks, 3))],
        out_specs=[whole((2, length // 2, wide)), whole((heads, length))],
        out_shape=[shape((2, length // 2, wide), BF), shape((heads, length), F32)],
        scratch_shapes=[
            pltpu.VMEM((heads, HD, length), BF),
            pltpu.VMEM((HD, length), BF),
            pltpu.VMEM((heads, length, 128), BF),
            pltpu.VMEM((heads, 128, length), BF),
            pltpu.VMEM((wide, length), BF),
            pltpu.VMEM((wide, length), BF),
            pltpu.VMEM((heads, length, TQ), F32),
        ],
        compiler_params=pltpu.CompilerParams(vmem_limit_bytes=VMEM_LIMIT),
        cost_estimate=pl.CostEstimate(
            flops=heads * length * length * 512, bytes_accessed=10 * length * wide, transcendentals=heads * length * length // 2
        ),
        name="attend",
    )(meta, lo, n, globs, qkv, qkv, qkv, seg_row, table)


def attend_back_kernel(meta, lo_ref, n_ref, glob_ref, q_ref, k_ref, v_ref, own_ref, oth_ref, ctx_ref, lse_ref, seg_ref,
                       rand_ref, dq_ref, dk_ref, dv_ref, key_feat, query_feat, key_wide, query_wide, value_one,
                       grad_turned, keys_turned, query_one, grad_one, inner_ref, dk, dv, dqt, grads):
    heads, length = lse_ref.shape
    quarter = length // 4
    fill_features(seg_ref, rand_ref, glob_ref[0], glob_ref[1], key_feat, query_feat)
    for rel, source in ((0, own_ref), (1, oth_ref)):
        for n in range(2):
            at = 2 * n + lax.rem(meta[0] + rel, 2)
            rows = pl.ds(pl.multiple_of(at * quarter, quarter), quarter)
            grads[0, rows, :] = source[quarter * n : quarter * n + quarter, :]
            grads[1, rows, :] = ctx_ref[rel, quarter * n : quarter * n + quarter, :]
    low = lax.broadcasted_iota(jnp.int32, (length, 128), 1) < HD
    zero = jnp.zeros((length, 128), BF)
    for p in range(heads // 2):
        cols = slice(128 * p, 128 * p + 128)
        scaled, keys = widen_pair(p, q_ref, k_ref, key_feat, query_feat, key_wide, query_wide)
        keys_turned[cols, :] = keys
        grad, value = grads[0, :, cols], v_ref[:, cols]
        for e in range(2):
            keep = low if e == 0 else ~low
            value_one[2 * p + e] = jnp.where(keep, value, zero)
            query_one[2 * p + e] = jnp.where(keep, scaled, zero)
            grad_one[2 * p + e] = jnp.where(keep, grad, zero)
        turned = grad.T
        grad_turned[cols, :] = turned
        product = turned.astype(F32) * grads[1, :, cols].T.astype(F32)
        for e in range(2):
            h = 2 * p + e
            inner_ref[h : h + 1, :] = jnp.sum(product[HD * e : HD * e + HD], axis=0, keepdims=True)
    dk[...] = jnp.zeros_like(dk)
    dv[...] = jnp.zeros_like(dv)

    def tile(i, _):
        qs = pl.ds(pl.multiple_of(i * TQ, TQ), TQ)
        start = lo_ref[i]

        def body(j, carry):
            ks = pl.ds(pl.multiple_of(start + j * TK, 128), TK)
            new = []
            for p in range(heads // 2):
                cols = slice(128 * p, 128 * p + 128)
                more_k, more_v = [], []
                for h in (2 * p, 2 * p + 1):
                    scores = nn(key_wide[h, ks, :], query_wide[h, :, qs])
                    prob = jnp.exp(scores - lse_ref[h : h + 1, qs])
                    grad_prob = nn(value_one[h, ks, :], grad_turned[cols, qs])
                    grad_scores = (prob * (grad_prob - inner_ref[h : h + 1, qs])).astype(BF)
                    new.append(carry[h] + nn(keys_turned[HD * h : HD * h + HD, ks], grad_scores))
                    more_k.append(nn(grad_scores, query_one[h, qs, :]))
                    more_v.append(nn(prob.astype(BF), grad_one[h, qs, :]))
                dk[ks, cols] += more_k[0] + more_k[1]
                dv[ks, cols] += more_v[0] + more_v[1]
            return tuple(new)

        found = lax.fori_loop(0, n_ref[i], body, (jnp.zeros((HD, TQ), F32),) * heads)
        for h in range(heads):
            dqt[HD * h : HD * h + HD, qs] = (found[h] * HD**-0.5).astype(BF)
        return 0

    lax.fori_loop(0, length // TQ, tile, 0)
    for p in range(heads // 2):
        cols = slice(128 * p, 128 * p + 128)
        dq_ref[:, cols] = dqt[cols, :].T
    dk_ref[...] = dk[...].astype(BF)
    dv_ref[...] = dv[...].astype(BF)


def attend_back(meta, qkv, own, oth, ctx, lse, seg_row, table, globs, lo, n):
    length = qkv.shape[0]
    heads, blocks = table.shape[:2]
    wide = heads * HD
    third = lambda w: pl.BlockSpec((length, wide), lambda i: (0, w))
    half = whole((length // 2, wide))
    return pl.pallas_call(
        attend_back_kernel,
        grid=(1,),
        in_specs=[smem()] * 4
        + [third(0), third(1), third(2), half, half, whole((2, length // 2, wide)), whole((heads, length))]
        + [whole((1, length)), whole((heads, blocks, 3))],
        out_specs=[whole((length, wide))] * 3,
        out_shape=[shape((length, wide), BF)] * 3,
        scratch_shapes=[
            pltpu.VMEM((heads, HD, length), BF),
            pltpu.VMEM((HD, length), BF),
            pltpu.VMEM((heads, length, 128), BF),
            pltpu.VMEM((heads, 128, length), BF),
            pltpu.VMEM((heads, length, 128), BF),
            pltpu.VMEM((wide, length), BF),
            pltpu.VMEM((wide, length), BF),
            pltpu.VMEM((heads, length, 128), BF),
            pltpu.VMEM((heads, length, 128), BF),
            pltpu.VMEM((heads, length), F32),
            pltpu.VMEM((length, wide), F32),
            pltpu.VMEM((length, wide), F32),
            pltpu.VMEM((wide, length), BF),
            pltpu.VMEM((2, length, wide), BF),
        ],
        compiler_params=pltpu.CompilerParams(vmem_limit_bytes=VMEM_LIMIT),
        cost_estimate=pl.CostEstimate(
            flops=heads * length * length * 1280, bytes_accessed=20 * length * wide, transcendentals=heads * length * length // 2
        ),
        name="attend_back",
    )(meta, lo, n, globs, qkv, qkv, qkv, own, oth, ctx, lse, seg_row, table)


def key_ranges(segment):
    length = segment.shape[0]
    first, last = segment[::TQ], segment[TQ - 1 :: TQ]
    lo = jnp.sum(segment[None, :] < first[:, None], axis=1, dtype=jnp.int32) // 128 * 128
    hi = jnp.sum(segment[None, :] <= last[:, None], axis=1, dtype=jnp.int32)
    n = (hi - lo + TK - 1) // TK
    return jnp.minimum(lo, length - n * TK), n


def centre(value):
    centred = value - jnp.mean(value, axis=1, keepdims=True)
    rate = lax.rsqrt(jnp.mean(centred * centred, axis=1, keepdims=True) + EPSILON)
    return centred * rate, rate


def norm_back(grad, normed, rate):
    return rate * (
        grad
        - jnp.mean(grad, axis=1, keepdims=True)
        - normed * jnp.mean(grad * normed, axis=1, keepdims=True)
    )


def cut(value):
    half = value.shape[1] // 2
    return value[:, :half], value[:, half:]


class Packed:
    def __init__(self, ref):
        self.ref = ref
        self.width = ref.shape[3]
        self.depth = 2 * self.width // CHIPS
        self.groups = (ref.shape[2] - self.depth) // (2 * self.depth)
        self.low = self.depth * (1 + self.groups)
        self.deep = ref.shape[2] - self.low
        self.span = self.width // self.deep

    def at_proj(self, h, hc):
        return (hc, slice(CHIPS // 2 * h, CHIPS // 2 * h + CHIPS // 2), slice(0, self.depth), slice(None))

    def at_inner(self, h, g):
        return (h, slice(0, CHIPS), slice(self.depth * (1 + g), self.depth * (2 + g)), slice(None))

    def at_down(self, h, g, hc):
        first = CHIPS // 2 * h + self.span * g
        return (hc, slice(first, first + self.span), slice(self.low, self.low + self.deep), slice(None))

    def read(self, where):
        value = self.ref[where]
        return value.reshape(-1, self.width)

    def write(self, where, value):
        a, b = where[1], where[2]
        self.ref[where] = value.reshape(a.stop - a.start, b.stop - b.start, self.width).astype(self.ref.dtype)


def ffn_kernel(plan, pieces_n, *refs):
    meta = refs[0]
    own_pieces = refs[1 : 1 + pieces_n]
    oth_pieces = refs[1 + pieces_n : 1 + 2 * pieces_n]
    (ctx_own, ctx_oth, x_ref, dout_ref, vec_ref, bias_ref,
     out_ref, hid_ref, gf_ref, low_ref, gp_ref, gr_ref, ga_ref, gc_own, gc_oth, vg_ref, bg_ref,
     w_ref, slope, sems) = refs[1 + 2 * pieces_n :]
    here = placed(meta)
    c = here["c"]
    step = pl.program_id(0)

    @pl.when(step == 0)
    def _():
        copies = []
        for rel, pieces in ((0, own_pieces), (1, oth_pieces)):
            for p, m, chip, first, end in plan.walk(here):
                copies.append(
                    pltpu.make_async_copy(
                        pieces[p].at[m], w_ref.at[lax.rem(c + rel, 2), chip, first:end, :], sems.at[len(copies)]
                    )
                )
        for copy in copies:
            copy.start()
        for copy in copies:
            copy.wait()
        vg_ref[...] = jnp.zeros_like(vg_ref)
        bg_ref[...] = jnp.zeros_like(bg_ref)

    w = Packed(w_ref)
    wide = w.width
    vec = lambda n: vec_ref[n : n + 1, :]
    own, oth = ctx_own[...], ctx_oth[...]
    context = (jnp.where(c == 0, own, oth), jnp.where(c == 0, oth, own))
    attn = jnp.concatenate(
        [nn(context[0], w.read(w.at_proj(0, hc))) + nn(context[1], w.read(w.at_proj(1, hc))) for hc in range(2)], axis=1
    )
    n1, rate1 = centre(x_ref[...].astype(F32) + (attn + vec(0)))
    x1 = n1 * vec(1) + vec(2)
    low = x1.astype(BF)
    low_ref[...] = low
    ffn = [None, None]
    chunks = [(h, g) for h in range(2) for g in range(w.groups)]
    for number, (h, g) in enumerate(chunks):
        cols = slice(wide * number, wide * number + wide)
        pre = nn(low, w.read(w.at_inner(h, g))) + bias_ref[0:1, cols]
        below = 0.5 + 0.5 * lax.erf(pre * 0.7071067811865476)
        slope[:, cols] = below + pre * (jnp.exp(-0.5 * (pre * pre)) * 0.3989422804014327)
        hidden = (pre * below).astype(BF)
        hid_ref[:, cols] = hidden
        for hc in range(2):
            more = nn(hidden, w.read(w.at_down(h, g, hc)))
            ffn[hc] = more if ffn[hc] is None else ffn[hc] + more
    n2, rate2 = centre(x1 + (jnp.concatenate(ffn, axis=1) + vec(3)))
    out_ref[...] = (n2 * vec(4) + vec(5)).astype(BF)

    total = lambda value: jnp.sum(value, axis=0, keepdims=True)
    grad = dout_ref[...].astype(F32)
    gr2 = norm_back(grad * vec(4), n2, rate2)
    gf = gr2.astype(BF)
    gf_ref[...] = gf
    vg_ref[4:5, :] += total(grad * n2)
    vg_ref[5:6, :] += total(grad)
    vg_ref[3:4, :] += total(gf.astype(F32))
    gf_halves = cut(gf)
    gx1 = gr2
    for number, (h, g) in enumerate(chunks):
        cols = slice(wide * number, wide * number + wide)
        grad_hidden = nt(gf_halves[0], w.read(w.at_down(h, g, 0))) + nt(gf_halves[1], w.read(w.at_down(h, g, 1)))
        gp = (grad_hidden * slope[:, cols]).astype(BF)
        gp_ref[:, cols] = gp
        bg_ref[0:1, cols] += total(gp.astype(F32))
        gx1 = gx1 + nt(gp, w.read(w.at_inner(h, g)))
    gr1 = norm_back(gx1 * vec(1), n1, rate1)
    gr_ref[...] = gr1
    ga = gr1.astype(BF)
    ga_ref[...] = ga
    vg_ref[1:2, :] += total(gx1 * n1)
    vg_ref[2:3, :] += total(gx1)
    vg_ref[0:1, :] += total(ga.astype(F32))
    ga_halves = cut(ga)
    gc = [nt(ga_halves[0], w.read(w.at_proj(h, 0))) + nt(ga_halves[1], w.read(w.at_proj(h, 1))) for h in range(2)]
    gc_own[...] = jnp.where(c == 0, gc[0], gc[1]).astype(BF)
    gc_oth[...] = jnp.where(c == 0, gc[1], gc[0]).astype(BF)


def feed_forward(plan, meta, own_pieces, oth_pieces, ctx, ctx_oth, x_own, d_own, vectors, inner_bias):
    rows, model = x_own.shape
    wide = inner_bias.shape[1]
    half = model // 2
    packed = (2, CHIPS, model // CHIPS * (1 + wide // 2 // half) + wide // CHIPS, half)
    tile = lambda n: pl.BlockSpec((TILE, n), lambda i: (i, 0))
    return pl.pallas_call(
        lambda *refs: ffn_kernel(plan, len(own_pieces), *refs),
        grid=(rows // TILE,),
        in_specs=[smem()]
        + [anywhere()] * (2 * len(own_pieces))
        + [pl.BlockSpec((None, TILE, half), lambda i: (0, i, 0)), tile(half), tile(model), tile(model)]
        + [whole(vectors.shape), whole(inner_bias.shape)],
        out_specs=[tile(model), tile(wide), tile(model), tile(model), tile(wide), tile(model), tile(model), tile(half), tile(half)]
        + [whole((8, model)), whole((8, wide))],
        out_shape=[
            shape((rows, model), BF),
            shape((rows, wide), BF),
            shape((rows, model), BF),
            shape((rows, model), BF),
            shape((rows, wide), BF),
            shape((rows, model), F32),
            shape((rows, model), BF),
            shape((rows, half), BF),
            shape((rows, half), BF),
            shape((8, model), F32),
            shape((8, wide), F32),
        ],
        scratch_shapes=[
            pltpu.VMEM(packed, BF),
            pltpu.VMEM((TILE, wide), F32),
            pltpu.SemaphoreType.DMA((2 * plan.entries(),)),
        ],
        compiler_params=pltpu.CompilerParams(vmem_limit_bytes=VMEM_LIMIT),
        cost_estimate=pl.CostEstimate(
            flops=4 * rows * model * (model + 2 * wide), bytes_accessed=rows * (8 * wide + 20 * model), transcendentals=2 * rows * wide
        ),
        name="feed_forward",
    )(meta, *own_pieces, *oth_pieces, ctx, ctx_oth, x_own, d_own, vectors, inner_bias)


def weight_grads_kernel(plan, pieces_n, *refs):
    meta, hid_ref, gp_ref, gf_ref, low_ref, ctx_own, ctx_oth, ga_ref = refs[:8]
    own_pieces = refs[8 : 8 + pieces_n]
    oth_pieces = refs[8 + pieces_n : 8 + 2 * pieces_n]
    g_ref, sems = refs[8 + 2 * pieces_n :]
    here = placed(meta)
    c = here["c"]
    step = pl.program_id(0)
    w = Packed(g_ref)

    @pl.when(step == 0)
    def _():
        own, oth = ctx_own[...], ctx_oth[...]
        context = (jnp.where(c == 0, own, oth), jnp.where(c == 0, oth, own))
        for hc, part in enumerate(cut(ga_ref[...])):
            for h in range(2):
                w.write(w.at_proj(h, hc), tn(context[h], part))

    inner = tn(low_ref[...], gp_ref[...])
    down = cut(tn(hid_ref[...], gf_ref[...]))
    for number in range(2 * w.groups):

        @pl.when(step == number)
        def _():
            h, g = divmod(number, w.groups)
            w.write(w.at_inner(h, g), inner)
            for hc in range(2):
                w.write(w.at_down(h, g, hc), down[hc])

    @pl.when(step == 2 * w.groups - 1)
    def _():
        copies = []
        for rel, pieces in ((0, own_pieces), (1, oth_pieces)):
            for p, m, chip, first, end in plan.walk(here):
                copies.append(
                    pltpu.make_async_copy(
                        g_ref.at[lax.rem(c + rel, 2), chip, first:end, :], pieces[p].at[m], sems.at[len(copies)]
                    )
                )
        for copy in copies:
            copy.start()
        for copy in copies:
            copy.wait()


def piece_shapes(plan, width):
    made = []
    for (first, end, _), count in zip(plan.parts, plan.counts()):
        made += [shape((CHIPS // count, end - first, width), BF)] * count
    return made


def weight_grads(plan, meta, hid, gp, gf, low, ctx, ctx_oth, ga):
    rows, model = gf.shape
    wide, half = hid.shape[1], model // 2
    packed = (2, CHIPS, model // CHIPS * (1 + wide // 2 // half) + wide // CHIPS, half)
    pieces = piece_shapes(plan, half)
    cols = pl.BlockSpec((rows, half), lambda i: (0, i))
    found = pl.pallas_call(
        lambda *refs: weight_grads_kernel(plan, len(pieces), *refs),
        grid=(wide // half,),
        in_specs=[smem(), cols, cols, whole((rows, model)), whole((rows, model))]
        + [pl.BlockSpec((None, rows, half), lambda i: (0, 0, 0)), whole((rows, half)), whole((rows, model))],
        out_specs=[anywhere()] * (2 * len(pieces)),
        out_shape=pieces * 2,
        scratch_shapes=[pltpu.VMEM(packed, BF), pltpu.SemaphoreType.DMA((2 * plan.entries(),))],
        compiler_params=pltpu.CompilerParams(vmem_limit_bytes=VMEM_LIMIT),
        cost_estimate=pl.CostEstimate(
            flops=2 * rows * model * (model + 2 * wide), bytes_accessed=rows * (4 * wide + 8 * model), transcendentals=0
        ),
        name="weight_grads",
    )(meta, hid, gp, gf, low, ctx, ctx_oth, ga)
    return found[: len(pieces)], found[len(pieces) :]


def qkv_grads_kernel(plan, pieces_n, *refs):
    meta, x_ref, dq_ref, dk_ref, dv_ref = refs[:5]
    pieces = refs[5 : 5 + pieces_n]
    sums_ref, g_ref, sems = refs[5 + pieces_n :]
    here = placed(meta)
    depth, width = g_ref.shape[1] // 3, g_ref.shape[2]
    x = x_ref[...]
    for w, source in enumerate((dq_ref, dk_ref, dv_ref)):
        grad = source[...]
        g_ref[:, depth * w : depth * w + depth, :] = tn(x, grad).reshape(CHIPS, depth, width).astype(BF)
        sums_ref[w : w + 1, :] = jnp.sum(grad.astype(F32), axis=0, keepdims=True)
    copies = []
    for i, (p, m, chip, first, end) in enumerate(plan.walk(here)):
        copies.append(pltpu.make_async_copy(g_ref.at[chip, first:end, :], pieces[p].at[m], sems.at[i]))
    for copy in copies:
        copy.start()
    for copy in copies:
        copy.wait()


def qkv_grads(plan, meta, x_full, dq, dk, dv):
    rows, model = x_full.shape
    width, depth = dq.shape[1], model // CHIPS
    pieces = piece_shapes(plan, width)
    found = pl.pallas_call(
        lambda *refs: qkv_grads_kernel(plan, len(pieces), *refs),
        grid=(1,),
        in_specs=[smem(), whole((rows, model))] + [whole((rows, width))] * 3,
        out_specs=[anywhere()] * len(pieces) + [whole((8, width))],
        out_shape=pieces + [shape((8, width), F32)],
        scratch_shapes=[pltpu.VMEM((CHIPS, 3 * depth, width), BF), pltpu.SemaphoreType.DMA((plan.entries(),))],
        compiler_params=pltpu.CompilerParams(vmem_limit_bytes=VMEM_LIMIT),
        cost_estimate=pl.CostEstimate(
            flops=6 * rows * model * width, bytes_accessed=2 * rows * (model + 3 * width), transcendentals=0
        ),
        name="qkv_grads",
    )(meta, x_full, dq, dk, dv)
    return found[:-1], found[-1]


def input_grads_kernel(meta, dq_ref, dk_ref, dv_ref, w_ref, out_ref):
    depth, width = w_ref.shape[1] // 3, w_ref.shape[2]
    total = None
    for w, source in enumerate((dq_ref, dk_ref, dv_ref)):
        weight = w_ref[:, depth * w : depth * w + depth, :].reshape(CHIPS * depth, width)
        more = nt(source[...], weight)
        total = more if total is None else total + more
    out_ref[...] = total.astype(BF)


def input_grads(meta, dq, dk, dv, weights):
    rows, width = dq.shape
    chips, deep, _ = weights.shape
    model = chips * deep // 3
    quarter = rows // 4
    part = pl.BlockSpec((quarter, width), lambda i, meta: (i, 0))
    return pl.pallas_call(
        input_grads_kernel,
        grid_spec=pltpu.PrefetchScalarGridSpec(
            num_scalar_prefetch=1,
            grid=(4,),
            in_specs=[part, part, part, whole(weights.shape)],
            out_specs=pl.BlockSpec(
                (None, quarter, model), lambda i, meta: (lax.rem(meta[0] + i, 2), i // 2, 0)
            ),
        ),
        out_shape=shape((2, 2 * quarter, model), BF),
        compiler_params=pltpu.CompilerParams(vmem_limit_bytes=VMEM_LIMIT),
        cost_estimate=pl.CostEstimate(
            flops=6 * rows * model * width, bytes_accessed=2 * rows * (model + 3 * width), transcendentals=0
        ),
        name="input_grads",
    )(meta, dq, dk, dv, weights)


def pack_vectors(vectors, inner_bias):
    row = jnp.concatenate(list(vectors) + [inner_bias])
    return jnp.pad(row, (0, -row.shape[0] % 128))


def body(
    tokens,
    qkv_weight,
    query_bias,
    value_bias,
    proj_weight,
    proj_bias,
    attn_gain,
    attn_shift,
    inner_weight,
    inner_bias,
    down_weight,
    down_bias,
    ffn_gain,
    ffn_shift,
    seg_ids,
    rand_blocks,
    glob_blocks,
    d_out,
):
    dp, seq = lax.axis_index("dp"), lax.axis_index("seq")
    members = lax.axis_size("dp") * lax.axis_size("seq")
    near = lax.axis_size("dp") == 8
    y, c = seq // 2, seq % 2
    even = c == 0
    meta = jnp.stack([c, dp % 2, y, dp // 2]).astype(jnp.int32)
    model = tokens.shape[3]
    half = model // 2
    ffw = inner_weight.shape[1]
    share = qkv_weight.shape[0]
    share_f = down_weight.shape[0]
    groups = ffw // 2 // half
    depth, deep = model // CHIPS, ffw // CHIPS
    low = depth * (1 + groups)

    vectors = (query_bias, value_bias, proj_bias, attn_gain, attn_shift, down_bias, ffn_gain, ffn_shift)
    row = pack_vectors(vectors, inner_bias)
    if near:
        plan_a = Plan([(0, 64, "zxy"), (64, 3 * depth, "yzx")])
        plan_b = Plan([(0, 208, "zxy"), (208, low + deep, "yzx")])

        def sections(h):
            col = lambda w, first: w[:, first : first + half]
            found = [col(qkv_weight, model * w + half * h) for w in range(3)] + [col(proj_weight, half * h)]
            found += [col(inner_weight, ffw // 2 * h + half * g) for g in range(groups)]
            found += [col(down_weight, half * h)]
            return jnp.concatenate(found, axis=0)

        zero, one = sections(0), sections(1)
        mine, theirs = jnp.where(even, zero, one), jnp.where(even, one, zero)
        came = swap(theirs, "core")
        first, second = jnp.where(even, mine, came), jnp.where(even, came, mine)
        laid, at = [], 0
        for length in [share] * (4 + groups) + [share_f]:
            laid += [first[at : at + length], second[at : at + length]]
            at += length
        chunk_a = jnp.concatenate(laid[:6], axis=0)
        chunk_b = jnp.concatenate(laid[6:], axis=0)
        came = swap(row, "core")
        rows = jnp.where(even, jnp.stack([row, came]), jnp.stack([came, row]))
        for dim in "yxz":
            rows = jnp.concatenate([rows] + others(rows, dim), axis=0)
        entry = jnp.arange(CHIPS)
        y_rel, x_rel, z_rel = entry % 2, entry // 2 % 2, entry // 4
        source = (meta[3] - z_rel) % 4 * 4 + (meta[1] ^ x_rel) * 2 + (meta[2] ^ y_rel)
        order = (source[None, :] == jnp.arange(CHIPS)[:, None]).astype(BF)
        rows = nn(order, rows.reshape(CHIPS, -1)).reshape(members, -1)
        pieces_a = []
        for start, end, way in plan_a.parts:
            pieces_a += gather(chunk_a[start:end], way)
    else:
        plan_a = Plan([(0, 3 * depth, None)])
        plan_b = Plan([(0, low + deep, None)])
        everyone = lambda w: lax.all_gather(w, ("dp", "seq"), axis=0, tiled=True)
        full_qkv, full_proj, full_inner, full_down = map(everyone, (qkv_weight, proj_weight, inner_weight, down_weight))
        rows = everyone(row[None]).astype(F32)

        def packed(h):
            col = lambda w, first: lax.dynamic_slice_in_dim(w, first, half, 1).reshape(CHIPS, -1, half)
            a = jnp.concatenate([col(full_qkv, model * w + half * h) for w in range(3)], axis=1)
            b = [col(full_proj, half * h)] + [col(full_inner, ffw // 2 * h + half * g) for g in range(groups)]
            return a, jnp.concatenate(b + [col(full_down, half * h)], axis=1)

        chunk_a, own_b = packed(c)
        pieces_a, own_b, oth_b = [chunk_a], [own_b], [packed(1 - c)[1]]
    spread = rows[:, : 8 * share].reshape(members, 8, share).transpose(1, 0, 2).reshape(8, model)
    hidden_bias = rows[:, 8 * share : 8 * share + share_f * 1].reshape(1, ffw)
    pick = lambda v: lax.dynamic_slice_in_dim(v, c * half, half, 0)
    bias = jnp.concatenate([pick(spread[0]), jnp.zeros((half,), F32), pick(spread[1])])[None]

    low_y = y == 0
    pair = lambda kept, came: jnp.where(low_y, jnp.stack([kept, came]), jnp.stack([came, kept]))

    def to_chip(value):
        kept = jnp.where(low_y, value[0], value[1])
        return pair(kept, swap(jnp.where(low_y, value[1], value[0]), "y"))

    def from_chip(value):
        kept = jnp.where(low_y, value[0], value[1])
        return pair(kept, swap(jnp.where(low_y, value[1], value[0]), "y"))

    x_own = to_chip(tokens[:, 0])
    x_oth = swap(x_own, "core")
    x_full = jnp.where(even, jnp.stack([x_own, x_oth], 1), jnp.stack([x_oth, x_own], 1)).reshape(-1, model)
    x_own = x_own.reshape(-1, model)
    segment = jnp.where(low_y, seg_ids[0, 0], seg_ids[1, 0])
    globs = jnp.where(low_y, glob_blocks[0, 0], glob_blocks[1, 0])
    tables = rand_blocks[:, 0]
    turn = lambda v, to: lax.ppermute(v, "seq", to)
    spot = lambda a, b: 2 * a + b
    one = turn(jnp.where(even, tables[0], tables[1]), [(spot(a, b), spot(b, a)) for a in range(2) for b in range(2)])
    two = turn(jnp.where(even, tables[1], tables[0]), [(spot(a, b), spot(1 - b, a)) for a in range(2) for b in range(2)])
    table = jnp.where(low_y, jnp.concatenate([one, two]), jnp.concatenate([two, one]))
    lo, n = key_ranges(segment)

    qkv, w_qkv = project_qkv(plan_a, meta, pieces_a, x_full, bias)
    d_own = to_chip(d_out[:, 0]).reshape(-1, model)
    if near:
        own_b = []
        for start, end, way in plan_b.parts:
            own_b += gather(chunk_b[start:end], way)
        oth_b = [swap(piece, "core") for piece in own_b]
    ctx, lse = attend(meta, qkv, segment[None], table, globs, lo, n)
    ctx_oth = swap(ctx[1], "core")
    found = feed_forward(plan_b, meta, own_b, oth_b, ctx, ctx_oth, x_own, d_own, spread[2:], hidden_bias)
    out, hid, gf, x1_low, gp, gr1, ga, gc_own, gc_oth, vg, bg = found
    layer_out = from_chip(out.reshape(2, -1, model))[:, None]

    gc_came = swap(gc_oth, "core")
    grads_own, grads_oth = weight_grads(plan_b, meta, hid, gp, gf, x1_low, ctx, ctx_oth, ga)
    dq, dk, dv = attend_back(meta, qkv, gc_own, gc_came, ctx, lse, segment[None], table, globs, lo, n)
    grads_qkv, sums = qkv_grads(plan_a, meta, x_full, dq, dk, dv)
    back = input_grads(meta, dq, dk, dv, w_qkv)
    grad_own = gr1 + (back[0].astype(F32) + swap(back[1], "core").astype(F32))
    grad_input = from_chip(grad_own.astype(BF).reshape(2, -1, model))[:, None]

    nil = jnp.zeros((half,), F32)
    across = lambda v: jnp.where(even, jnp.concatenate([v, nil]), jnp.concatenate([nil, v]))
    small = jnp.concatenate([across(sums[0])[None], across(sums[2])[None], vg[:6]], axis=0)
    small = small.reshape(8, members, share).transpose(1, 0, 2).reshape(members, 8 * share)
    small = jnp.concatenate([small, bg[0].reshape(members, share_f)], axis=1)
    if near:
        small = small + swap(small, "core")
        for dim in "yxz":
            total = small
            for came in others(small, dim):
                total = total + came
            small = total
        small = lax.dynamic_slice_in_dim(small, dp * 4 + seq, 1, 0)[0]

        def chip_sum(pieces, plan):
            sums, at = [], 0
            for (_, _, way), count in zip(plan.parts, plan.counts()):
                turned = [p.reshape((-1,) + p.shape[1:]) for p in pieces[at : at + count]]
                sums.append(scatter_sum(turned, way[::-1]))
                at += count
            return jnp.concatenate(sums, axis=0)

        both = [a + swap(b, "core") for a, b in zip(grads_own, grads_oth)]
        total = jnp.concatenate([chip_sum(grads_qkv, plan_a), chip_sum(both, plan_b)], axis=0)
        mine, theirs, at = [], [], 0
        for length in [share] * (4 + groups) + [share_f]:
            first, second = total[at : at + length], total[at + length : at + 2 * length]
            mine.append(jnp.where(even, first, second))
            theirs.append(jnp.where(even, second, first))
            at += 2 * length
        mine = jnp.concatenate(mine, axis=0)
        came = swap(jnp.concatenate(theirs, axis=0).astype(BF), "core").astype(F32)
        halves = jnp.where(even, jnp.stack([mine, came]), jnp.stack([came, mine]))
        cuts, at = [], 0
        for length in [share] * (4 + groups) + [share_f]:
            cuts.append(halves[:, at : at + length])
            at += length
        side = lambda v: [v[0], v[1]]
        grad_qkv = jnp.concatenate([v for w in range(3) for v in side(cuts[w])], axis=1)
        grad_proj = jnp.concatenate(side(cuts[3]), axis=1)
        grad_inner = jnp.concatenate([cuts[4 + g][h] for h in range(2) for g in range(groups)], axis=1)
        grad_down = jnp.concatenate(side(cuts[4 + groups]), axis=1)
    else:
        scatter = lambda v: lax.psum_scatter(v.astype(F32), ("dp", "seq"), scatter_dimension=0, tiled=True)
        small = scatter(small)[0]
        full = jnp.where(even, jnp.stack([grads_own[0], grads_oth[0]]), jnp.stack([grads_oth[0], grads_own[0]]))
        part = lambda h, a, b: full[h, :, a:b].reshape(-1, half)
        zero = jnp.zeros((model, half), BF)
        third = lambda w: grads_qkv[0][:, depth * w : depth * w + depth].reshape(-1, half)
        place = lambda v: jnp.where(even, jnp.concatenate([v, zero], axis=1), jnp.concatenate([zero, v], axis=1))
        grad_qkv = scatter(jnp.concatenate([place(third(w)) for w in range(3)], axis=1))
        grad_proj = scatter(jnp.concatenate([part(h, 0, depth) for h in range(2)], axis=1))
        grad_inner = scatter(
            jnp.concatenate(
                [part(h, depth * (1 + g), depth * (2 + g)) for h in range(2) for g in range(groups)], axis=1
            )
        )
        grad_down = scatter(jnp.concatenate([part(h, low, low + deep) for h in range(2)], axis=1))
    vector = [small[share * i : share * i + share] for i in range(8)]
    return (
        layer_out,
        grad_input,
        grad_qkv,
        vector[0],
        vector[1],
        grad_proj,
        vector[2],
        vector[3],
        vector[4],
        grad_inner,
        small[8 * share : 8 * share + share_f],
        grad_down,
        vector[5],
        vector[6],
        vector[7],
    )


def solution(mesh):
    row, vec = P(("dp", "seq"), None), P(("dp", "seq"))
    wide = P(None, "dp", "seq", None)
    return jax.shard_map(
        body,
        mesh=mesh,
        in_specs=(wide, row, vec, vec, row, vec, vec, vec, row, vec, row, vec, vec, vec)
        + (P(None, "dp", None), P(None, "dp", "seq", None, None), P(None, "dp", None), wide),
        out_specs=(wide, wide, row, vec, vec, row, vec, vec, vec, row, vec, row, vec, vec, vec),
        check_vma=False,
    )
```

```python
import jax
import jax.numpy as jnp
from jax import lax
from jax.experimental import pallas as pl
from jax.experimental.pallas import tpu as pltpu
from jax.sharding import PartitionSpec as P

HD = 64
BLOCK = 64
EPSILON = 1e-06
BIG = float(2.0**100)
LOWEST = -3.0e38
TQ = 256
TK = 512
CHIPS = 16
TILE = 256
BF = jnp.bfloat16
F32 = jnp.float32
VMEM_LIMIT = 60 << 20


def nn(left, right):
    return lax.dot_general(left, right, (((1,), (0,)), ((), ())), preferred_element_type=F32)


def nt(left, right):
    return lax.dot_general(left, right, (((1,), (1,)), ((), ())), preferred_element_type=F32)


def tn(left, right):
    return lax.dot_general(left, right, (((0,), (0,)), ((), ())), preferred_element_type=F32)


def smem():
    return pl.BlockSpec(memory_space=pltpu.SMEM)


def anywhere():
    return pl.BlockSpec(memory_space=pl.ANY)


def shape(dims, kind):
    return jax.ShapeDtypeStruct(dims, kind)


def after(value, *ready):
    if not ready:
        return value
    return lax.optimization_barrier((value,) + ready)[0]


def swap(value, dim):
    if dim == "x":
        return lax.ppermute(value, "dp", [(d, d ^ 1) for d in range(lax.axis_size("dp"))])
    bit = 1 if dim == "core" else 2
    return lax.ppermute(value, "seq", [(s, s ^ bit) for s in range(4)])


def shift_z(value, by):
    size = lax.axis_size("dp") // 2
    return lax.ppermute(value, "dp", [(2 * z + x, (z + by) % size * 2 + x) for z in range(size) for x in range(2)])


ZS = 4


def gather_z(chunk):
    return jnp.stack([chunk] + [shift_z(chunk, by) for by in range(1, ZS)])


def scatter_z(total, *late):
    summed = total[0].astype(F32)
    for r in range(1, ZS):
        summed = summed + after(shift_z(total[r].astype(BF), ZS - r), *late).astype(F32)
    return summed


def add(a, b):
    return (a.astype(F32) + b.astype(F32)).astype(BF)


def fold_first(a_far, b_far, a_near, b_near, *late):
    a, b = after(swap(a_far, "y"), *late), after(swap(b_far, "x"), *late)
    return add(a_near, a), add(b_near, b)


def fold_second(a, b, *late):
    a_came, b_came = after(swap(a[ZS:], "x"), *late), after(swap(b[ZS:], "y"), *late)
    return jnp.concatenate([add(b[:ZS], b_came), add(a[:ZS], a_came)], axis=1), (a_came, b_came)


def chip_at(order, other, index, here):
    z = lax.rem(here["z"] - index % ZS + ZS, ZS)
    near = {order[0]: index // ZS, order[1]: other}
    return z * 4 + lax.rem(here["x"] + near["x"], 2) * 2 + lax.rem(here["y"] + near["y"], 2)


def placed(meta):
    return {"c": meta[0], "x": meta[1], "y": meta[2], "z": meta[3]}


class Plan:
    def __init__(self, sections, cut):
        self.sections, self.cut = sections, cut
        self.rows = sum(sections)

    def parts(self):
        if self.cut is None:
            return [(0, self.rows, None)]
        return [(self.cut, self.rows, "xy"), (0, self.cut, "yx")]

    def shapes(self, width):
        if self.cut is None:
            return [shape((CHIPS, self.rows, width), BF)]
        return [shape((CHIPS // 2, end - first, width), BF) for first, end, _ in self.parts() for _ in range(2)]

    def walk(self, here):
        piece = 0
        for first, end, order in self.parts():
            for other in range(1 if order is None else 2):
                for m in range(CHIPS if order is None else CHIPS // 2):
                    chip = m if order is None else chip_at(order, other, m, here)
                    start = 0
                    for number, length in enumerate(self.sections):
                        lo, hi = max(start, first), min(start + length, end)
                        if lo < hi:
                            yield piece, m, lo - first, hi - first, chip, number, lo - start
                        start += length
                piece += 1

    def entries(self):
        return sum(1 for _ in self.walk({"c": 0, "x": 0, "y": 0, "z": 0}))


def move(plan, here, pieces, target, sems, base, back=False):
    copies = []
    for i, (p, m, lo, hi, chip, number, at) in enumerate(plan.walk(here)):
        near, far = pieces[p].at[m, lo:hi, :], target(number, chip, slice(at, at + hi - lo))
        if back:
            near, far = far, near
        copies.append(pltpu.make_async_copy(near, far, sems.at[base + i]))
    for copy in copies:
        copy.start()
    return copies


def spread_vectors(rows, first, second, marks, hidden_marks):
    count = rows.shape[0]
    number = lax.broadcasted_iota(jnp.int32, (9 * CHIPS, count), 0)
    entry = lax.broadcasted_iota(jnp.int32, (9 * CHIPS, count), 1)
    picker = (entry == lax.rem(number, CHIPS) * 16 + number // CHIPS).astype(F32).astype(BF)
    picked = nn(picker, rows).astype(BF)
    model = first.shape[1]
    vectors = nn(picked[: 8 * CHIPS], first).reshape(8, CHIPS, model) * marks[None]
    hidden = nn(picked[8 * CHIPS :], second).reshape(4, 4, model) * hidden_marks[None]
    return jnp.sum(vectors, axis=1), jnp.sum(hidden, axis=1)


def spread_tables(model, share, share_f, *ready):
    lane, col = jnp.arange(384)[:, None], jnp.arange(model)[None, :]
    if ready:
        lane = after(lane, *ready)
    first = (lane == 128 * (col // share % 2) + col % share).astype(BF)
    second = (lane == 128 * (col // share_f % 2) + col % share_f).astype(BF)
    marks = (jnp.arange(CHIPS)[:, None] == col // (2 * share)).astype(F32)
    hidden_marks = (jnp.arange(4)[:, None] == col // (2 * share_f)).astype(F32)
    return first, second, marks, hidden_marks


def pack_kernel(meta, qkv_ref, proj_ref, inner_ref, down_ref, mine_ref, theirs_ref):
    model = proj_ref.shape[1]
    half, share = model // 2, proj_ref.shape[0]
    for rel, out in ((0, mine_ref), (1, theirs_ref)):
        h = lax.rem(meta[0] + rel, 2)
        lanes = lambda first, n: pl.ds(pl.multiple_of(first, 128), n)
        at = 0
        for p in range(half // 128):
            for w in range(3):
                out[at : at + share, 128 * w : 128 * w + 128] = qkv_ref[:, lanes(model * w + half * h + 128 * p, 128)]
            at += share
        out[at : at + share, :] = proj_ref[:, lanes(half * h, half)]
        at += share
        for g in range(inner_ref.shape[1] // 2 // half):
            out[at : at + share, :] = inner_ref[:, lanes(inner_ref.shape[1] // 2 * h + half * g, half)]
            at += share
        out[at : at + down_ref.shape[0], :] = down_ref[:, lanes(half * h, half)]


def pack(meta, qkv, proj, inner, down):
    half = proj.shape[1] // 2
    rows = proj.shape[0] * (half // 128 + 1 + inner.shape[1] // 2 // half) + down.shape[0]
    return pl.pallas_call(
        pack_kernel,
        in_specs=[smem()] + [pl.BlockSpec(memory_space=pltpu.VMEM)] * 4,
        out_specs=[pl.BlockSpec(memory_space=pltpu.VMEM)] * 2,
        out_shape=[shape((rows, half), BF)] * 2,
        cost_estimate=pl.CostEstimate(flops=0, bytes_accessed=8 * rows * half, transcendentals=0),
        name="pack",
    )(meta, qkv, proj, inner, down)


def qkv_kernel(plan, pieces_n, *refs):
    meta = refs[0]
    pieces = refs[1 : 1 + pieces_n]
    x_ref, first, second, marks, hidden_marks, out_ref, w_ref, vec_ref, rows_ref, bias_ref, sems = refs[1 + pieces_n :]
    here = placed(meta)
    wide = out_ref.shape[1]
    third = wide // 3

    @pl.when(pl.program_id(0) == 0)
    def _():
        def target(number, chip, rows):
            if number == 3:
                return rows_ref.at[chip, rows, :]
            return w_ref.at[chip, rows, third * number : third * number + third]

        for copy in move(plan, here, pieces, target, sems, 0):
            copy.wait()
        rows = rows_ref[...].reshape(CHIPS * 16, 384)
        vectors, hidden = spread_vectors(rows, first[...], second[...], marks[...], hidden_marks[...])
        vec_ref[0:8, :] = vectors
        vec_ref[8:12, :] = hidden
        vec_ref[12:16, :] = jnp.zeros_like(hidden)
        mine = jnp.where(here["c"] == 0, vectors[:, :third], vectors[:, third:])
        bias_ref[...] = jnp.zeros_like(bias_ref)
        for p in range(3):
            for w, source in ((0, 0), (2, 1)):
                at = third * p + 128 * w
                bias_ref[0:1, at : at + 128] = mine[source : source + 1, 128 * p : 128 * p + 128]

    weight = w_ref[...].reshape(-1, wide)
    out_ref[...] = (nn(x_ref[...], weight) + bias_ref[0:1, :]).astype(BF)


def project_qkv(plan, meta, pieces, x_full, tables):
    rows, model = x_full.shape
    width, depth = model // 2, model // CHIPS
    wide = 3 * width
    tile = 512
    return pl.pallas_call(
        lambda *refs: qkv_kernel(plan, len(pieces), *refs),
        grid=(rows // tile,),
        in_specs=[smem()]
        + [anywhere()] * len(pieces)
        + [pl.BlockSpec((tile, model), lambda i: (i, 0))]
        + [whole(t.shape) for t in tables],
        out_specs=[
            pl.BlockSpec((tile, wide), lambda i: (i, 0)),
            whole((CHIPS, depth, wide)),
            whole((16, model)),
        ],
        out_shape=[shape((rows, wide), BF), shape((CHIPS, depth, wide), BF), shape((16, model), F32)],
        scratch_shapes=[
            pltpu.VMEM((CHIPS, 16, width), BF),
            pltpu.VMEM((8, wide), F32),
            pltpu.SemaphoreType.DMA((plan.entries(),)),
        ],
        compiler_params=pltpu.CompilerParams(vmem_limit_bytes=VMEM_LIMIT),
        cost_estimate=pl.CostEstimate(
            flops=2 * rows * model * wide, bytes_accessed=2 * rows * (model + wide), transcendentals=0
        ),
        name="project_qkv",
    )(meta, *pieces, x_full, *tables)


def fill_features(seg_ref, rand_ref, first_global, second_global, key_ref, query_ref):
    heads, _, length = key_ref.shape
    blocks = length // BLOCK
    at = lax.broadcasted_iota(jnp.int32, (blocks, length), 1) // BLOCK
    row = lax.broadcasted_iota(jnp.int32, (blocks, length), 0)
    seen = jnp.abs(at - row) <= 1
    for chosen in (first_global, second_global):
        seen = seen | (at == chosen) | (row == chosen)
    same = lax.broadcasted_iota(jnp.int32, (HD - blocks, length), 0) == seg_ref[...]
    for h in range(heads):
        picked = seen
        for r in range(rand_ref.shape[2]):
            picked = picked | (at == rand_ref[h, :, r : r + 1])
        key_ref[h, 0:blocks, :] = jnp.where(picked, 0.0, 1.0).astype(BF)
        key_ref[h, blocks:HD, :] = jnp.where(same, 0.0, 1.0).astype(BF)
    query_ref[0:blocks, :] = jnp.where(at == row, -BIG, 0.0).astype(BF)
    query_ref[blocks:HD, :] = jnp.where(same, -BIG, 0.0).astype(BF)


def of_pair(ref, p, w):
    return ref[:, 384 * p + 128 * w : 384 * p + 128 * w + 128]


def widen_pair(p, qkv_ref, key_feat, query_feat, key_wide, query_wide):
    scaled = of_pair(qkv_ref, p, 0) * BF(HD**-0.5)
    queries, keys = scaled.T, of_pair(qkv_ref, p, 1).T
    a, b = 2 * p, 2 * p + 1
    query_wide[a, 0:HD, :] = queries[0:HD]
    query_wide[a, HD:128, :] = query_feat[...]
    query_wide[b, 0:HD, :] = query_feat[...]
    query_wide[b, HD:128, :] = queries[HD:128]
    key_wide[a] = jnp.concatenate([keys[0:HD], key_feat[a]], axis=0).T
    key_wide[b] = jnp.concatenate([key_feat[b], keys[HD:128]], axis=0).T
    return scaled, keys


def attend_kernel(meta, lo_ref, n_ref, glob_ref, qkv_ref, seg_ref, rand_ref, out_ref, lse_ref,
                  key_feat, query_feat, key_wide, query_wide, values, turned, store):
    heads, length = lse_ref.shape
    fill_features(seg_ref, rand_ref, glob_ref[0], glob_ref[1], key_feat, query_feat)
    for p in range(heads // 2):
        widen_pair(p, qkv_ref, key_feat, query_feat, key_wide, query_wide)
        values[128 * p : 128 * p + 128, :] = of_pair(qkv_ref, p, 2).T

    def tile(i, _):
        qs = pl.ds(pl.multiple_of(i * TQ, TQ), TQ)
        start = lo_ref[i]

        def scan(j, tops):
            ks = pl.ds(pl.multiple_of(start + j * TK, 128), TK)
            to = pl.ds(pl.multiple_of(j * TK, TK), TK)
            raised = []
            for h in range(heads):
                scores = nn(key_wide[h, ks, :], query_wide[h, :, qs])
                store[h, to, :] = scores
                raised.append(jnp.maximum(tops[h], jnp.max(scores.reshape(TK // 8, 8, TQ), axis=0)))
            return tuple(raised)

        tops = lax.fori_loop(0, n_ref[i], scan, (jnp.full((8, TQ), LOWEST, F32),) * heads)
        tops = [jnp.max(top, axis=0, keepdims=True) for top in tops]

        def collect(j, carry):
            ks = pl.ds(pl.multiple_of(start + j * TK, 128), TK)
            at = pl.ds(pl.multiple_of(j * TK, TK), TK)
            new = []
            for h in range(heads):
                total, summed = carry[h]
                expo = jnp.exp(store[h, at, :] - tops[h])
                total = total + jnp.sum(expo.reshape(TK // 8, 8, TQ), axis=0)
                summed = summed + nn(values[HD * h : HD * h + HD, ks], expo.astype(BF))
                new.append((total, summed))
            return tuple(new)

        none = (jnp.zeros((8, TQ), F32), jnp.zeros((HD, TQ), F32))
        found = lax.fori_loop(0, n_ref[i], collect, (none,) * heads)
        for h in range(heads):
            total, summed = found[h]
            total = jnp.sum(total, axis=0, keepdims=True)
            turned[HD * h : HD * h + HD, qs] = (summed / total).astype(BF)
            lse_ref[h : h + 1, qs] = tops[h] + jnp.log(total)
        return 0

    lax.fori_loop(0, length // TQ, tile, 0)
    quarter = length // 4
    for p in range(heads // 2):
        result = turned[128 * p : 128 * p + 128, :].T
        for n in range(4):
            rel = lax.rem(meta[0] + n, 2)
            out_ref[rel, quarter * (n // 2) : quarter * (n // 2) + quarter, 128 * p : 128 * p + 128] = result[
                quarter * n : quarter * n + quarter
            ]


def whole(dims):
    return pl.BlockSpec(dims, lambda *_: (0,) * len(dims))


def attend(meta, qkv, number, seg_row, table, globs, lo, n):
    length = qkv.shape[0]
    heads, blocks = table.shape[:2]
    wide = heads * HD
    return pl.pallas_call(
        attend_kernel,
        grid=(1,),
        in_specs=[smem()] * 4
        + [pl.BlockSpec((length, 3 * wide), lambda i: (0, number)), whole((1, length)), whole((heads, blocks, 3))],
        out_specs=[whole((2, length // 2, wide)), whole((heads, length))],
        out_shape=[shape((2, length // 2, wide), BF), shape((heads, length), F32)],
        scratch_shapes=[
            pltpu.VMEM((heads, HD, length), BF),
            pltpu.VMEM((HD, length), BF),
            pltpu.VMEM((heads, length, 128), BF),
            pltpu.VMEM((heads, 128, length), BF),
            pltpu.VMEM((wide, length), BF),
            pltpu.VMEM((wide, length), BF),
            pltpu.VMEM((heads, length, TQ), F32),
        ],
        compiler_params=pltpu.CompilerParams(vmem_limit_bytes=VMEM_LIMIT),
        cost_estimate=pl.CostEstimate(
            flops=heads * length * length * 700, bytes_accessed=10 * length * wide, transcendentals=heads * length * length // 2
        ),
        name="attend",
    )(meta, lo, n, globs, qkv, seg_row, table)


def attend_back_kernel(meta, lo_ref, n_ref, glob_ref, qkv_ref, own_ref, oth_ref, ctx_ref, lse_ref, seg_ref,
                       rand_ref, out_ref, key_feat, query_feat, key_wide, query_wide, value_one,
                       grad_turned, keys_turned, query_one, grad_one, inner_ref, dk, dv, dqt, grads):
    heads, length = lse_ref.shape
    quarter = length // 4
    fill_features(seg_ref, rand_ref, glob_ref[0], glob_ref[1], key_feat, query_feat)
    for rel, source in ((0, own_ref), (1, oth_ref)):
        for n in range(2):
            at = 2 * n + lax.rem(meta[0] + rel, 2)
            rows = pl.ds(pl.multiple_of(at * quarter, quarter), quarter)
            grads[0, rows, :] = source[quarter * n : quarter * n + quarter, :]
            grads[1, rows, :] = ctx_ref[rel, quarter * n : quarter * n + quarter, :]
    low = lax.broadcasted_iota(jnp.int32, (length, 128), 1) < HD
    zero = jnp.zeros((length, 128), BF)
    for p in range(heads // 2):
        cols = slice(128 * p, 128 * p + 128)
        scaled, keys = widen_pair(p, qkv_ref, key_feat, query_feat, key_wide, query_wide)
        keys_turned[cols, :] = keys
        grad, value = grads[0, :, cols], of_pair(qkv_ref, p, 2)
        for e in range(2):
            keep = low if e == 0 else ~low
            value_one[2 * p + e] = jnp.where(keep, value, zero)
            query_one[2 * p + e] = jnp.where(keep, scaled, zero)
            grad_one[2 * p + e] = jnp.where(keep, grad, zero)
        turned = grad.T
        grad_turned[cols, :] = turned
        product = turned.astype(F32) * grads[1, :, cols].T.astype(F32)
        for e in range(2):
            h = 2 * p + e
            inner_ref[h : h + 1, :] = jnp.sum(product[HD * e : HD * e + HD], axis=0, keepdims=True)
    dk[...] = jnp.zeros_like(dk)
    dv[...] = jnp.zeros_like(dv)

    def tile(i, _):
        qs = pl.ds(pl.multiple_of(i * TQ, TQ), TQ)
        start = lo_ref[i]

        def body(j, carry):
            ks = pl.ds(pl.multiple_of(start + j * TK, 128), TK)
            new = []
            for p in range(heads // 2):
                cols = slice(128 * p, 128 * p + 128)
                more_k, more_v = [], []
                for h in (2 * p, 2 * p + 1):
                    scores = nn(key_wide[h, ks, :], query_wide[h, :, qs])
                    prob = jnp.exp(scores - lse_ref[h : h + 1, qs])
                    grad_prob = nn(value_one[h, ks, :], grad_turned[cols, qs])
                    grad_scores = (prob * (grad_prob - inner_ref[h : h + 1, qs])).astype(BF)
                    new.append(carry[h] + nn(keys_turned[HD * h : HD * h + HD, ks], grad_scores))
                    more_k.append(nn(grad_scores, query_one[h, qs, :]))
                    more_v.append(nn(prob.astype(BF), grad_one[h, qs, :]))
                dk[ks, cols] += more_k[0] + more_k[1]
                dv[ks, cols] += more_v[0] + more_v[1]
            return tuple(new)

        found = lax.fori_loop(0, n_ref[i], body, (jnp.zeros((HD, TQ), F32),) * heads)
        for h in range(heads):
            dqt[HD * h : HD * h + HD, qs] = (found[h] * HD**-0.5).astype(BF)
        return 0

    lax.fori_loop(0, length // TQ, tile, 0)
    for p in range(heads // 2):
        cols = slice(128 * p, 128 * p + 128)
        for w, value in enumerate((dqt[cols, :].T, dk[:, cols].astype(BF), dv[:, cols].astype(BF))):
            out_ref[:, 384 * p + 128 * w : 384 * p + 128 * w + 128] = value


def attend_back(meta, qkv, number, own, oth, ctx, lse, part, seg_row, table, globs, lo, n):
    length = qkv.shape[0]
    heads, blocks = table.shape[:2]
    wide = heads * HD
    group = lambda w, i=number: pl.BlockSpec((length, w), lambda _: (0, i))
    half = pl.BlockSpec((length // 2, wide), lambda _: (0, number))
    return pl.pallas_call(
        attend_back_kernel,
        grid=(1,),
        in_specs=[smem()] * 4
        + [group(3 * wide), half, half, pl.BlockSpec((2, length // 2, wide), lambda _: (0, 0, part))]
        + [whole((heads, length)), whole((1, length)), whole((heads, blocks, 3))],
        out_specs=whole((length, 3 * wide)),
        out_shape=shape((length, 3 * wide), BF),
        scratch_shapes=[
            pltpu.VMEM((heads, HD, length), BF),
            pltpu.VMEM((HD, length), BF),
            pltpu.VMEM((heads, length, 128), BF),
            pltpu.VMEM((heads, 128, length), BF),
            pltpu.VMEM((heads, length, 128), BF),
            pltpu.VMEM((wide, length), BF),
            pltpu.VMEM((wide, length), BF),
            pltpu.VMEM((heads, length, 128), BF),
            pltpu.VMEM((heads, length, 128), BF),
            pltpu.VMEM((heads, length), F32),
            pltpu.VMEM((length, wide), F32),
            pltpu.VMEM((length, wide), F32),
            pltpu.VMEM((wide, length), BF),
            pltpu.VMEM((2, length, wide), BF),
        ],
        compiler_params=pltpu.CompilerParams(vmem_limit_bytes=VMEM_LIMIT),
        cost_estimate=pl.CostEstimate(
            flops=heads * length * length * 1500, bytes_accessed=20 * length * wide, transcendentals=heads * length * length // 2
        ),
        name="attend_back",
    )(meta, lo, n, globs, qkv, own, oth, ctx, lse, seg_row, table)


def key_ranges(segment):
    length = segment.shape[0]
    first, last = segment[::TQ], segment[TQ - 1 :: TQ]
    lo = jnp.sum(segment[None, :] < first[:, None], axis=1, dtype=jnp.int32) // 128 * 128
    hi = jnp.sum(segment[None, :] <= last[:, None], axis=1, dtype=jnp.int32)
    n = (hi - lo + TK - 1) // TK
    return jnp.minimum(lo, length - n * TK), n


def centre(value):
    centred = value - jnp.mean(value, axis=1, keepdims=True)
    rate = lax.rsqrt(jnp.mean(centred * centred, axis=1, keepdims=True) + EPSILON)
    return centred * rate, rate


def norm_back(grad, normed, rate):
    return rate * (
        grad
        - jnp.mean(grad, axis=1, keepdims=True)
        - normed * jnp.mean(grad * normed, axis=1, keepdims=True)
    )


def cut(value):
    half = value.shape[1] // 2
    return value[:, :half], value[:, half:]


def wide_target(proj, inner, down, half):
    width = proj.shape[2] // 2
    groups = inner.shape[2] // 2 // width

    def target(number, chip, rows):
        if number == 0:
            return proj.at[chip, rows, pl.ds(pl.multiple_of(half * width, 128), width)]
        if number <= groups:
            first = half * (groups * width) + width * (number - 1)
            return inner.at[chip, rows, pl.ds(pl.multiple_of(first, 128), width)]
        return down.at[chip, rows, pl.ds(pl.multiple_of(half * width, 128), width)]

    return target


def ffn_kernel(plan, pieces_n, ctx_n, *refs):
    meta = refs[0]
    own_pieces = refs[1 : 1 + pieces_n]
    oth_pieces = refs[1 + pieces_n : 1 + 2 * pieces_n]
    refs = refs[1 + 2 * pieces_n :]
    ctx_own, ctx_oth = refs[:ctx_n], refs[ctx_n : 2 * ctx_n]
    (x_ref, dout_ref, vec_ref,
     out_ref, hid_ref, gf_ref, low_ref, gp_ref, gr_ref, ga_ref, gc_own, gc_oth, ctx_ref, vg_ref,
     proj, inner, down, slope, sems) = refs[2 * ctx_n :]
    here = placed(meta)
    c = here["c"]
    step = pl.program_id(0)
    model = x_ref.shape[1]
    wide = hid_ref.shape[1]

    @pl.when(step == 0)
    def _():
        copies = []
        for rel, pieces in ((0, own_pieces), (1, oth_pieces)):
            target = wide_target(proj, inner, down, lax.rem(c + rel, 2))
            copies += move(plan, here, pieces, target, sems, len(copies))
        for copy in copies:
            copy.wait()
        vg_ref[...] = jnp.zeros_like(vg_ref)

    vec = lambda n: vec_ref[n : n + 1, :]
    w_proj = proj[...].reshape(model, model)
    w_inner = lambda j: inner[:, :, model * j : model * j + model].reshape(model, model)
    span = CHIPS * model // wide
    w_down = lambda j: down[span * j : span * j + span].reshape(model, model)
    own = jnp.concatenate([ref[...] for ref in ctx_own], axis=1)
    oth = jnp.concatenate([ref[...] for ref in ctx_oth], axis=1)
    context = jnp.concatenate([jnp.where(c == 0, own, oth), jnp.where(c == 0, oth, own)], axis=1)
    ctx_ref[...] = context
    attn = nn(context, w_proj)
    n1, rate1 = centre(x_ref[...].astype(F32) + (attn + vec(2)))
    x1 = n1 * vec(3) + vec(4)
    low = x1.astype(BF)
    low_ref[...] = low
    ffn = None
    chunks = wide // model
    for j in range(chunks):
        cols = slice(model * j, model * j + model)
        pre = nn(low, w_inner(j)) + vec(8 + j)
        below = 0.5 + 0.5 * lax.erf(pre * 0.7071067811865476)
        slope[:, cols] = below + pre * (jnp.exp(-0.5 * (pre * pre)) * 0.3989422804014327)
        hidden = (pre * below).astype(BF)
        hid_ref[:, cols] = hidden
        more = nn(hidden, w_down(j))
        ffn = more if ffn is None else ffn + more
    n2, rate2 = centre(x1 + (ffn + vec(5)))
    out_ref[...] = (n2 * vec(6) + vec(7)).astype(BF)

    total = lambda value: jnp.sum(value, axis=0, keepdims=True)
    grad = dout_ref[...].astype(F32)
    gr2 = norm_back(grad * vec(6), n2, rate2)
    gf = gr2.astype(BF)
    gf_ref[...] = gf
    vg_ref[6:7, :] += total(grad * n2)
    vg_ref[7:8, :] += total(grad)
    vg_ref[5:6, :] += total(gf.astype(F32))
    gx1 = gr2
    for j in range(chunks):
        cols = slice(model * j, model * j + model)
        gp = (nt(gf, w_down(j)) * slope[:, cols]).astype(BF)
        gp_ref[:, cols] = gp
        vg_ref[8 + j : 9 + j, :] += total(gp.astype(F32))
        gx1 = gx1 + nt(gp, w_inner(j))
    gr1 = norm_back(gx1 * vec(3), n1, rate1)
    gr_ref[...] = gr1
    ga = gr1.astype(BF)
    ga_ref[...] = ga
    vg_ref[3:4, :] += total(gx1 * n1)
    vg_ref[4:5, :] += total(gx1)
    vg_ref[2:3, :] += total(ga.astype(F32))
    gc = cut(nt(ga, w_proj))
    gc_own[...] = jnp.where(c == 0, gc[0], gc[1]).astype(BF)
    gc_oth[...] = jnp.where(c == 0, gc[1], gc[0]).astype(BF)


def feed_forward(plan, meta, own_pieces, oth_pieces, ctx, ctx_oth, x_own, d_own, vectors, wide):
    rows, model = x_own.shape
    half = model // 2
    tile = lambda n: pl.BlockSpec((TILE, n), lambda i: (i, 0))
    return pl.pallas_call(
        lambda *refs: ffn_kernel(plan, len(own_pieces), len(ctx), *refs),
        grid=(rows // TILE,),
        in_specs=[smem()]
        + [anywhere()] * (2 * len(own_pieces))
        + [pl.BlockSpec((None, TILE, v.shape[2]), lambda i: (0, i, 0)) for v in ctx]
        + [tile(v.shape[1]) for v in ctx_oth]
        + [tile(model), tile(model), whole(vectors.shape)],
        out_specs=[tile(model), tile(wide), tile(model), tile(model), tile(wide), tile(model), tile(model)]
        + [tile(half), tile(half), tile(model), whole((16, model))],
        out_shape=[
            shape((rows, model), BF),
            shape((rows, wide), BF),
            shape((rows, model), BF),
            shape((rows, model), BF),
            shape((rows, wide), BF),
            shape((rows, model), F32),
            shape((rows, model), BF),
            shape((rows, half), BF),
            shape((rows, half), BF),
            shape((rows, model), BF),
            shape((16, model), F32),
        ],
        scratch_shapes=[
            pltpu.VMEM((CHIPS, model // CHIPS, model), BF),
            pltpu.VMEM((CHIPS, model // CHIPS, wide), BF),
            pltpu.VMEM((CHIPS, wide // CHIPS, model), BF),
            pltpu.VMEM((TILE, wide), F32),
            pltpu.SemaphoreType.DMA((2 * plan.entries(),)),
        ],
        compiler_params=pltpu.CompilerParams(vmem_limit_bytes=VMEM_LIMIT),
        cost_estimate=pl.CostEstimate(
            flops=4 * rows * model * (model + 2 * wide), bytes_accessed=rows * (8 * wide + 20 * model), transcendentals=2 * rows * wide
        ),
        name="feed_forward",
    )(meta, *own_pieces, *oth_pieces, *ctx, *ctx_oth, x_own, d_own, vectors)


def weight_grads_kernel(plan, pieces_n, *refs):
    meta, hid_ref, gp_ref, gf_ref, low_ref, ctx_ref, ga_ref = refs[:7]
    own_pieces = refs[7 : 7 + pieces_n]
    oth_pieces = refs[7 + pieces_n : 7 + 2 * pieces_n]
    proj, inner, down, sems = refs[7 + 2 * pieces_n :]
    here = placed(meta)
    c = here["c"]
    step = pl.program_id(0)
    model = gf_ref.shape[1]
    span = CHIPS * model // inner.shape[2]
    steps = inner.shape[2] // model

    @pl.when(step == 0)
    def _():
        proj[...] = tn(ctx_ref[...], ga_ref[...]).reshape(proj.shape).astype(BF)

    more_inner = tn(low_ref[...], gp_ref[...])
    inner[:, :, pl.ds(pl.multiple_of(step * model, 128), model)] = more_inner.reshape(CHIPS, -1, model).astype(BF)
    more_down = tn(hid_ref[...], gf_ref[...])
    down[pl.ds(step * span, span)] = more_down.reshape(span, -1, model).astype(BF)

    @pl.when(step == steps - 1)
    def _():
        copies = []
        for rel, pieces in ((0, own_pieces), (1, oth_pieces)):
            target = wide_target(proj, inner, down, lax.rem(c + rel, 2))
            copies += move(plan, here, pieces, target, sems, len(copies), back=True)
        for copy in copies:
            copy.wait()


def weight_grads(plan, meta, hid, gp, gf, low, context, ga):
    rows, model = gf.shape
    wide, half = hid.shape[1], model // 2
    pieces = plan.shapes(half)
    cols = pl.BlockSpec((rows, model), lambda i: (0, i))
    found = pl.pallas_call(
        lambda *refs: weight_grads_kernel(plan, len(pieces), *refs),
        grid=(wide // model,),
        in_specs=[smem(), cols, cols] + [whole((rows, model))] * 4,
        out_specs=[anywhere()] * (2 * len(pieces)),
        out_shape=pieces * 2,
        scratch_shapes=[
            pltpu.VMEM((CHIPS, model // CHIPS, model), BF),
            pltpu.VMEM((CHIPS, model // CHIPS, wide), BF),
            pltpu.VMEM((CHIPS, wide // CHIPS, model), BF),
            pltpu.SemaphoreType.DMA((2 * plan.entries(),)),
        ],
        compiler_params=pltpu.CompilerParams(vmem_limit_bytes=VMEM_LIMIT),
        cost_estimate=pl.CostEstimate(
            flops=2 * rows * model * (model + 2 * wide), bytes_accessed=rows * (4 * wide + 8 * model), transcendentals=0
        ),
        name="weight_grads",
    )(meta, hid, gp, gf, low, context, ga)
    return found[: len(pieces)], found[len(pieces) :]


def gather_vectors(vectors, hidden, first, second, marks, hidden_marks):
    model = first.shape[1]
    one = nt((vectors[:, None, :] * marks[None]).reshape(-1, model).astype(BF), first)
    two = nt((hidden[:, None, :] * hidden_marks[None]).reshape(-1, model).astype(BF), second)
    laid = jnp.concatenate([one, two], axis=0).astype(BF)
    number = lax.broadcasted_iota(jnp.int32, (9 * CHIPS, 16 * CHIPS), 0)
    entry = lax.broadcasted_iota(jnp.int32, (9 * CHIPS, 16 * CHIPS), 1)
    picker = (entry == lax.rem(number, CHIPS) * 16 + number // CHIPS).astype(F32).astype(BF)
    return tn(picker, laid)


def qkv_grads_kernel(plan, pieces_n, groups, *refs):
    meta, x_ref = refs[:2]
    grads = refs[2 : 2 + groups]
    vg_ref, first, second, marks, hidden_marks = refs[2 + groups : 7 + groups]
    pieces = refs[7 + groups : 7 + groups + pieces_n]
    g_ref, rows_ref, vec_ref, sems = refs[7 + groups + pieces_n :]
    here = placed(meta)
    even = here["c"] == 0
    width = x_ref.shape[1] // 2
    x = x_ref[...]
    vec_ref[...] = vg_ref[...]
    none = jnp.zeros((1, 128), F32)
    for p, source in enumerate(grads):
        grad = source[...]
        g_ref[p] = tn(x, grad).reshape(g_ref.shape[1:]).astype(BF)
        summed = jnp.sum(grad.astype(F32), axis=0, keepdims=True)
        for row, w in ((0, 0), (1, 2)):
            value = summed[:, 128 * w : 128 * w + 128]
            vec_ref[row : row + 1, 128 * p : 128 * p + 128] = jnp.where(even, value, none)
            at = width + 128 * p
            vec_ref[row : row + 1, at : at + 128] = jnp.where(even, none, value)
    found = gather_vectors(vec_ref[0:8, :], vec_ref[8:12, :], first[...], second[...], marks[...], hidden_marks[...])
    rows_ref[...] = found.reshape(rows_ref.shape).astype(BF)

    def target(number, chip, rows):
        if number == 3:
            return rows_ref.at[chip, rows, :]
        return g_ref.at[number, chip, rows, :]

    for copy in move(plan, here, pieces, target, sems, 0, back=True):
        copy.wait()


def qkv_grads(plan, meta, x_full, grads, vg, tables):
    rows, model = x_full.shape
    width, depth = grads[0].shape[1], model // CHIPS
    pieces = plan.shapes(width)
    return pl.pallas_call(
        lambda *refs: qkv_grads_kernel(plan, len(pieces), len(grads), *refs),
        grid=(1,),
        in_specs=[smem(), whole((rows, model))]
        + [whole((rows, width))] * len(grads)
        + [whole(vg.shape)]
        + [whole(t.shape) for t in tables],
        out_specs=[anywhere()] * len(pieces),
        out_shape=pieces,
        scratch_shapes=[
            pltpu.VMEM((len(grads), CHIPS, depth, width), BF),
            pltpu.VMEM((CHIPS, 16, width), BF),
            pltpu.VMEM((16, model), F32),
            pltpu.SemaphoreType.DMA((plan.entries(),)),
        ],
        compiler_params=pltpu.CompilerParams(vmem_limit_bytes=VMEM_LIMIT),
        cost_estimate=pl.CostEstimate(
            flops=6 * rows * model * width, bytes_accessed=2 * rows * (model + 3 * width), transcendentals=0
        ),
        name="qkv_grads",
    )(meta, x_full, *grads, vg, *tables)


def input_grads_kernel(meta, *refs):
    *grads, w_ref, out_ref = refs
    width = grads[0].shape[1]
    total = None
    for p, source in enumerate(grads):
        weight = w_ref[:, :, width * p : width * p + width].reshape(-1, width)
        more = nt(source[...], weight)
        total = more if total is None else total + more
    out_ref[...] = total.astype(BF)


def input_grads(meta, grads, weights):
    rows, width = grads[0].shape
    model = weights.shape[0] * weights.shape[1]
    quarter = rows // 4
    part = pl.BlockSpec((quarter, width), lambda i, meta: (i, 0))
    return pl.pallas_call(
        input_grads_kernel,
        grid_spec=pltpu.PrefetchScalarGridSpec(
            num_scalar_prefetch=1,
            grid=(4,),
            in_specs=[part] * len(grads) + [whole(weights.shape)],
            out_specs=pl.BlockSpec(
                (None, quarter, model), lambda i, meta: (lax.rem(meta[0] + i, 2), i // 2, 0)
            ),
        ),
        out_shape=shape((2, 2 * quarter, model), BF),
        compiler_params=pltpu.CompilerParams(vmem_limit_bytes=VMEM_LIMIT),
        cost_estimate=pl.CostEstimate(
            flops=6 * rows * model * width, bytes_accessed=2 * rows * (model + 3 * width), transcendentals=0
        ),
        name="input_grads",
    )(meta, *grads, weights)


def body(
    tokens,
    qkv_weight,
    query_bias,
    value_bias,
    proj_weight,
    proj_bias,
    attn_gain,
    attn_shift,
    inner_weight,
    inner_bias,
    down_weight,
    down_bias,
    ffn_gain,
    ffn_shift,
    seg_ids,
    rand_blocks,
    glob_blocks,
    d_out,
):
    dp, seq = lax.axis_index("dp"), lax.axis_index("seq")
    members = lax.axis_size("dp") * lax.axis_size("seq")
    near = lax.axis_size("dp") == 2 * ZS
    y, c = seq // 2, seq % 2
    even, low_y = c == 0, y == 0
    meta = jnp.stack([c, dp % 2, y, dp // 2]).astype(jnp.int32)
    model = tokens.shape[3]
    half = model // 2
    ffw = inner_weight.shape[1]
    share, share_f = qkv_weight.shape[0], down_weight.shape[0]
    groups = ffw // 2 // half
    depth, deep = model // CHIPS, ffw // CHIPS
    by_parity = lambda mine, other: (jnp.where(even, mine, other), jnp.where(even, other, mine))

    def columns(h):
        qkv = [[model * w + half * h + 128 * p for w in range(3)] for p in range(half // 128)]
        return qkv, half * h, [ffw // 2 * h + half * g for g in range(groups)]

    pair = lambda kept, came: jnp.where(low_y, jnp.stack([kept, came]), jnp.stack([came, kept]))

    def to_chip(value, ready=(), late=()):
        kept = jnp.where(low_y, value[0], value[1])
        given = jnp.where(low_y, value[1], value[0])
        came = swap(after(given, *ready) if ready else given, "y")
        return pair(kept, after(came, *late) if late else came)

    vectors = (query_bias, value_bias, proj_bias, attn_gain, attn_shift, down_bias, ffn_gain, ffn_shift)
    sections_a, sections_b = [depth] * 3 + [16], [depth] * (1 + groups) + [deep]
    if near:
        plan_a = Plan(sections_a, 80)
        plan_b = Plan(sections_b, 256)

        x_own = to_chip(tokens[:, 0])
        mine, theirs = pack(meta, qkv_weight, proj_weight, inner_weight, down_weight)
        came = swap(theirs, "core")
        first, second = by_parity(mine, came)
        small = jnp.concatenate([jnp.pad(jnp.stack(vectors), ((0, 0), (0, 128 - share))),
                                 jnp.pad(inner_bias[None], ((0, 7), (0, 128 - share_f)))])
        small = jnp.concatenate(by_parity(small, swap(small, "core")) + (jnp.zeros_like(small),), axis=1)
        laid, at = [], 0
        for length in [share] * (4 + groups) + [share_f]:
            laid += [first[at : at + length], second[at : at + length]]
            at += length
        chunk_a = jnp.concatenate(laid[:6] + [small], axis=0)
        chunk_b = jnp.concatenate(laid[6:], axis=0)

        def split_z(chunk, plan):
            found = gather_z(chunk)
            return found[:, plan.cut :], found[:, : plan.cut]

        def first_side(a, b, *late):
            a_came, b_came = after(swap(a, "x"), *late), after(swap(b, "y"), *late)
            return jnp.concatenate([a, a_came]), jnp.concatenate([b, b_came])

        def second_side(a, b, *late):
            return [a, after(swap(a, "y"), *late), b, after(swap(b, "x"), *late)]

        za = split_z(chunk_a, plan_a)
        tables = spread_tables(model, depth // 2, deep // 2, chunk_a)
        x_oth = swap(x_own, "core")
        za = [after(v, x_oth) for v in za]
        zb = split_z(after(chunk_b, *za), plan_b)
        pieces_a = second_side(*first_side(*za))
    else:
        plan_a, plan_b = Plan(sections_a, None), Plan(sections_b, None)
        x_own = to_chip(tokens[:, 0])
        x_oth = swap(x_own, "core")
        tables = spread_tables(model, depth // 2, deep // 2)
        everyone = lambda w: lax.all_gather(w, ("dp", "seq"), axis=0, tiled=True)
        full_qkv, full_proj, full_inner, full_down = map(everyone, (qkv_weight, proj_weight, inner_weight, down_weight))
        row = everyone(jnp.concatenate(list(vectors) + [inner_bias])[None])
        full_vectors = row[:, : 8 * share].reshape(members, 8, share).transpose(1, 0, 2).reshape(8, CHIPS, 2, -1)
        full_bias = row[:, 8 * share :].reshape(1, CHIPS, 2, -1)
        padded = lambda v: jnp.pad(v, ((0, 0),) * 3 + ((0, 128 - v.shape[3]),))
        rows = jnp.concatenate([padded(full_vectors), padded(full_bias)], axis=0)
        rows = jnp.pad(rows, ((0, 7), (0, 0), (0, 1), (0, 0))).transpose(1, 0, 2, 3).reshape(CHIPS, 16, 384)

        def packed(h):
            qkv, first, inner = columns(h)
            col = lambda w, at, n=half: w[:, at : at + n].reshape(CHIPS, -1, n)
            a = [jnp.concatenate([col(full_qkv, at, 128) for at in p], axis=2) for p in qkv]
            b = [col(full_proj, first)] + [col(full_inner, at) for at in inner] + [col(full_down, first)]
            return jnp.concatenate(a + [rows], axis=1), jnp.concatenate(b, axis=1)

        zero, one = packed(0), packed(1)
        pieces_a = [jnp.where(even, zero[0], one[0])]
        own_b, oth_b = [[v] for v in by_parity(zero[1], one[1])]
        chunk_a = pieces_a[0]

    x_full = jnp.where(even, jnp.stack([x_own, x_oth], 1), jnp.stack([x_oth, x_own], 1)).reshape(-1, model)
    x_own = x_own.reshape(-1, model)
    segment = jnp.where(low_y, seg_ids[0, 0], seg_ids[1, 0])
    globs = jnp.where(low_y, glob_blocks[0, 0], glob_blocks[1, 0])
    lo, n = key_ranges(segment)
    blocks = rand_blocks[:, 0]
    of_chip = by_parity(blocks, swap(blocks, "core"))
    for_chip = jnp.where(low_y, *(jnp.concatenate([v[m] for v in of_chip]) for m in range(2)))
    for_other = jnp.where(low_y, *(jnp.concatenate([v[1 - m] for v in of_chip]) for m in range(2)))
    table = jnp.where(c == y, for_chip, swap(after(for_other, x_oth), "y"))

    qkv, w_qkv, spread = project_qkv(plan_a, meta, pieces_a, x_full, tables)
    spots = (segment[None], globs, lo, n)
    attention = lambda heads, number, source: attend(meta, source, number, spots[0], table[heads], *spots[1:])
    ctx_b, lse_b = attention(slice(4, 6), 2, qkv)
    ctx_b_oth = swap(ctx_b[1], "core")
    qkv_later = qkv
    if near:
        ones = first_side(*[after(v, x_full, *pieces_a) for v in zb], ctx_b)
        qkv_later = after(qkv, *ones)
    ctx_a, lse_a = attention(slice(0, 4), 0, qkv_later)
    ctx_a_oth = swap(ctx_a[1], "core")
    d_own = to_chip(d_out[:, 0], pieces_a, (ctx_a,)).reshape(-1, model)
    if near:
        own_b = second_side(*ones, ctx_a)
        oth_b = [swap(piece, "core") for piece in own_b]
    found = feed_forward(plan_b, meta, own_b, oth_b, [ctx_a, ctx_b], [ctx_a_oth, ctx_b_oth], x_own, d_own, spread, ffw)
    out, hid, gf, x1_low, gp, gr1, ga, gc_own, gc_oth, context, vg = found

    gc_came = swap(gc_oth, "core")
    grads_own, grads_oth = weight_grads(plan_b, meta, hid, gp, gf, x1_low, context, ga)
    layer_given = out.reshape(2, -1, model)

    def attention_back(p, *ready):
        ctx, lse, part = (ctx_a, lse_a, p) if p < 2 else (ctx_b, lse_b, 0)
        return attend_back(meta, qkv, p, after(gc_own, *ready), gc_came, ctx, lse[2 * part : 2 * part + 2], part, spots[0],
                           table[2 * p : 2 * p + 2], *spots[1:])

    if near:
        far = [add(grads_own[i], swap(grads_oth[i], "core")) for i in (1, 3)]
        grads = [attention_back(0, *far)]
        layer_out = to_chip(layer_given, (), (grads[0],))[:, None]
        close = [add(grads_own[i], after(swap(grads_oth[i], "core"), grads[0])) for i in (0, 2)]
        grads.append(attention_back(1, *close, layer_out))
        down_b = fold_first(*far, *close, grads[1])
        grads.append(attention_back(2, *down_b))
        down_b, ready = fold_second(*down_b, grads[2])
    else:
        grads = [attention_back(p) for p in range(3)]
        layer_out = to_chip(layer_given)[:, None]
        ready = ()
    grads_qkv = qkv_grads(plan_a, meta, x_full, [after(grads[0], *ready)] + grads[1:], vg, tables)
    back = input_grads(meta, [after(grads[0], grads_qkv[0])] + grads[1:], w_qkv)
    grad_own = gr1 + (back[0].astype(F32) + swap(back[1], "core").astype(F32))
    grad_input = to_chip(grad_own.astype(BF).reshape(2, -1, model))[:, None]

    if near:
        down_a = fold_first(*[grads_qkv[i] for i in (1, 3, 0, 2)], back)
        total_b = scatter_z(down_b, *down_a)
        down_a, _ = fold_second(*down_a, grad_own)
        total_a = scatter_z(after(down_a, total_b), grad_input)
        kept, given = by_parity(total_a[3 * depth :, :128], total_a[3 * depth :, 128:256])
        small = kept + swap(given, "core")
        small = jnp.concatenate([small[v, :share] for v in range(8)] + [small[8, :share_f]])

        def finish(total, lengths):
            mine, theirs, at = [], [], 0
            for length in lengths:
                kept, given = by_parity(total[at : at + length], total[at + length : at + 2 * length])
                mine.append(kept)
                theirs.append(given)
                at += 2 * length
            mine = jnp.concatenate(mine, axis=0)
            came = swap(jnp.concatenate(theirs, axis=0).astype(BF), "core").astype(F32)
            halves, cuts, at = by_parity(mine, came), [], 0
            for length in lengths:
                cuts.append([v[at : at + length] for v in halves])
                at += length
            return cuts

        cuts_a = finish(total_a, [share] * 3)
        cuts_b = finish(total_b, [share] * (1 + groups) + [share_f])
    else:
        scatter = lambda v: lax.psum_scatter(v.astype(F32), ("dp", "seq"), scatter_dimension=0, tiled=True)
        found = grads_qkv[0][:, 3 * depth :].astype(F32)
        found = jnp.stack([found[:, :, :128], found[:, :, 128:256]], axis=1).transpose(2, 0, 1, 3)
        small = jnp.concatenate([found[v, :, :, :depth // 2].reshape(-1, 1) for v in range(8)], axis=1)
        small = jnp.concatenate([small.reshape(members, share, 8).transpose(0, 2, 1).reshape(members, -1),
                                 found[8, :, :, : deep // 2].reshape(members, share_f)], axis=1)
        small = scatter(small)[0]
        zero = jnp.zeros((model, half), BF)
        cuts_a, at = [], 0
        for length in sections_a[:3]:
            part = grads_qkv[0][:, at : at + length].reshape(-1, half)
            cuts_a.append([scatter(v) for v in by_parity(part, zero)])
            at += length
        halves = by_parity(grads_own[0], grads_oth[0])
        cuts_b, at = [], 0
        for length in sections_b:
            cuts_b.append([scatter(v[:, at : at + length].reshape(-1, half)) for v in halves])
            at += length
    cut_w = lambda h, p, w: cuts_a[p][h][:, 128 * w : 128 * w + 128]
    grad_qkv = jnp.concatenate([cut_w(h, p, w) for w in range(3) for h in range(2) for p in range(3)], axis=1)
    grad_proj = jnp.concatenate(cuts_b[0], axis=1)
    grad_inner = jnp.concatenate([cuts_b[1 + g][h] for h in range(2) for g in range(groups)], axis=1)
    grad_down = jnp.concatenate(cuts_b[1 + groups], axis=1)
    vector = [small[share * i : share * i + share] for i in range(8)]
    return (
        layer_out,
        grad_input,
        grad_qkv,
        vector[0],
        vector[1],
        grad_proj,
        vector[2],
        vector[3],
        vector[4],
        grad_inner,
        small[8 * share :],
        grad_down,
        vector[5],
        vector[6],
        vector[7],
    )


def solution(mesh):
    row, vec = P(("dp", "seq"), None), P(("dp", "seq"))
    wide = P(None, "dp", "seq", None)
    return jax.shard_map(
        body,
        mesh=mesh,
        in_specs=(wide, row, vec, vec, row, vec, vec, vec, row, vec, row, vec, vec, vec)
        + (P(None, "dp", None), P(None, "dp", "seq", None, None), P(None, "dp", None), wide),
        out_specs=(wide, wide, row, vec, vec, row, vec, vec, vec, row, vec, row, vec, vec, vec),
        check_vma=False,
    )
```

```python
import jax
import jax.numpy as jnp
from jax import lax
from jax.experimental import pallas as pl
from jax.experimental.pallas import tpu as pltpu
from jax.sharding import PartitionSpec as P

HD = 64
BLOCK = 64
EPSILON = 1e-06
BIG = float(2.0**100)
LOWEST = -3.0e38
TQ = 256
TK = 512
CHIPS = 16
TILE = 256
BF = jnp.bfloat16
F32 = jnp.float32
VMEM_LIMIT = 60 << 20
COST = 1.0
CUT = 320
BACK_CUT = 224


def nn(left, right):
    return lax.dot_general(left, right, (((1,), (0,)), ((), ())), preferred_element_type=F32)


def nt(left, right):
    return lax.dot_general(left, right, (((1,), (1,)), ((), ())), preferred_element_type=F32)


def tn(left, right):
    return lax.dot_general(left, right, (((0,), (0,)), ((), ())), preferred_element_type=F32)


def smem():
    return pl.BlockSpec(memory_space=pltpu.SMEM)


def anywhere():
    return pl.BlockSpec(memory_space=pl.ANY)


def cost(flops, bytes_accessed, transcendentals):
    part = lambda value: int(value * COST)
    return pl.CostEstimate(flops=part(flops), bytes_accessed=part(bytes_accessed), transcendentals=part(transcendentals))


def shape(dims, kind):
    return jax.ShapeDtypeStruct(dims, kind)


def after(value, *ready):
    if not ready:
        return value
    return lax.optimization_barrier((value,) + ready)[0]


def swap(value, dim):
    if dim == "x":
        return lax.ppermute(value, "dp", [(d, d ^ 1) for d in range(lax.axis_size("dp"))])
    bit = 1 if dim == "core" else 2
    return lax.ppermute(value, "seq", [(s, s ^ bit) for s in range(4)])


def shift_z(value, by):
    size = lax.axis_size("dp") // 2
    return lax.ppermute(value, "dp", [(2 * z + x, (z + by) % size * 2 + x) for z in range(size) for x in range(2)])


ZS = 4


def stage(*values):
    return lax.optimization_barrier(values)


def shifts_z(chunk, *by):
    return [shift_z(chunk, k) for k in by]


def scatter_z(total, *by):
    return [shift_z(total[r], ZS - r) for r in by]


def split_rows(value, cut):
    return value[:, cut:], value[:, :cut]


def added(*values):
    return sum(v.astype(F32) for v in values)


def add(*values):
    return added(*values).astype(BF)


def chip_at(order, near, index, here):
    z = lax.rem(here["z"] - index % ZS + ZS, ZS)
    near = {order[0]: near[0], order[1]: near[1]}
    return z * 4 + lax.rem(here["x"] + near["x"], 2) * 2 + lax.rem(here["y"] + near["y"], 2)


def placed(meta):
    return {"c": meta[0], "x": meta[1], "y": meta[2], "z": meta[3]}


class Plan:
    def __init__(self, sections, cut, joined=False):
        self.sections, self.cut, self.joined = sections, cut, joined
        self.rows = sum(sections)

    def pieces(self):
        if self.cut is None:
            return [(0, self.rows, None, [None] * CHIPS)]
        found = []
        if not self.joined:
            found.append((0, self.rows, "xy", [(0, 0)] * ZS))
        for first, end, order in ((self.cut, self.rows, "xy"), (0, self.cut, "yx")):
            if self.joined:
                found += [(first, end, order, [(m // ZS, last) for m in range(2 * ZS)]) for last in range(2)]
            else:
                found += [(first, end, order, [sides] * ZS) for sides in ((1, 0), (0, 1), (1, 1))]
        return found

    def shapes(self, width):
        return [shape((len(sides), end - first, width), BF) for first, end, _, sides in self.pieces()]

    def walk(self, here):
        for piece, (first, end, order, sides) in enumerate(self.pieces()):
            for m, side in enumerate(sides):
                chip = m if side is None else chip_at(order, side, m, here)
                start = 0
                for number, length in enumerate(self.sections):
                    lo, hi = max(start, first), min(start + length, end)
                    if lo < hi:
                        yield piece, m, lo - first, hi - first, chip, number, lo - start
                    start += length

    def entries(self):
        return sum(1 for _ in self.walk({"c": 0, "x": 0, "y": 0, "z": 0}))


def move(plan, here, pieces, target, sems, base, numbers=None, back=False):
    copies = []
    for i, (p, m, lo, hi, chip, number, at) in enumerate(plan.walk(here)):
        if numbers is None or number in numbers:
            near, far = pieces[p].at[m, lo:hi, :], target(number, chip, slice(at, at + hi - lo))
            if back:
                near, far = far, near
            copies.append(pltpu.make_async_copy(near, far, sems.at[base + i]))
    return copies


def run(copies):
    for copy in copies:
        copy.start()
    for copy in copies:
        copy.wait()


def spread_vectors(rows, first, second, marks, hidden_marks):
    count = rows.shape[0]
    number = lax.broadcasted_iota(jnp.int32, (9 * CHIPS, count), 0)
    entry = lax.broadcasted_iota(jnp.int32, (9 * CHIPS, count), 1)
    picker = (entry == lax.rem(number, CHIPS) * 16 + number // CHIPS).astype(F32).astype(BF)
    picked = nn(picker, rows).astype(BF)
    model = first.shape[1]
    vectors = nn(picked[: 8 * CHIPS], first).reshape(8, CHIPS, model) * marks[None]
    hidden = nn(picked[8 * CHIPS :], second).reshape(4, 4, model) * hidden_marks[None]
    return jnp.sum(vectors, axis=1), jnp.sum(hidden, axis=1)


def spread_tables(model, share, share_f, *ready):
    lane, col = jnp.arange(384)[:, None], jnp.arange(model)[None, :]
    if ready:
        lane = after(lane, *ready)
    first = (lane == 128 * (col // share % 2) + col % share).astype(BF)
    second = (lane == 128 * (col // share_f % 2) + col % share_f).astype(BF)
    marks = (jnp.arange(CHIPS)[:, None] == col // (2 * share)).astype(F32)
    hidden_marks = (jnp.arange(4)[:, None] == col // (2 * share_f)).astype(F32)
    return first, second, marks, hidden_marks


def pack_kernel(meta, qkv_ref, proj_ref, inner_ref, down_ref, mine_ref, theirs_ref):
    model = proj_ref.shape[1]
    half, share = model // 2, proj_ref.shape[0]
    for rel, out in ((0, mine_ref), (1, theirs_ref)):
        h = lax.rem(meta[0] + rel, 2)
        lanes = lambda first, n: pl.ds(pl.multiple_of(first, 128), n)
        at = 0
        for p in range(half // 128):
            for w in range(3):
                out[at : at + share, 128 * w : 128 * w + 128] = qkv_ref[:, lanes(model * w + half * h + 128 * p, 128)]
            at += share
        out[at : at + share, :] = proj_ref[:, lanes(half * h, half)]
        at += share
        for g in range(inner_ref.shape[1] // 2 // half):
            out[at : at + share, :] = inner_ref[:, lanes(inner_ref.shape[1] // 2 * h + half * g, half)]
            at += share
        out[at : at + down_ref.shape[0], :] = down_ref[:, lanes(half * h, half)]


def pack(meta, qkv, proj, inner, down):
    half = proj.shape[1] // 2
    rows = proj.shape[0] * (half // 128 + 1 + inner.shape[1] // 2 // half) + down.shape[0]
    return pl.pallas_call(
        pack_kernel,
        in_specs=[smem()] + [pl.BlockSpec(memory_space=pltpu.VMEM)] * 4,
        out_specs=[pl.BlockSpec(memory_space=pltpu.VMEM)] * 2,
        out_shape=[shape((rows, half), BF)] * 2,
        cost_estimate=cost(flops=0, bytes_accessed=8 * rows * half, transcendentals=0),
        name="pack",
    )(meta, qkv, proj, inner, down)


def qkv_kernel(plan, pieces_n, *refs):
    meta = refs[0]
    pieces = refs[1 : 1 + pieces_n]
    own_ref, oth_ref, first, second, marks, hidden_marks, out_ref, w_ref, vec_ref, rows_ref, bias_ref, sems = refs[1 + pieces_n :]
    here = placed(meta)
    wide = out_ref.shape[1]
    third = wide // 3

    @pl.when(pl.program_id(0) == 0)
    def _():
        def target(number, chip, rows):
            if number == 3:
                return rows_ref.at[chip, rows, :]
            return w_ref.at[chip, rows, third * number : third * number + third]

        run(move(plan, here, pieces, target, sems, 0))
        rows = rows_ref[...].reshape(CHIPS * 16, 384)
        vectors, hidden = spread_vectors(rows, first[...], second[...], marks[...], hidden_marks[...])
        vec_ref[0:8, :] = vectors
        vec_ref[8:12, :] = hidden
        vec_ref[12:16, :] = jnp.zeros_like(hidden)
        mine = jnp.where(here["c"] == 0, vectors[:, :third], vectors[:, third:])
        bias_ref[...] = jnp.zeros_like(bias_ref)
        for p in range(3):
            for w, source in ((0, 0), (2, 1)):
                at = third * p + 128 * w
                bias_ref[0:1, at : at + 128] = mine[source : source + 1, 128 * p : 128 * p + 128]

    weight = w_ref[...].reshape(-1, wide)
    x = jnp.where(pl.program_id(0) < 2, own_ref[...], oth_ref[...])
    out_ref[...] = (nn(x, weight) + bias_ref[0:1, :]).astype(BF)


def project_qkv(plan, meta, pieces, x_own, x_oth, tables):
    _, tile, model = x_own.shape
    rows = 4 * tile
    width, depth = model // 2, model // CHIPS
    wide = 3 * width
    full = lambda dims: pl.BlockSpec(dims, lambda i, meta: (0,) * len(dims))
    return pl.pallas_call(
        lambda *refs: qkv_kernel(plan, len(pieces), *refs),
        grid_spec=pltpu.PrefetchScalarGridSpec(
            num_scalar_prefetch=1,
            grid=(4,),
            in_specs=[anywhere()] * len(pieces)
            + [pl.BlockSpec((None, tile, model), lambda i, meta: (jnp.minimum(i, 1), 0, 0))]
            + [pl.BlockSpec((None, tile, model), lambda i, meta: (jnp.maximum(i - 2, 0), 0, 0))]
            + [full(t.shape) for t in tables],
            out_specs=[
                pl.BlockSpec((tile, wide), lambda i, meta: (2 * lax.rem(i, 2) + lax.rem(meta[0] + i // 2, 2), 0)),
                full((CHIPS, depth, wide)),
                full((16, model)),
            ],
            scratch_shapes=[
                pltpu.VMEM((CHIPS, 16, width), BF),
                pltpu.VMEM((8, wide), F32),
                pltpu.SemaphoreType.DMA((plan.entries(),)),
            ],
        ),
        out_shape=[shape((rows, wide), BF), shape((CHIPS, depth, wide), BF), shape((16, model), F32)],
        compiler_params=pltpu.CompilerParams(vmem_limit_bytes=VMEM_LIMIT),
        cost_estimate=cost(
            flops=2 * rows * model * wide, bytes_accessed=2 * rows * (model + wide), transcendentals=0
        ),
        name="project_qkv",
    )(meta, *pieces, x_own, x_oth, *tables)


def fill_features(seg_ref, rand_ref, first_global, second_global, key_ref, query_ref):
    heads, _, length = key_ref.shape
    blocks = length // BLOCK
    at = lax.broadcasted_iota(jnp.int32, (blocks, length), 1) // BLOCK
    row = lax.broadcasted_iota(jnp.int32, (blocks, length), 0)
    seen = jnp.abs(at - row) <= 1
    for chosen in (first_global, second_global):
        seen = seen | (at == chosen) | (row == chosen)
    same = lax.broadcasted_iota(jnp.int32, (HD - blocks, length), 0) == seg_ref[...]
    for h in range(heads):
        picked = seen
        for r in range(rand_ref.shape[2]):
            picked = picked | (at == rand_ref[h, :, r : r + 1])
        key_ref[h, 0:blocks, :] = jnp.where(picked, 0.0, 1.0).astype(BF)
        key_ref[h, blocks:HD, :] = jnp.where(same, 0.0, 1.0).astype(BF)
    query_ref[0:blocks, :] = jnp.where(at == row, -BIG, 0.0).astype(BF)
    query_ref[blocks:HD, :] = jnp.where(same, -BIG, 0.0).astype(BF)


def of_pair(ref, p, w):
    return ref[:, 384 * p + 128 * w : 384 * p + 128 * w + 128]


def widen_pair(p, qkv_ref, key_feat, query_feat, key_wide, query_wide):
    scaled = of_pair(qkv_ref, p, 0) * BF(HD**-0.5)
    queries, keys = scaled.T, of_pair(qkv_ref, p, 1).T
    a, b = 2 * p, 2 * p + 1
    query_wide[a, 0:HD, :] = queries[0:HD]
    query_wide[a, HD:128, :] = query_feat[...]
    query_wide[b, 0:HD, :] = query_feat[...]
    query_wide[b, HD:128, :] = queries[HD:128]
    key_wide[a] = jnp.concatenate([keys[0:HD], key_feat[a]], axis=0).T
    key_wide[b] = jnp.concatenate([key_feat[b], keys[HD:128]], axis=0).T
    return scaled, keys


def over_keys(start, n, step, carry):
    carry = lax.fori_loop(0, n // 2, lambda j, carry: step(start + j * TK, j * TK, TK, carry), carry)
    done = n // 2 * TK
    return lax.fori_loop(0, lax.rem(n, 2), lambda j, carry: step(start + done, done, TK // 2, carry), carry)


def attend_kernel(meta, lo_ref, n_ref, glob_ref, qkv_ref, seg_ref, rand_ref, own_ref, oth_ref, lse_ref,
                  key_feat, query_feat, key_wide, query_wide, values, turned, store):
    heads, length = lse_ref.shape
    fill_features(seg_ref, rand_ref, glob_ref[0], glob_ref[1], key_feat, query_feat)
    for p in range(heads // 2):
        widen_pair(p, qkv_ref, key_feat, query_feat, key_wide, query_wide)
        values[128 * p : 128 * p + 128, :] = of_pair(qkv_ref, p, 2).T

    def tile(i, _):
        qs = pl.ds(pl.multiple_of(i * TQ, TQ), TQ)

        def scan(start, at, size, tops):
            ks = pl.ds(pl.multiple_of(start, 128), size)
            to = pl.ds(pl.multiple_of(at, TK), size)
            raised = []
            for h in range(heads):
                scores = nn(key_wide[h, ks, :], query_wide[h, :, qs])
                store[h, to, :] = scores
                raised.append(jnp.maximum(tops[h], jnp.max(scores.reshape(size // 8, 8, TQ), axis=0)))
            return tuple(raised)

        tops = over_keys(lo_ref[i], n_ref[i], scan, (jnp.full((8, TQ), LOWEST, F32),) * heads)
        tops = [jnp.max(top, axis=0, keepdims=True) for top in tops]

        def collect(start, at, size, carry):
            ks = pl.ds(pl.multiple_of(start, 128), size)
            to = pl.ds(pl.multiple_of(at, TK), size)
            new = []
            for h in range(heads):
                total, summed = carry[h]
                expo = jnp.exp(store[h, to, :] - tops[h])
                total = total + jnp.sum(expo.reshape(size // 8, 8, TQ), axis=0)
                summed = summed + nn(values[HD * h : HD * h + HD, ks], expo.astype(BF))
                new.append((total, summed))
            return tuple(new)

        none = (jnp.zeros((8, TQ), F32), jnp.zeros((HD, TQ), F32))
        found = over_keys(lo_ref[i], n_ref[i], collect, (none,) * heads)
        for h in range(heads):
            total, summed = found[h]
            total = jnp.sum(total, axis=0, keepdims=True)
            turned[HD * h : HD * h + HD, qs] = (summed / total).astype(BF)
            lse_ref[h : h + 1, qs] = tops[h] + jnp.log(total)
        return 0

    lax.fori_loop(0, length // TQ, tile, 0)
    quarter = length // 4
    even = meta[0] == 0
    for p in range(heads // 2):
        result = turned[128 * p : 128 * p + 128, :].T
        for n in range(2):
            one, two = (result[quarter * k : quarter * k + quarter] for k in (2 * n, 2 * n + 1))
            where = (slice(quarter * n, quarter * n + quarter), slice(128 * p, 128 * p + 128))
            own_ref[where] = jnp.where(even, one, two)
            oth_ref[where] = jnp.where(even, two, one)


def whole(dims):
    return pl.BlockSpec(dims, lambda *_: (0,) * len(dims))


def attend(meta, qkv, number, seg_row, table, globs, lo, n):
    length = qkv.shape[0]
    heads, blocks = table.shape[:2]
    wide = heads * HD
    return pl.pallas_call(
        attend_kernel,
        grid=(1,),
        in_specs=[smem()] * 4
        + [pl.BlockSpec((length, 3 * wide), lambda i: (0, number)), whole((1, length)), whole((heads, blocks, 3))],
        out_specs=[whole((length // 2, wide))] * 2 + [whole((heads, length))],
        out_shape=[shape((length // 2, wide), BF)] * 2 + [shape((heads, length), F32)],
        scratch_shapes=[
            pltpu.VMEM((heads, HD, length), BF),
            pltpu.VMEM((HD, length), BF),
            pltpu.VMEM((heads, length, 128), BF),
            pltpu.VMEM((heads, 128, length), BF),
            pltpu.VMEM((wide, length), BF),
            pltpu.VMEM((wide, length), BF),
            pltpu.VMEM((heads, length, TQ), F32),
        ],
        compiler_params=pltpu.CompilerParams(vmem_limit_bytes=VMEM_LIMIT),
        cost_estimate=cost(
            flops=heads * length * length * 700, bytes_accessed=10 * length * wide, transcendentals=heads * length * length // 2
        ),
        name="attend",
    )(meta, lo, n, globs, qkv, seg_row, table)


def attend_back_kernel(meta, lo_ref, n_ref, glob_ref, qkv_ref, own_ref, oth_ref, ctx_own, ctx_oth, lse_ref, seg_ref,
                       rand_ref, out_ref, key_feat, query_feat, key_wide, query_wide, value_one,
                       grad_turned, keys_turned, query_one, grad_one, inner_ref, dk, dv, dqt, grads):
    heads, length = lse_ref.shape
    quarter = length // 4
    fill_features(seg_ref, rand_ref, glob_ref[0], glob_ref[1], key_feat, query_feat)
    for rel, source, ctx in ((0, own_ref, ctx_own), (1, oth_ref, ctx_oth)):
        for n in range(2):
            at = 2 * n + lax.rem(meta[0] + rel, 2)
            rows = pl.ds(pl.multiple_of(at * quarter, quarter), quarter)
            grads[0, rows, :] = source[quarter * n : quarter * n + quarter, :]
            grads[1, rows, :] = ctx[quarter * n : quarter * n + quarter, :]
    low = lax.broadcasted_iota(jnp.int32, (length, 128), 1) < HD
    zero = jnp.zeros((length, 128), BF)
    for p in range(heads // 2):
        cols = slice(128 * p, 128 * p + 128)
        scaled, keys = widen_pair(p, qkv_ref, key_feat, query_feat, key_wide, query_wide)
        keys_turned[cols, :] = keys
        grad, value = grads[0, :, cols], of_pair(qkv_ref, p, 2)
        for e in range(2):
            keep = low if e == 0 else ~low
            value_one[2 * p + e] = jnp.where(keep, value, zero)
            query_one[2 * p + e] = jnp.where(keep, scaled, zero)
            grad_one[2 * p + e] = jnp.where(keep, grad, zero)
        turned = grad.T
        grad_turned[cols, :] = turned
        product = turned.astype(F32) * grads[1, :, cols].T.astype(F32)
        for e in range(2):
            h = 2 * p + e
            inner_ref[h : h + 1, :] = jnp.sum(product[HD * e : HD * e + HD], axis=0, keepdims=True)
    dk[...] = jnp.zeros_like(dk)
    dv[...] = jnp.zeros_like(dv)

    def tile(i, _):
        qs = pl.ds(pl.multiple_of(i * TQ, TQ), TQ)

        def body(start, at, size, carry):
            ks = pl.ds(pl.multiple_of(start, 128), size)
            new = []
            for p in range(heads // 2):
                cols = slice(128 * p, 128 * p + 128)
                more_k, more_v = [], []
                for h in (2 * p, 2 * p + 1):
                    scores = nn(key_wide[h, ks, :], query_wide[h, :, qs])
                    prob = jnp.exp(scores - lse_ref[h : h + 1, qs])
                    grad_prob = nn(value_one[h, ks, :], grad_turned[cols, qs])
                    grad_scores = (prob * (grad_prob - inner_ref[h : h + 1, qs])).astype(BF)
                    new.append(carry[h] + nn(keys_turned[HD * h : HD * h + HD, ks], grad_scores))
                    more_k.append(nn(grad_scores, query_one[h, qs, :]))
                    more_v.append(nn(prob.astype(BF), grad_one[h, qs, :]))
                dk[ks, cols] += more_k[0] + more_k[1]
                dv[ks, cols] += more_v[0] + more_v[1]
            return tuple(new)

        found = over_keys(lo_ref[i], n_ref[i], body, (jnp.zeros((HD, TQ), F32),) * heads)
        for h in range(heads):
            dqt[HD * h : HD * h + HD, qs] = (found[h] * HD**-0.5).astype(BF)
        return 0

    lax.fori_loop(0, length // TQ, tile, 0)
    for p in range(heads // 2):
        cols = slice(128 * p, 128 * p + 128)
        for w, value in enumerate((dqt[cols, :].T, dk[:, cols].astype(BF), dv[:, cols].astype(BF))):
            out_ref[:, 384 * p + 128 * w : 384 * p + 128 * w + 128] = value


def attend_back(meta, qkv, number, own, oth, ctx, ctx_oth, lse, part, seg_row, table, globs, lo, n):
    length = qkv.shape[0]
    heads, blocks = table.shape[:2]
    wide = heads * HD
    group = lambda w, i=number: pl.BlockSpec((length, w), lambda _: (0, i))
    half = pl.BlockSpec((length // 2, wide), lambda _: (0, number))
    return pl.pallas_call(
        attend_back_kernel,
        grid=(1,),
        in_specs=[smem()] * 4
        + [group(3 * wide), half, half]
        + [pl.BlockSpec((length // 2, wide), lambda _: (0, part))] * 2
        + [whole((heads, length)), whole((1, length)), whole((heads, blocks, 3))],
        out_specs=whole((length, 3 * wide)),
        out_shape=shape((length, 3 * wide), BF),
        scratch_shapes=[
            pltpu.VMEM((heads, HD, length), BF),
            pltpu.VMEM((HD, length), BF),
            pltpu.VMEM((heads, length, 128), BF),
            pltpu.VMEM((heads, 128, length), BF),
            pltpu.VMEM((heads, length, 128), BF),
            pltpu.VMEM((wide, length), BF),
            pltpu.VMEM((wide, length), BF),
            pltpu.VMEM((heads, length, 128), BF),
            pltpu.VMEM((heads, length, 128), BF),
            pltpu.VMEM((heads, length), F32),
            pltpu.VMEM((length, wide), F32),
            pltpu.VMEM((length, wide), F32),
            pltpu.VMEM((wide, length), BF),
            pltpu.VMEM((2, length, wide), BF),
        ],
        compiler_params=pltpu.CompilerParams(vmem_limit_bytes=VMEM_LIMIT),
        cost_estimate=cost(
            flops=heads * length * length * 1500, bytes_accessed=20 * length * wide, transcendentals=heads * length * length // 2
        ),
        name="attend_back",
    )(meta, lo, n, globs, qkv, own, oth, ctx, ctx_oth, lse, seg_row, table)


def key_ranges(segment):
    length = segment.shape[0]
    first, last = segment[::TQ], segment[TQ - 1 :: TQ]
    lo = jnp.sum(segment[None, :] < first[:, None], axis=1, dtype=jnp.int32) // 128 * 128
    hi = jnp.sum(segment[None, :] <= last[:, None], axis=1, dtype=jnp.int32)
    n = (hi - lo + TK // 2 - 1) // (TK // 2)
    return jnp.minimum(lo, length - n * (TK // 2)), n


def centre(value):
    centred = value - jnp.mean(value, axis=1, keepdims=True)
    rate = lax.rsqrt(jnp.mean(centred * centred, axis=1, keepdims=True) + EPSILON)
    return centred * rate, rate


def norm_back(grad, normed, rate):
    return rate * (
        grad
        - jnp.mean(grad, axis=1, keepdims=True)
        - normed * jnp.mean(grad * normed, axis=1, keepdims=True)
    )


def cut(value):
    half = value.shape[1] // 2
    return value[:, :half], value[:, half:]


def wide_target(proj, inner, down, half):
    width = proj.shape[2] // 2
    groups = inner.shape[2] // 2 // width

    def target(number, chip, rows):
        if number == 0:
            return proj.at[chip, rows, pl.ds(pl.multiple_of(half * width, 128), width)]
        if number <= groups:
            first = half * (groups * width) + width * (number - 1)
            return inner.at[chip, rows, pl.ds(pl.multiple_of(first, 128), width)]
        return down.at[chip, rows, pl.ds(pl.multiple_of(half * width, 128), width)]

    return target


def ffn_kernel(plan, pieces_n, ctx_n, *refs):
    meta = refs[0]
    own_pieces = refs[1 : 1 + pieces_n]
    oth_pieces = refs[1 + pieces_n : 1 + 2 * pieces_n]
    refs = refs[1 + 2 * pieces_n :]
    ctx_own, ctx_oth = refs[:ctx_n], refs[ctx_n : 2 * ctx_n]
    (x_ref, dout_ref, vec_ref,
     kept_ref, given_ref, gr_kept, gr_given, hid_ref, gf_ref, low_ref, gp_ref, ga_ref, gc_own, gc_oth, ctx_ref, vg_ref,
     proj, inner, down, slope, sems) = refs[2 * ctx_n :]
    here = placed(meta)
    c = here["c"]
    step = pl.program_id(0)
    model = x_ref.shape[1]
    wide = hid_ref.shape[1]

    def copies(*numbers):
        found = []
        for rel, pieces in ((0, own_pieces), (1, oth_pieces)):
            target = wide_target(proj, inner, down, lax.rem(c + rel, 2))
            found += move(plan, here, pieces, target, sems, rel * plan.entries(), numbers)
        return found

    first, last = 0, len(plan.sections) - 1
    orders = [(first,), tuple(range(1, last)), (last,)]

    @pl.when(step == 0)
    def _():
        for numbers in orders:
            for copy in copies(*numbers):
                copy.start()
        vg_ref[...] = jnp.zeros_like(vg_ref)

    def arrived(which):
        @pl.when(step == 0)
        def _():
            for copy in copies(*orders[which]):
                copy.wait()

    vec = lambda n: vec_ref[n : n + 1, :]
    w_proj = lambda: proj[...].reshape(model, model)
    w_inner = lambda j: inner[:, :, model * j : model * j + model].reshape(model, model)
    span = CHIPS * model // wide
    w_down = lambda j: down[span * j : span * j + span].reshape(model, model)
    own = jnp.concatenate([ref[...] for ref in ctx_own], axis=1)
    oth = jnp.concatenate([ref[...] for ref in ctx_oth], axis=1)
    context = jnp.concatenate([jnp.where(c == 0, own, oth), jnp.where(c == 0, oth, own)], axis=1)
    ctx_ref[...] = context
    arrived(0)
    attn = nn(context, w_proj())
    n1, rate1 = centre(x_ref[...].astype(F32) + (attn + vec(2)))
    x1 = n1 * vec(3) + vec(4)
    low = x1.astype(BF)
    low_ref[...] = low
    ffn = None
    chunks = wide // model
    arrived(1)
    arrived(2)
    for j in range(chunks):
        cols = slice(model * j, model * j + model)
        pre = nn(low, w_inner(j)) + vec(8 + j)
        below = 0.5 + 0.5 * lax.erf(pre * 0.7071067811865476)
        slope[:, cols] = below + pre * (jnp.exp(-0.5 * (pre * pre)) * 0.3989422804014327)
        hidden = (pre * below).astype(BF)
        hid_ref[:, cols] = hidden
        more = nn(hidden, w_down(j))
        ffn = more if ffn is None else ffn + more
    n2, rate2 = centre(x1 + (ffn + vec(5)))
    out = (n2 * vec(6) + vec(7)).astype(BF)
    stays = step // 2 == here["y"]

    @pl.when(stays)
    def _():
        kept_ref[...] = out

    @pl.when(jnp.logical_not(stays))
    def _():
        given_ref[...] = out


    total = lambda value: jnp.sum(value, axis=0, keepdims=True)
    grad = dout_ref[...].astype(F32)
    gr2 = norm_back(grad * vec(6), n2, rate2)
    gf = gr2.astype(BF)
    gf_ref[...] = gf
    vg_ref[6:7, :] += total(grad * n2)
    vg_ref[7:8, :] += total(grad)
    vg_ref[5:6, :] += total(gf.astype(F32))
    gx1 = gr2
    for j in range(chunks):
        cols = slice(model * j, model * j + model)
        gp = (nt(gf, w_down(j)) * slope[:, cols]).astype(BF)
        gp_ref[:, cols] = gp
        vg_ref[8 + j : 9 + j, :] += total(gp.astype(F32))
        gx1 = gx1 + nt(gp, w_inner(j))
    gr1 = norm_back(gx1 * vec(3), n1, rate1)

    @pl.when(stays)
    def _():
        gr_kept[...] = gr1

    @pl.when(jnp.logical_not(stays))
    def _():
        gr_given[...] = gr1

    ga = gr1.astype(BF)
    ga_ref[...] = ga
    vg_ref[3:4, :] += total(gx1 * n1)
    vg_ref[4:5, :] += total(gx1)
    vg_ref[2:3, :] += total(ga.astype(F32))
    gc = cut(nt(ga, w_proj()))
    gc_own[...] = jnp.where(c == 0, gc[0], gc[1]).astype(BF)
    gc_oth[...] = jnp.where(c == 0, gc[1], gc[0]).astype(BF)


def feed_forward(plan, meta, own_pieces, oth_pieces, ctx, ctx_oth, x_own, d_own, vectors, wide):
    rows, model = x_own.shape
    half = model // 2
    tile = lambda n: pl.BlockSpec((TILE, n), lambda i, meta: (i, 0))
    full = lambda dims: pl.BlockSpec(dims, lambda i, meta: (0,) * len(dims))
    side = lambda mine: pl.BlockSpec(
        (TILE, model), lambda i, meta: (jnp.clip(i - (2 * meta[2] if mine else 2 - 2 * meta[2]), 0, 1), 0)
    )
    scratch = [
        pltpu.VMEM((CHIPS, model // CHIPS, model), BF),
        pltpu.VMEM((CHIPS, model // CHIPS, wide), BF),
        pltpu.VMEM((CHIPS, wide // CHIPS, model), BF),
        pltpu.VMEM((TILE, wide), F32),
        pltpu.SemaphoreType.DMA((2 * plan.entries(),)),
    ]
    outs = [(wide, BF), (model, BF), (model, BF), (wide, BF), (model, BF), (half, BF), (half, BF), (model, BF)]
    return pl.pallas_call(
        lambda *refs: ffn_kernel(plan, len(own_pieces), len(ctx), *refs),
        grid_spec=pltpu.PrefetchScalarGridSpec(
            num_scalar_prefetch=1,
            grid=(rows // TILE,),
            in_specs=[anywhere()] * (2 * len(own_pieces))
            + [tile(v.shape[1]) for v in ctx + ctx_oth]
            + [tile(model), tile(model), full(vectors.shape)],
            out_specs=[side(True), side(False)] * 2 + [tile(w) for w, _ in outs] + [full((16, model))],
            scratch_shapes=scratch,
        ),
        out_shape=[shape((rows // 2, model), BF)] * 2 + [shape((rows // 2, model), F32)] * 2 + [shape((rows, w), kind) for w, kind in outs] + [shape((16, model), F32)],
        compiler_params=pltpu.CompilerParams(vmem_limit_bytes=VMEM_LIMIT),
        cost_estimate=cost(
            flops=4 * rows * model * (model + 2 * wide), bytes_accessed=rows * (8 * wide + 20 * model), transcendentals=2 * rows * wide
        ),
        name="feed_forward",
    )(meta, *own_pieces, *oth_pieces, *ctx, *ctx_oth, x_own, d_own, vectors)


def weight_grads_kernel(plan, pieces_n, *refs):
    meta, hid_ref, gp_ref, gf_ref, low_ref, ctx_ref, ga_ref = refs[:7]
    own_pieces = refs[7 : 7 + pieces_n]
    oth_pieces = refs[7 + pieces_n : 7 + 2 * pieces_n]
    proj, inner, down, sems = refs[7 + 2 * pieces_n :]
    here = placed(meta)
    c = here["c"]
    step = pl.program_id(0)
    model = gf_ref.shape[1]
    span = CHIPS * model // inner.shape[2]
    steps = inner.shape[2] // model

    @pl.when(step == 0)
    def _():
        proj[...] = tn(ctx_ref[...], ga_ref[...]).reshape(proj.shape).astype(BF)

    more_inner = tn(low_ref[...], gp_ref[...])
    inner[:, :, pl.ds(pl.multiple_of(step * model, 128), model)] = more_inner.reshape(CHIPS, -1, model).astype(BF)
    more_down = tn(hid_ref[...], gf_ref[...])
    down[pl.ds(step * span, span)] = more_down.reshape(span, -1, model).astype(BF)

    @pl.when(step == steps - 1)
    def _():
        copies = []
        for rel, pieces in ((0, own_pieces), (1, oth_pieces)):
            target = wide_target(proj, inner, down, lax.rem(c + rel, 2))
            copies += move(plan, here, pieces, target, sems, len(copies), back=True)
        run(copies)


def weight_grads(plan, meta, hid, gp, gf, low, context, ga):
    rows, model = gf.shape
    wide, half = hid.shape[1], model // 2
    pieces = plan.shapes(half)
    cols = pl.BlockSpec((rows, model), lambda i: (0, i))
    found = pl.pallas_call(
        lambda *refs: weight_grads_kernel(plan, len(pieces), *refs),
        grid=(wide // model,),
        in_specs=[smem(), cols, cols] + [whole((rows, model))] * 4,
        out_specs=[anywhere()] * (2 * len(pieces)),
        out_shape=pieces * 2,
        scratch_shapes=[
            pltpu.VMEM((CHIPS, model // CHIPS, model), BF),
            pltpu.VMEM((CHIPS, model // CHIPS, wide), BF),
            pltpu.VMEM((CHIPS, wide // CHIPS, model), BF),
            pltpu.SemaphoreType.DMA((2 * plan.entries(),)),
        ],
        compiler_params=pltpu.CompilerParams(vmem_limit_bytes=VMEM_LIMIT),
        cost_estimate=cost(
            flops=2 * rows * model * (model + 2 * wide), bytes_accessed=rows * (4 * wide + 8 * model), transcendentals=0
        ),
        name="weight_grads",
    )(meta, hid, gp, gf, low, context, ga)
    return found[: len(pieces)], found[len(pieces) :]


def gather_vectors(vectors, hidden, first, second, marks, hidden_marks):
    model = first.shape[1]
    one = nt((vectors[:, None, :] * marks[None]).reshape(-1, model).astype(BF), first)
    two = nt((hidden[:, None, :] * hidden_marks[None]).reshape(-1, model).astype(BF), second)
    laid = jnp.concatenate([one, two], axis=0).astype(BF)
    number = lax.broadcasted_iota(jnp.int32, (9 * CHIPS, 16 * CHIPS), 0)
    entry = lax.broadcasted_iota(jnp.int32, (9 * CHIPS, 16 * CHIPS), 1)
    picker = (entry == lax.rem(number, CHIPS) * 16 + number // CHIPS).astype(F32).astype(BF)
    return tn(picker, laid)


def qkv_grads_kernel(plan, pieces_n, pairs, number, last, *refs):
    meta, own_ref, oth_ref = refs[:3]
    grads = refs[3 : 3 + pairs]
    refs = refs[3 + pairs :]
    if last:
        (known_ref, vg_ref, first, second, marks, hidden_marks), refs = refs[:6], refs[6:]
    pieces, refs = refs[:pieces_n], refs[pieces_n:]
    if last:
        g_ref, sems, rows_ref, vec_ref, sums_ref = refs
    else:
        sums_ref, g_ref, sems = refs
    here = placed(meta)
    quarter, width = own_ref.shape[1], own_ref.shape[2] // 2
    sums_ref[...] = known_ref[...] if last else jnp.zeros_like(sums_ref)
    for p, source in enumerate(grads):
        total = None
        for rel, x_ref in ((0, own_ref), (1, oth_ref)):
            for n in range(2):
                at = 2 * n + lax.rem(here["c"] + rel, 2)
                more = tn(x_ref[n], source[pl.ds(pl.multiple_of(at * quarter, quarter), quarter), :])
                total = more if total is None else total + more
        g_ref[p] = total.reshape(g_ref.shape[1:]).astype(BF)
        sums_ref[number + p : number + p + 1, :] = jnp.sum(source[...].astype(F32), axis=0, keepdims=True)
    if last:
        even = here["c"] == 0
        vec_ref[...] = vg_ref[...]
        none = jnp.zeros((1, 128), F32)
        for p in range(number + pairs):
            for row, w in ((0, 0), (1, 2)):
                value = sums_ref[p : p + 1, 128 * w : 128 * w + 128]
                vec_ref[row : row + 1, 128 * p : 128 * p + 128] = jnp.where(even, value, none)
                at = width + 128 * p
                vec_ref[row : row + 1, at : at + 128] = jnp.where(even, none, value)
        found = gather_vectors(vec_ref[0:8, :], vec_ref[8:12, :], first[...], second[...], marks[...], hidden_marks[...])
        rows_ref[...] = found.reshape(rows_ref.shape).astype(BF)

    def target(section, chip, rows):
        if section == pairs:
            return rows_ref.at[chip, rows, :]
        return g_ref.at[section, chip, rows, :]

    run(move(plan, here, pieces, target, sems, 0, back=True))


def qkv_grads(plan, meta, x_own, x_oth, grads, number, sums=None, vg=None, tables=()):
    rows, model = 4 * x_own.shape[1], x_own.shape[2]
    width, depth = grads[0].shape[1], model // CHIPS
    last = vg is not None
    pieces = plan.shapes(width)
    more = [sums, vg, *tables] if last else []
    summed = shape((8, width), F32)
    found = pl.pallas_call(
        lambda *refs: qkv_grads_kernel(plan, len(pieces), len(grads), number, last, *refs),
        grid=(1,),
        in_specs=[smem(), whole(x_own.shape), whole(x_own.shape)]
        + [whole((rows, width))] * len(grads)
        + [whole(v.shape) for v in more],
        out_specs=[anywhere()] * len(pieces) + ([] if last else [whole(summed.shape)]),
        out_shape=pieces + ([] if last else [summed]),
        scratch_shapes=[
            pltpu.VMEM((len(grads), CHIPS, depth, width), BF),
            pltpu.SemaphoreType.DMA((plan.entries(),)),
        ]
        + ([pltpu.VMEM((CHIPS, 16, width), BF), pltpu.VMEM((16, model), F32), pltpu.VMEM((8, width), F32)] if last else []),
        compiler_params=pltpu.CompilerParams(vmem_limit_bytes=VMEM_LIMIT),
        cost_estimate=cost(
            flops=2 * len(grads) * rows * model * width, bytes_accessed=2 * rows * (model + 3 * width), transcendentals=0
        ),
        name="qkv_grads",
    )(meta, x_own, x_oth, *grads, *more)
    return found if last else (found[:-1], found[-1])


def input_grads_kernel(meta, *refs):
    *grads, w_ref, own_ref, oth_ref = refs
    width = grads[0].shape[1]
    total = None
    for p, source in enumerate(grads):
        weight = w_ref[:, :, width * p : width * p + width].reshape(-1, width)
        more = nt(source[...], weight)
        total = more if total is None else total + more

    @pl.when(pl.program_id(0) == 0)
    def _():
        oth_ref[...] = total.astype(BF)

    @pl.when(pl.program_id(0) == 1)
    def _():
        own_ref[...] = total.astype(BF)


def input_grads(meta, grads, weights, given):
    rows, width = grads[0].shape
    model = weights.shape[0] * weights.shape[1]
    quarter = rows // 4
    half = lambda meta: 1 - meta[2] if given else meta[2]
    at = lambda i, meta: 2 * half(meta) + lax.rem(meta[0] + 1 + i, 2)
    return pl.pallas_call(
        input_grads_kernel,
        grid_spec=pltpu.PrefetchScalarGridSpec(
            num_scalar_prefetch=1,
            grid=(2,),
            in_specs=[pl.BlockSpec((quarter, width), lambda i, meta: (at(i, meta), 0))] * len(grads) + [whole(weights.shape)],
            out_specs=[whole((quarter, model))] * 2,
        ),
        out_shape=[shape((quarter, model), BF)] * 2,
        compiler_params=pltpu.CompilerParams(vmem_limit_bytes=VMEM_LIMIT),
        cost_estimate=cost(
            flops=3 * rows * model * width, bytes_accessed=rows * (model + 3 * width), transcendentals=0
        ),
        name="input_grads",
    )(meta, *grads, weights)


def body(
    tokens,
    qkv_weight,
    query_bias,
    value_bias,
    proj_weight,
    proj_bias,
    attn_gain,
    attn_shift,
    inner_weight,
    inner_bias,
    down_weight,
    down_bias,
    ffn_gain,
    ffn_shift,
    seg_ids,
    rand_blocks,
    glob_blocks,
    d_out,
):
    dp, seq = lax.axis_index("dp"), lax.axis_index("seq")
    members = lax.axis_size("dp") * lax.axis_size("seq")
    near = lax.axis_size("dp") == 2 * ZS
    y, c = seq // 2, seq % 2
    even, low_y = c == 0, y == 0
    meta = jnp.stack([c, dp % 2, y, dp // 2]).astype(jnp.int32)
    model = tokens.shape[3]
    half = model // 2
    ffw = inner_weight.shape[1]
    share, share_f = qkv_weight.shape[0], down_weight.shape[0]
    groups = ffw // 2 // half
    depth, deep = model // CHIPS, ffw // CHIPS
    by_parity = lambda mine, other: (jnp.where(even, mine, other), jnp.where(even, other, mine))

    pair = lambda kept, came: jnp.where(low_y, jnp.stack([kept, came]), jnp.stack([came, kept]))

    def given_kept(value):
        return jnp.where(low_y, value[1], value[0]), jnp.where(low_y, value[0], value[1])

    vectors = (query_bias, value_bias, proj_bias, attn_gain, attn_shift, down_bias, ffn_gain, ffn_shift)
    sections_a, sections_b = [depth] * 3 + [16], [depth] * (1 + groups) + [deep]
    lengths_a, lengths_b = [share] * 3, [share] * (1 + groups) + [share_f]
    segment = jnp.where(low_y, seg_ids[0, 0], seg_ids[1, 0])
    globs = jnp.where(low_y, glob_blocks[0, 0], glob_blocks[1, 0])
    lo, n = key_ranges(segment)
    blocks = rand_blocks[:, 0]
    x_given, x_kept = given_kept(tokens[:, 0])

    def pick_blocks(came):
        of_chip = by_parity(blocks, came)
        mine = jnp.where(low_y, *(jnp.concatenate([v[m] for v in of_chip]) for m in range(2)))
        return mine, jnp.where(low_y, *(jnp.concatenate([v[1 - m] for v in of_chip]) for m in range(2)))

    def attention(heads, number, qkv, table):
        return attend(meta, qkv, number, segment[None], table[heads], globs, lo, n)

    def attention_back(p, qkv, own, oth, ctx, ctx_oth, lse, table):
        part = p if p < 2 else 0
        return attend_back(meta, qkv, p, own, oth, ctx, ctx_oth, lse, part, segment[None], table[2 * p : 2 * p + 2], globs, lo, n)

    if near:
        plan_a, plan_b = Plan(sections_a, 80), Plan(sections_b, CUT)
        back_b = Plan(sections_b, BACK_CUT, True)
        back_early, back_late = Plan([depth] * 2, depth, True), Plan([depth, 16], 32, True)
        mine, theirs = pack(meta, qkv_weight, proj_weight, inner_weight, down_weight)
        came = swap(theirs, "core")
        small = jnp.concatenate([jnp.pad(jnp.stack(vectors), ((0, 0), (0, 128 - share))),
                                 jnp.pad(inner_bias[None], ((0, 7), (0, 128 - share_f)))])
        small = jnp.concatenate(by_parity(small, swap(small, "core")) + (jnp.zeros_like(small),), axis=1)
        first, second = by_parity(mine, came)
        laid, at = [], 0
        for length in lengths_a + lengths_b:
            laid += [first[at : at + length], second[at : at + length]]
            at += length
        chunk_a = jnp.concatenate(laid[:6] + [small], axis=0)
        chunk_b = jnp.concatenate(laid[6:], axis=0)
        chunk_a, chunk_b, x_given = stage(chunk_a, chunk_b, x_given)

        za = shifts_z(chunk_a, 1, 2, 3)
        x_came = swap(x_given, "y")
        blocks_came = swap(blocks, "core")
        zb = shifts_z(chunk_b, 1)
        chunk_a, chunk_b, x_came, blocks_came, *rest = stage(chunk_a, chunk_b, x_came, blocks_came, *za, *zb)
        za, zb = rest[:3], rest[3:]

        near_a = jnp.stack([chunk_a] + za)
        a, b = split_rows(near_a, plan_a.cut)
        a_x, b_y, a_y, b_x = swap(a, "x"), swap(b, "y"), swap(a, "y"), swap(b, "x")
        zb += shifts_z(chunk_b, 2)
        near_a, a_x, b_y, a_y, b_x, x_came, blocks_came, chunk_b, *zb = stage(
            near_a, a_x, b_y, a_y, b_x, x_came, blocks_came, chunk_b, *zb
        )
        x_own = pair(x_kept, x_came)
        x_oth = swap(x_own, "core")
        a_xy, b_yx = swap(a_x, "y"), swap(b_y, "x")
        zb += shifts_z(chunk_b, 3)
        blocks_mine, blocks_given = pick_blocks(blocks_came)
        blocks_came = swap(blocks_given, "y")
        tables = spread_tables(model, depth // 2, deep // 2, chunk_b)
        a_xy, b_yx, blocks_came, chunk_b, x_own, x_oth, *rest = stage(
            a_xy, b_yx, blocks_came, chunk_b, x_own, x_oth, *tables, *zb
        )
        tables, zb = rest[:4], rest[4:]
        pieces = [near_a, a_x, a_y, a_xy, b_y, b_x, b_yx]

        table = jnp.where(c == y, blocks_mine, blocks_came)
        near_b = jnp.stack([chunk_b] + zb)
        a, b = split_rows(near_b, plan_b.cut)
        a_x, b_y, a_y, b_x = swap(a, "x"), swap(b, "y"), swap(a, "y"), swap(b, "x")
        near_oth = swap(near_b, "core")
        qkv, w_qkv, spread = project_qkv(plan_a, meta, pieces, x_own, x_oth, tables)
        ctx_b, ctx_b_give, lse_b = attention(slice(4, 6), 2, qkv, table)
        d_given, d_kept = given_kept(after(d_out[:, 0], chunk_b))
        near_b, near_oth, a_x, b_y, a_y, b_x, qkv, ctx_b, ctx_b_give, d_given = stage(
            near_b, near_oth, a_x, b_y, a_y, b_x, qkv, ctx_b, ctx_b_give, d_given
        )

        a_xy, b_yx = swap(a_x, "y"), swap(b_y, "x")
        d_came = swap(d_given, "y")
        early = [a_x, a_y, b_y, b_x]
        early_oth = [swap(v, "core") for v in early]
        ctx_b_oth = swap(ctx_b_give, "core")
        ctx_a, ctx_a_give, lse_a = attention(slice(0, 4), 0, qkv, table)
        a_xy, b_yx, d_came, ctx_b_oth, ctx_a, ctx_a_give, *early_oth = stage(
            a_xy, b_yx, d_came, ctx_b_oth, ctx_a, ctx_a_give, *early_oth
        )
        own_b = [near_b] + early[:2] + [a_xy] + early[2:] + [b_yx]
        oth_b = [near_oth] + early_oth[:2] + [swap(a_xy, "core")] + early_oth[2:] + [swap(b_yx, "core")]
        ctx_a_oth = swap(ctx_a_give, "core")
        d_own = pair(d_kept, d_came).reshape(-1, model)
        found = feed_forward(plan_b, meta, own_b, oth_b, [ctx_a, ctx_b], [ctx_a_oth, ctx_b_oth], x_own.reshape(-1, model),
                             d_own, spread, ffw)
        out_kept, out_given, gr_kept, gr_given, hid, gf, x1_low, gp, ga, gc_own, gc_oth, context, vg = found

        out_came, gc_came = swap(out_given, "y"), swap(gc_oth, "core")
        grads_own, grads_oth = weight_grads(back_b, meta, hid, gp, gf, x1_low, context, ga)
        out_came, gc_came, *rest = stage(out_came, gc_came, *grads_own, *grads_oth)
        a, a_far, b, b_far, a_oth, a_far_oth, b_oth, b_far_oth = rest
        layer_out = pair(out_kept, out_came)[:, None]
        a_far, b_far = add(a_far, swap(a_far_oth, "core")), add(b_far, swap(b_far_oth, "core"))
        a_far, b_far, gc_came, a_oth, b_oth = stage(a_far, b_far, gc_came, a_oth, b_oth)

        a_came, b_came = swap(a_far, "y"), swap(b_far, "x")
        a_oth, b_oth = swap(a_oth, "core"), swap(b_oth, "core")
        back = lambda p, own, ctx, oth, lse: attention_back(p, qkv, own, gc_came, ctx, oth, lse, table)
        grad_0 = back(0, gc_own, ctx_a, ctx_a_give, lse_a[0:2])
        a_came, b_came, a_oth, b_oth, grad_0, gc_own = stage(a_came, b_came, a_oth, b_oth, grad_0, gc_own)
        a, b = add(a, a_oth, a_came), add(b, b_oth, b_came)
        a_came, b_came = swap(a[ZS:], "x"), swap(b[ZS:], "y")
        grad_1 = back(1, gc_own, ctx_a, ctx_a_give, lse_a[2:4])
        a, b, a_came, b_came, grad_1, gc_own = stage(a, b, a_came, b_came, grad_1, gc_own)
        total = jnp.concatenate([add(b[:ZS], b_came), add(a[:ZS], a_came)], axis=1)
        came_b = scatter_z(total, 1, 2, 3)
        (qa, qa_far, qb, qb_far), sums = qkv_grads(back_early, meta, x_own, x_oth, [grad_0, grad_1], 0)
        qa_came, qb_came = swap(qa_far, "y"), swap(qb_far, "x")
        grad_2 = back(2, after(gc_own, sums), ctx_b, ctx_b_give, lse_b)
        total, qa, qb, qa_came, qb_came, sums, grad_2, *came_b = stage(total, qa, qb, qa_came, qb_came, sums, grad_2, *came_b)
        ra, ra_far, rb, rb_far = qkv_grads(back_late, meta, x_own, x_oth, [grad_2], 2, sums, vg, tables)
        ra_came, rb_came = swap(ra_far, "y"), swap(rb_far, "x")
        grads = [grad_0, grad_1, after(grad_2, ra)]
        own_given, oth_given = input_grads(meta, grads, w_qkv, True)
        oth_given = swap(oth_given, "core")
        total_b = added(total[0], *came_b)
        ra, rb, ra_came, rb_came, own_given, oth_given, total_b = stage(
            ra, rb, ra_came, rb_came, own_given, oth_given, total_b
        )
        gx_came = swap(add(gr_given, own_given, oth_given), "y")
        qa = jnp.concatenate([add(qa, qa_came), add(ra, ra_came)], axis=1)
        qb = jnp.concatenate([add(qb, qb_came), add(rb, rb_came)], axis=1)
        qa_came, qb_came = swap(qa[ZS:], "x"), swap(qb[ZS:], "y")
        own_kept, oth_kept = input_grads(meta, [grad_0, grad_1, after(grad_2, qa)], w_qkv, False)
        qa, qb, qa_came, qb_came, own_kept, oth_kept = stage(qa, qb, qa_came, qb_came, own_kept, oth_kept)
        total = jnp.concatenate([add(qb[:ZS], qb_came), add(qa[:ZS], qa_came)], axis=1)
        came = scatter_z(total, 1, 2, 3)
        oth_kept = swap(oth_kept, "core")
        gx_kept = add(gr_kept, own_kept, oth_kept)

        def finish(total, lengths):
            mine, theirs, at = [], [], 0
            for length in lengths:
                kept, given = by_parity(total[at : at + length], total[at + length : at + 2 * length])
                mine.append(kept)
                theirs.append(given)
                at += 2 * length
            mine = jnp.concatenate(mine, axis=0)
            came = swap(jnp.concatenate(theirs, axis=0).astype(BF), "core").astype(F32)
            halves, cuts, at = by_parity(mine, came), [], 0
            for length in lengths:
                cuts.append([v[at : at + length] for v in halves])
                at += length
            return cuts

        cuts_b = finish(total_b, lengths_b)
        gx_came, gx_kept, total, *came = stage(gx_came, gx_kept, total, *came)
        grad_input = pair(gx_kept, gx_came)[:, None]
        total_a = added(total[0], *came)
        ends = (0, depth, depth + 32, 2 * depth + 32, 3 * depth)
        one, three, two, rest = (total_a[i:j] for i, j in zip(ends[:4], ends[1:]))
        total_a = jnp.concatenate([one, two, three, rest, total_a[3 * depth :]])
        cuts_a = finish(total_a, lengths_a)
        kept, given = by_parity(total_a[3 * depth :, :128], total_a[3 * depth :, 128:256])
        small = kept + swap(given, "core")
        small = jnp.concatenate([small[v, :share] for v in range(8)] + [small[8, :share_f]])
    else:
        plan_a, plan_b = Plan(sections_a, None), Plan(sections_b, None)
        everyone = lambda w: lax.all_gather(w, ("dp", "seq"), axis=0, tiled=True)
        full_qkv, full_proj, full_inner, full_down = map(everyone, (qkv_weight, proj_weight, inner_weight, down_weight))
        row = everyone(jnp.concatenate(list(vectors) + [inner_bias])[None])
        full_vectors = row[:, : 8 * share].reshape(members, 8, share).transpose(1, 0, 2).reshape(8, CHIPS, 2, -1)
        full_bias = row[:, 8 * share :].reshape(1, CHIPS, 2, -1)
        padded = lambda v: jnp.pad(v, ((0, 0),) * 3 + ((0, 128 - v.shape[3]),))
        rows = jnp.concatenate([padded(full_vectors), padded(full_bias)], axis=0)
        rows = jnp.pad(rows, ((0, 7), (0, 0), (0, 1), (0, 0))).transpose(1, 0, 2, 3).reshape(CHIPS, 16, 384)

        def packed(h):
            col = lambda w, at, width=half: w[:, at : at + width].reshape(CHIPS, -1, width)
            a = [
                jnp.concatenate([col(full_qkv, model * w + half * h + 128 * p, 128) for w in range(3)], axis=2)
                for p in range(3)
            ]
            b = [col(full_proj, half * h)] + [col(full_inner, ffw // 2 * h + half * g) for g in range(groups)]
            return jnp.concatenate(a + [rows], axis=1), jnp.concatenate(b + [col(full_down, half * h)], axis=1)

        zero, one = packed(0), packed(1)
        pieces_a = [jnp.where(even, zero[0], one[0])]
        own_b, oth_b = [[v] for v in by_parity(zero[1], one[1])]
        tables = spread_tables(model, depth // 2, deep // 2)
        x_own = pair(x_kept, swap(x_given, "y"))
        x_oth = swap(x_own, "core")
        d_given, d_kept = given_kept(d_out[:, 0])
        d_own = pair(d_kept, swap(d_given, "y")).reshape(-1, model)
        blocks_mine, blocks_given = pick_blocks(swap(blocks, "core"))
        table = jnp.where(c == y, blocks_mine, swap(blocks_given, "y"))
        qkv, w_qkv, spread = project_qkv(plan_a, meta, pieces_a, x_own, x_oth, tables)
        ctx_a, ctx_a_give, lse_a = attention(slice(0, 4), 0, qkv, table)
        ctx_b, ctx_b_give, lse_b = attention(slice(4, 6), 2, qkv, table)
        ctx_oth = [swap(v, "core") for v in (ctx_a_give, ctx_b_give)]
        found = feed_forward(plan_b, meta, own_b, oth_b, [ctx_a, ctx_b], ctx_oth, x_own.reshape(-1, model), d_own, spread, ffw)
        out_kept, out_given, gr_kept, gr_given, hid, gf, x1_low, gp, ga, gc_own, gc_oth, context, vg = found
        layer_out = pair(out_kept, swap(out_given, "y"))[:, None]
        gc_came = swap(gc_oth, "core")
        grads_own, grads_oth = weight_grads(plan_b, meta, hid, gp, gf, x1_low, context, ga)
        ctxs = [(ctx_a, ctx_a_give, lse_a[2 * p : 2 * p + 2]) for p in range(2)] + [(ctx_b, ctx_b_give, lse_b)]
        grads = [attention_back(p, qkv, gc_own, gc_came, *ctxs[p], table) for p in range(3)]
        pieces = qkv_grads(plan_a, meta, x_own, x_oth, grads, 0, jnp.zeros((8, 3 * 128), F32), vg, tables)
        own_given, oth_given = input_grads(meta, grads, w_qkv, True)
        own_kept, oth_kept = input_grads(meta, grads, w_qkv, False)
        gx_came = swap(add(gr_given, own_given, swap(oth_given, "core")), "y")
        grad_input = pair(add(gr_kept, own_kept, swap(oth_kept, "core")), gx_came)[:, None]
        scatter = lambda v: lax.psum_scatter(v.astype(F32), ("dp", "seq"), scatter_dimension=0, tiled=True)
        found = pieces[0][:, 3 * depth :].astype(F32)
        found = jnp.stack([found[:, :, :128], found[:, :, 128:256]], axis=1).transpose(2, 0, 1, 3)
        small = jnp.concatenate([found[v, :, :, : depth // 2].reshape(-1, 1) for v in range(8)], axis=1)
        small = jnp.concatenate([small.reshape(members, share, 8).transpose(0, 2, 1).reshape(members, -1),
                                 found[8, :, :, : deep // 2].reshape(members, share_f)], axis=1)
        small = scatter(small)[0]
        zero = jnp.zeros((model, half), BF)
        cuts_a, cuts_b = [], []
        for p in range(3):
            part = pieces[0][:, depth * p : depth * p + depth].reshape(-1, half)
            cuts_a.append([scatter(v) for v in by_parity(part, zero)])
        halves, at = by_parity(grads_own[0], grads_oth[0]), 0
        for length in sections_b:
            cuts_b.append([scatter(v[:, at : at + length].reshape(-1, half)) for v in halves])
            at += length

    cut_w = lambda h, p, w: cuts_a[p][h][:, 128 * w : 128 * w + 128]
    grad_qkv = jnp.concatenate([cut_w(h, p, w) for w in range(3) for h in range(2) for p in range(3)], axis=1)
    grad_proj = jnp.concatenate(cuts_b[0], axis=1)
    grad_inner = jnp.concatenate([cuts_b[1 + g][h] for h in range(2) for g in range(groups)], axis=1)
    grad_down = jnp.concatenate(cuts_b[1 + groups], axis=1)
    vector = [small[share * i : share * i + share] for i in range(8)]
    return (
        layer_out,
        grad_input,
        grad_qkv,
        vector[0],
        vector[1],
        grad_proj,
        vector[2],
        vector[3],
        vector[4],
        grad_inner,
        small[8 * share :],
        grad_down,
        vector[5],
        vector[6],
        vector[7],
    )


def solution(mesh):
    row, vec = P(("dp", "seq"), None), P(("dp", "seq"))
    wide = P(None, "dp", "seq", None)
    return jax.shard_map(
        body,
        mesh=mesh,
        in_specs=(wide, row, vec, vec, row, vec, vec, vec, row, vec, row, vec, vec, vec)
        + (P(None, "dp", None), P(None, "dp", "seq", None, None), P(None, "dp", None), wide),
        out_specs=(wide, wide, row, vec, vec, row, vec, vec, vec, row, vec, row, vec, vec, vec),
        check_vma=False,
    )
```

```python
import jax
import jax.numpy as jnp
from jax import lax
from jax.experimental import pallas as pl
from jax.experimental.pallas import tpu as pltpu
from jax.sharding import PartitionSpec as P

HD = 64
BLOCK = 64
EPSILON = 1e-06
BIG = float(2.0**100)
LOWEST = -3.0e38
TQ = 256
TK = 512
CHIPS = 16
TILE = 512
SUB = 256
BF = jnp.bfloat16
F32 = jnp.float32
VMEM_LIMIT = 60 << 20
COST = 1.0
CUT = 320
BACK_CUT = 224
EARLY = (160, 288)


def nn(left, right):
    return lax.dot_general(left, right, (((1,), (0,)), ((), ())), preferred_element_type=F32)


def nt(left, right):
    return lax.dot_general(left, right, (((1,), (1,)), ((), ())), preferred_element_type=F32)


def tn(left, right):
    return lax.dot_general(left, right, (((0,), (0,)), ((), ())), preferred_element_type=F32)


def smem():
    return pl.BlockSpec(memory_space=pltpu.SMEM)


def anywhere():
    return pl.BlockSpec(memory_space=pl.ANY)


def cost(flops, bytes_accessed, transcendentals):
    part = lambda value: int(value * COST)
    return pl.CostEstimate(flops=part(flops), bytes_accessed=part(bytes_accessed), transcendentals=part(transcendentals))


def shape(dims, kind):
    return jax.ShapeDtypeStruct(dims, kind)


def after(value, *ready):
    if not ready:
        return value
    return lax.optimization_barrier((value,) + ready)[0]


def swap(value, dim):
    if dim == "x":
        return lax.ppermute(value, "dp", [(d, d ^ 1) for d in range(lax.axis_size("dp"))])
    if dim == "xy":
        pairs = [(4 * d + s, 4 * (d ^ 1) + (s ^ 2)) for d in range(lax.axis_size("dp")) for s in range(4)]
        return lax.ppermute(value, ("dp", "seq"), pairs)
    bit = 1 if dim == "core" else 2
    return lax.ppermute(value, "seq", [(s, s ^ bit) for s in range(4)])


def shift_z(value, by):
    size = lax.axis_size("dp") // 2
    return lax.ppermute(value, "dp", [(2 * z + x, (z + by) % size * 2 + x) for z in range(size) for x in range(2)])


ZS = 4


def stage(*values):
    return lax.optimization_barrier(values)


def shifts_z(chunk, *by):
    return [shift_z(chunk, k) for k in by]


def scatter_z(total, *by):
    return [shift_z(total[r], ZS - r) for r in by]


def split_rows(value, cut):
    return value[:, cut:], value[:, :cut]


def added(*values):
    return sum(v.astype(F32) for v in values)


def add(*values):
    return added(*values).astype(BF)


def chip_at(order, near, index, here):
    z = lax.rem(here["z"] - index % ZS + ZS, ZS)
    near = {order[0]: near[0], order[1]: near[1]}
    return z * 4 + lax.rem(here["x"] + near["x"], 2) * 2 + lax.rem(here["y"] + near["y"], 2)


def placed(meta):
    return {"c": meta[0], "x": meta[1], "y": meta[2], "z": meta[3]}


class Plan:
    def __init__(self, sections, cut, joined=False, plain=False):
        self.sections, self.cut, self.joined, self.plain = sections, cut, joined, plain
        self.rows = sum(sections)

    def pieces(self):
        if self.cut is None:
            return [(0, self.rows, None, [None] * CHIPS)]
        if self.plain:
            return [(0, self.rows, "xy", [sides] * ZS) for sides in ((0, 0), (1, 0), (0, 1), (1, 1))]
        found = []
        if not self.joined:
            found.append((0, self.rows, "xy", [(0, 0)] * ZS))
        for first, end, order in ((self.cut, self.rows, "xy"), (0, self.cut, "yx")):
            if self.joined:
                found += [(first, end, order, [(m // ZS, last) for m in range(2 * ZS)]) for last in range(2)]
            else:
                found += [(first, end, order, [sides] * ZS) for sides in ((1, 0), (0, 1), (1, 1))]
        return found

    def shapes(self, width):
        return [shape((len(sides), end - first, width), BF) for first, end, _, sides in self.pieces()]

    def walk(self, here):
        for piece, (first, end, order, sides) in enumerate(self.pieces()):
            for m, side in enumerate(sides):
                chip = m if side is None else chip_at(order, side, m, here)
                start = 0
                for number, length in enumerate(self.sections):
                    lo, hi = max(start, first), min(start + length, end)
                    if lo < hi:
                        yield piece, m, lo - first, hi - first, chip, number, lo - start
                    start += length

    def entries(self):
        return sum(1 for _ in self.walk({"c": 0, "x": 0, "y": 0, "z": 0}))


def move(plan, here, pieces, target, sems, base, numbers=None, back=False):
    copies = []
    for i, (p, m, lo, hi, chip, number, at) in enumerate(plan.walk(here)):
        if numbers is None or number in numbers:
            near, far = pieces[p].at[m, lo:hi, :], target(number, chip, slice(at, at + hi - lo))
            if back:
                near, far = far, near
            copies.append(pltpu.make_async_copy(near, far, sems.at[base + i]))
    return copies


def run(copies):
    for copy in copies:
        copy.start()
    for copy in copies:
        copy.wait()


def spread_vectors(rows, first, second, marks, hidden_marks):
    count = rows.shape[0]
    number = lax.broadcasted_iota(jnp.int32, (9 * CHIPS, count), 0)
    entry = lax.broadcasted_iota(jnp.int32, (9 * CHIPS, count), 1)
    picker = (entry == lax.rem(number, CHIPS) * 16 + number // CHIPS).astype(F32).astype(BF)
    picked = nn(picker, rows).astype(BF)
    model = first.shape[1]
    vectors = nn(picked[: 8 * CHIPS], first).reshape(8, CHIPS, model) * marks[None]
    hidden = nn(picked[8 * CHIPS :], second).reshape(4, 4, model) * hidden_marks[None]
    return jnp.sum(vectors, axis=1), jnp.sum(hidden, axis=1)


def spread_tables(model, share, share_f, *ready):
    lane, col = jnp.arange(384)[:, None], jnp.arange(model)[None, :]
    if ready:
        lane, col = after(lane, *ready), after(col, *ready)
    first = (lane == 128 * (col // share % 2) + col % share).astype(BF)
    second = (lane == 128 * (col // share_f % 2) + col % share_f).astype(BF)
    marks = (jnp.arange(CHIPS)[:, None] == col // (2 * share)).astype(F32)
    hidden_marks = (jnp.arange(4)[:, None] == col // (2 * share_f)).astype(F32)
    return first, second, marks, hidden_marks


def pack_kernel(meta, qkv_ref, proj_ref, inner_ref, down_ref, mine_ref, theirs_ref):
    model = proj_ref.shape[1]
    half, share = model // 2, proj_ref.shape[0]
    for rel, out in ((0, mine_ref), (1, theirs_ref)):
        h = lax.rem(meta[0] + rel, 2)
        lanes = lambda first, n: pl.ds(pl.multiple_of(first, 128), n)
        at = 0
        for p in range(half // 128):
            for w in range(3):
                out[at : at + share, 128 * w : 128 * w + 128] = qkv_ref[:, lanes(model * w + half * h + 128 * p, 128)]
            at += share
        out[at : at + share, :] = proj_ref[:, lanes(half * h, half)]
        at += share
        for g in range(inner_ref.shape[1] // 2 // half):
            out[at : at + share, :] = inner_ref[:, lanes(inner_ref.shape[1] // 2 * h + half * g, half)]
            at += share
        out[at : at + down_ref.shape[0], :] = down_ref[:, lanes(half * h, half)]


def pack(meta, qkv, proj, inner, down):
    half = proj.shape[1] // 2
    rows = proj.shape[0] * (half // 128 + 1 + inner.shape[1] // 2 // half) + down.shape[0]
    return pl.pallas_call(
        pack_kernel,
        in_specs=[smem()] + [pl.BlockSpec(memory_space=pltpu.VMEM)] * 4,
        out_specs=[pl.BlockSpec(memory_space=pltpu.VMEM)] * 2,
        out_shape=[shape((rows, half), BF)] * 2,
        cost_estimate=cost(flops=0, bytes_accessed=8 * rows * half, transcendentals=0),
        name="pack",
    )(meta, qkv, proj, inner, down)


def lay_kernel(lengths_a, lengths_b, meta, mine_ref, came_ref, small_ref, small_came, a_ref, b_ref, all_ref):
    even = meta[0] == 0
    order = lambda mine, came: (jnp.where(even, mine, came), jnp.where(even, came, mine))
    at = 0
    for lengths, out in ((lengths_a, a_ref), (lengths_b, b_ref)):
        to = 0
        for length in lengths:
            for part in order(mine_ref[at : at + length, :], came_ref[at : at + length, :]):
                out[to : to + length, :] = part
                to += length
            at += length
    small = jnp.concatenate(order(small_ref[...], small_came[...]) + (jnp.zeros(small_ref.shape, BF),), axis=1)
    a_ref[a_ref.shape[0] - small.shape[0] :, :] = small
    all_ref[: a_ref.shape[0], :] = a_ref[...]
    all_ref[a_ref.shape[0] :, :] = b_ref[...]


def lay(meta, mine, came, small, small_came, lengths_a, lengths_b):
    width = mine.shape[1]
    rows = 2 * sum(lengths_a) + small.shape[0], 2 * sum(lengths_b)
    return pl.pallas_call(
        lambda *refs: lay_kernel(lengths_a, lengths_b, *refs),
        in_specs=[smem()] + [pl.BlockSpec(memory_space=pltpu.VMEM)] * 4,
        out_specs=[pl.BlockSpec(memory_space=pltpu.VMEM)] * 3,
        out_shape=[shape((n, width), BF) for n in (*rows, sum(rows))],
        cost_estimate=cost(flops=0, bytes_accessed=8 * sum(rows) * width, transcendentals=0),
        name="lay",
    )(meta, mine, came, small, small_came)


def qkv_kernel(plan, pieces_n, *refs):
    meta = refs[0]
    pieces = refs[1 : 1 + pieces_n]
    own_ref, oth_ref, first, second, marks, hidden_marks, out_ref, w_ref, vec_ref, rows_ref, bias_ref, sems = refs[1 + pieces_n :]
    here = placed(meta)
    wide = out_ref.shape[1]
    third = wide // 3

    @pl.when(pl.program_id(0) == 0)
    def _():
        def target(number, chip, rows):
            if number == 3:
                return rows_ref.at[chip, rows, :]
            return w_ref.at[chip, rows, third * number : third * number + third]

        run(move(plan, here, pieces, target, sems, 0))
        rows = rows_ref[...].reshape(CHIPS * 16, 384)
        vectors, hidden = spread_vectors(rows, first[...], second[...], marks[...], hidden_marks[...])
        vec_ref[0:8, :] = vectors
        vec_ref[8:12, :] = hidden
        vec_ref[12:16, :] = jnp.zeros_like(hidden)
        mine = jnp.where(here["c"] == 0, vectors[:, :third], vectors[:, third:])
        bias_ref[...] = jnp.zeros_like(bias_ref)
        for p in range(3):
            for w, source in ((0, 0), (2, 1)):
                at = third * p + 128 * w
                bias_ref[0:1, at : at + 128] = mine[source : source + 1, 128 * p : 128 * p + 128]

    weight = w_ref[...].reshape(-1, wide)
    x = jnp.where(pl.program_id(0) < 2, own_ref[...], oth_ref[...])
    out_ref[...] = (nn(x, weight) + bias_ref[0:1, :]).astype(BF)


def project_qkv(plan, meta, pieces, x_own, x_oth, tables):
    _, tile, model = x_own.shape
    rows = 4 * tile
    width, depth = model // 2, model // CHIPS
    wide = 3 * width
    full = lambda dims: pl.BlockSpec(dims, lambda i, meta: (0,) * len(dims))
    return pl.pallas_call(
        lambda *refs: qkv_kernel(plan, len(pieces), *refs),
        grid_spec=pltpu.PrefetchScalarGridSpec(
            num_scalar_prefetch=1,
            grid=(4,),
            in_specs=[anywhere()] * len(pieces)
            + [pl.BlockSpec((None, tile, model), lambda i, meta: (jnp.minimum(i, 1), 0, 0))]
            + [pl.BlockSpec((None, tile, model), lambda i, meta: (jnp.maximum(i - 2, 0), 0, 0))]
            + [full(t.shape) for t in tables],
            out_specs=[
                pl.BlockSpec((tile, wide), lambda i, meta: (2 * lax.rem(i, 2) + lax.rem(meta[0] + i // 2, 2), 0)),
                full((CHIPS, depth, wide)),
                full((16, model)),
            ],
            scratch_shapes=[
                pltpu.VMEM((CHIPS, 16, width), BF),
                pltpu.VMEM((8, wide), F32),
                pltpu.SemaphoreType.DMA((plan.entries(),)),
            ],
        ),
        out_shape=[shape((rows, wide), BF), shape((CHIPS, depth, wide), BF), shape((16, model), F32)],
        compiler_params=pltpu.CompilerParams(vmem_limit_bytes=14 << 20),
        cost_estimate=cost(
            flops=2 * rows * model * wide, bytes_accessed=2 * rows * (model + wide), transcendentals=0
        ),
        name="project_qkv",
    )(meta, *pieces, x_own, x_oth, *tables)


def fill_features(seg_ref, rand_ref, first_global, second_global, key_ref, query_ref):
    heads, _, length = key_ref.shape
    blocks = length // BLOCK
    at = lax.broadcasted_iota(jnp.int32, (blocks, length), 1) // BLOCK
    row = lax.broadcasted_iota(jnp.int32, (blocks, length), 0)
    seen = jnp.abs(at - row) <= 1
    for chosen in (first_global, second_global):
        seen = seen | (at == chosen) | (row == chosen)
    same = lax.broadcasted_iota(jnp.int32, (HD - blocks, length), 0) == seg_ref[...]
    for h in range(heads):
        picked = seen
        for r in range(rand_ref.shape[2]):
            picked = picked | (at == rand_ref[h, :, r : r + 1])
        key_ref[h, 0:blocks, :] = jnp.where(picked, 0.0, 1.0).astype(BF)
        key_ref[h, blocks:HD, :] = jnp.where(same, 0.0, 1.0).astype(BF)
    query_ref[0:blocks, :] = jnp.where(at == row, -BIG, 0.0).astype(BF)
    query_ref[blocks:HD, :] = jnp.where(same, -BIG, 0.0).astype(BF)


def of_pair(ref, p, w):
    return ref[:, 384 * p + 128 * w : 384 * p + 128 * w + 128]


def widen_pair(p, qkv_ref, key_feat, query_feat, key_wide, query_wide):
    scaled = of_pair(qkv_ref, p, 0) * BF(HD**-0.5)
    queries, keys = scaled.T, of_pair(qkv_ref, p, 1).T
    a, b = 2 * p, 2 * p + 1
    query_wide[a, 0:HD, :] = queries[0:HD]
    query_wide[a, HD:128, :] = query_feat[...]
    query_wide[b, 0:HD, :] = query_feat[...]
    query_wide[b, HD:128, :] = queries[HD:128]
    key_wide[a] = jnp.concatenate([keys[0:HD], key_feat[a]], axis=0).T
    key_wide[b] = jnp.concatenate([key_feat[b], keys[HD:128]], axis=0).T
    return scaled, keys


def over_keys(start, n, step, carry):
    carry = lax.fori_loop(0, n // 2, lambda j, carry: step(start + j * TK, j * TK, TK, carry), carry)
    done = n // 2 * TK
    return lax.fori_loop(0, lax.rem(n, 2), lambda j, carry: step(start + done, done, TK // 2, carry), carry)


def attend_kernel(meta, lo_ref, n_ref, glob_ref, qkv_ref, seg_ref, rand_ref, own_ref, oth_ref, lse_ref,
                  key_feat, query_feat, key_wide, query_wide, values, turned, store):
    heads, length = lse_ref.shape
    fill_features(seg_ref, rand_ref, glob_ref[0], glob_ref[1], key_feat, query_feat)
    for p in range(heads // 2):
        widen_pair(p, qkv_ref, key_feat, query_feat, key_wide, query_wide)
        values[128 * p : 128 * p + 128, :] = of_pair(qkv_ref, p, 2).T

    def tile(i, _):
        qs = pl.ds(pl.multiple_of(i * TQ, TQ), TQ)

        def scan(start, at, size, tops):
            ks = pl.ds(pl.multiple_of(start, 128), size)
            to = pl.ds(pl.multiple_of(at, TK), size)
            raised = []
            for h in range(heads):
                scores = nn(key_wide[h, ks, :], query_wide[h, :, qs])
                store[h, to, :] = scores
                raised.append(jnp.maximum(tops[h], jnp.max(scores.reshape(size // 8, 8, TQ), axis=0)))
            return tuple(raised)

        tops = over_keys(lo_ref[i], n_ref[i], scan, (jnp.full((8, TQ), LOWEST, F32),) * heads)
        tops = [jnp.max(top, axis=0, keepdims=True) for top in tops]

        def collect(start, at, size, carry):
            ks = pl.ds(pl.multiple_of(start, 128), size)
            to = pl.ds(pl.multiple_of(at, TK), size)
            new = []
            for h in range(heads):
                total, summed = carry[h]
                expo = jnp.exp(store[h, to, :] - tops[h])
                total = total + jnp.sum(expo.reshape(size // 8, 8, TQ), axis=0)
                summed = summed + nn(values[HD * h : HD * h + HD, ks], expo.astype(BF))
                new.append((total, summed))
            return tuple(new)

        none = (jnp.zeros((8, TQ), F32), jnp.zeros((HD, TQ), F32))
        found = over_keys(lo_ref[i], n_ref[i], collect, (none,) * heads)
        for h in range(heads):
            total, summed = found[h]
            total = jnp.sum(total, axis=0, keepdims=True)
            turned[HD * h : HD * h + HD, qs] = (summed / total).astype(BF)
            lse_ref[h : h + 1, qs] = tops[h] + jnp.log(total)
        return 0

    lax.fori_loop(0, length // TQ, tile, 0)
    quarter = length // 4
    even = meta[0] == 0
    for p in range(heads // 2):
        result = turned[128 * p : 128 * p + 128, :].T
        for n in range(2):
            one, two = (result[quarter * k : quarter * k + quarter] for k in (2 * n, 2 * n + 1))
            where = (slice(quarter * n, quarter * n + quarter), slice(128 * p, 128 * p + 128))
            own_ref[where] = jnp.where(even, one, two)
            oth_ref[where] = jnp.where(even, two, one)


def whole(dims):
    return pl.BlockSpec(dims, lambda *_: (0,) * len(dims))


def attend(meta, qkv, number, seg_row, table, globs, lo, n):
    length = qkv.shape[0]
    heads, blocks = table.shape[:2]
    wide = heads * HD
    return pl.pallas_call(
        attend_kernel,
        grid=(1,),
        in_specs=[smem()] * 4
        + [pl.BlockSpec((length, 3 * wide), lambda i: (0, number)), whole((1, length)), whole((heads, blocks, 3))],
        out_specs=[whole((length // 2, wide))] * 2 + [whole((heads, length))],
        out_shape=[shape((length // 2, wide), BF)] * 2 + [shape((heads, length), F32)],
        scratch_shapes=[
            pltpu.VMEM((heads, HD, length), BF),
            pltpu.VMEM((HD, length), BF),
            pltpu.VMEM((heads, length, 128), BF),
            pltpu.VMEM((heads, 128, length), BF),
            pltpu.VMEM((wide, length), BF),
            pltpu.VMEM((wide, length), BF),
            pltpu.VMEM((heads, length, TQ), F32),
        ],
        compiler_params=pltpu.CompilerParams(vmem_limit_bytes=28 << 20),
        cost_estimate=cost(
            flops=heads * length * length * 700, bytes_accessed=10 * length * wide, transcendentals=heads * length * length // 2
        ),
        name="attend",
    )(meta, lo, n, globs, qkv, seg_row, table)


def attend_back_kernel(meta, lo_ref, n_ref, glob_ref, qkv_ref, own_ref, oth_ref, ctx_own, ctx_oth, lse_ref, seg_ref,
                       rand_ref, out_ref, key_feat, query_feat, key_wide, query_wide, value_one,
                       grad_turned, keys_turned, query_one, grad_one, inner_ref, dk, dv, dqt, grads):
    heads, length = lse_ref.shape
    quarter = length // 4
    fill_features(seg_ref, rand_ref, glob_ref[0], glob_ref[1], key_feat, query_feat)
    for rel, source, ctx in ((0, own_ref, ctx_own), (1, oth_ref, ctx_oth)):
        for n in range(2):
            at = 2 * n + lax.rem(meta[0] + rel, 2)
            rows = pl.ds(pl.multiple_of(at * quarter, quarter), quarter)
            grads[0, rows, :] = source[quarter * n : quarter * n + quarter, :]
            grads[1, rows, :] = ctx[quarter * n : quarter * n + quarter, :]
    low = lax.broadcasted_iota(jnp.int32, (length, 128), 1) < HD
    zero = jnp.zeros((length, 128), BF)
    for p in range(heads // 2):
        cols = slice(128 * p, 128 * p + 128)
        scaled, keys = widen_pair(p, qkv_ref, key_feat, query_feat, key_wide, query_wide)
        keys_turned[cols, :] = keys
        grad, value = grads[0, :, cols], of_pair(qkv_ref, p, 2)
        for e in range(2):
            keep = low if e == 0 else ~low
            value_one[2 * p + e] = jnp.where(keep, value, zero)
            query_one[2 * p + e] = jnp.where(keep, scaled, zero)
            grad_one[2 * p + e] = jnp.where(keep, grad, zero)
        turned = grad.T
        grad_turned[cols, :] = turned
        product = turned.astype(F32) * grads[1, :, cols].T.astype(F32)
        for e in range(2):
            h = 2 * p + e
            inner_ref[h : h + 1, :] = jnp.sum(product[HD * e : HD * e + HD], axis=0, keepdims=True)
    dk[...] = jnp.zeros_like(dk)
    dv[...] = jnp.zeros_like(dv)

    def tile(i, _):
        qs = pl.ds(pl.multiple_of(i * TQ, TQ), TQ)

        def body(start, at, size, carry):
            ks = pl.ds(pl.multiple_of(start, 128), size)
            new = []
            for p in range(heads // 2):
                cols = slice(128 * p, 128 * p + 128)
                more_k, more_v = [], []
                for h in (2 * p, 2 * p + 1):
                    scores = nn(key_wide[h, ks, :], query_wide[h, :, qs])
                    prob = jnp.exp(scores - lse_ref[h : h + 1, qs])
                    grad_prob = nn(value_one[h, ks, :], grad_turned[cols, qs])
                    grad_scores = (prob * (grad_prob - inner_ref[h : h + 1, qs])).astype(BF)
                    new.append(carry[h] + nn(keys_turned[HD * h : HD * h + HD, ks], grad_scores))
                    more_k.append(nn(grad_scores, query_one[h, qs, :]))
                    more_v.append(nn(prob.astype(BF), grad_one[h, qs, :]))
                dk[ks, cols] += more_k[0] + more_k[1]
                dv[ks, cols] += more_v[0] + more_v[1]
            return tuple(new)

        found = over_keys(lo_ref[i], n_ref[i], body, (jnp.zeros((HD, TQ), F32),) * heads)
        for h in range(heads):
            dqt[HD * h : HD * h + HD, qs] = (found[h] * HD**-0.5).astype(BF)
        return 0

    lax.fori_loop(0, length // TQ, tile, 0)
    for p in range(heads // 2):
        cols = slice(128 * p, 128 * p + 128)
        for w, value in enumerate((dqt[cols, :].T, dk[:, cols].astype(BF), dv[:, cols].astype(BF))):
            out_ref[:, 384 * p + 128 * w : 384 * p + 128 * w + 128] = value


def attend_back(meta, qkv, number, own, oth, ctx, ctx_oth, lse, part, seg_row, table, globs, lo, n):
    length = qkv.shape[0]
    heads, blocks = table.shape[:2]
    wide = heads * HD
    group = lambda w, i=number: pl.BlockSpec((length, w), lambda _: (0, i))
    half = pl.BlockSpec((length // 2, wide), lambda _: (0, number))
    return pl.pallas_call(
        attend_back_kernel,
        grid=(1,),
        in_specs=[smem()] * 4
        + [group(3 * wide), half, half]
        + [pl.BlockSpec((length // 2, wide), lambda _: (0, part))] * 2
        + [whole((heads, length)), whole((1, length)), whole((heads, blocks, 3))],
        out_specs=whole((length, 3 * wide)),
        out_shape=shape((length, 3 * wide), BF),
        scratch_shapes=[
            pltpu.VMEM((heads, HD, length), BF),
            pltpu.VMEM((HD, length), BF),
            pltpu.VMEM((heads, length, 128), BF),
            pltpu.VMEM((heads, 128, length), BF),
            pltpu.VMEM((heads, length, 128), BF),
            pltpu.VMEM((wide, length), BF),
            pltpu.VMEM((wide, length), BF),
            pltpu.VMEM((heads, length, 128), BF),
            pltpu.VMEM((heads, length, 128), BF),
            pltpu.VMEM((heads, length), F32),
            pltpu.VMEM((length, wide), F32),
            pltpu.VMEM((length, wide), F32),
            pltpu.VMEM((wide, length), BF),
            pltpu.VMEM((2, length, wide), BF),
        ],
        compiler_params=pltpu.CompilerParams(vmem_limit_bytes=17 << 20),
        cost_estimate=cost(
            flops=heads * length * length * 1500, bytes_accessed=20 * length * wide, transcendentals=heads * length * length // 2
        ),
        name="attend_back",
    )(meta, lo, n, globs, qkv, own, oth, ctx, ctx_oth, lse, seg_row, table)


def key_ranges(segment):
    length = segment.shape[0]
    first, last = segment[::TQ], segment[TQ - 1 :: TQ]
    lo = jnp.sum(segment[None, :] < first[:, None], axis=1, dtype=jnp.int32) // 128 * 128
    hi = jnp.sum(segment[None, :] <= last[:, None], axis=1, dtype=jnp.int32)
    n = (hi - lo + TK // 2 - 1) // (TK // 2)
    return jnp.minimum(lo, length - n * (TK // 2)), n


def centre(value):
    centred = value - jnp.mean(value, axis=1, keepdims=True)
    rate = lax.rsqrt(jnp.mean(centred * centred, axis=1, keepdims=True) + EPSILON)
    return centred * rate, rate


def norm_back(grad, normed, rate):
    return rate * (
        grad
        - jnp.mean(grad, axis=1, keepdims=True)
        - normed * jnp.mean(grad * normed, axis=1, keepdims=True)
    )


def cut(value):
    half = value.shape[1] // 2
    return value[:, :half], value[:, half:]


def wide_target(proj, inner, down, half):
    width = proj.shape[2] // 2
    groups = inner.shape[2] // 2 // width

    def target(number, chip, rows):
        if number == 0:
            return proj.at[chip, rows, pl.ds(pl.multiple_of(half * width, 128), width)]
        if number <= groups:
            first = half * (groups * width) + width * (number - 1)
            return inner.at[chip, rows, pl.ds(pl.multiple_of(first, 128), width)]
        return down.at[chip, rows, pl.ds(pl.multiple_of(half * width, 128), width)]

    return target


def ffn_kernel(plan, pieces_n, ctx_n, *refs):
    meta = refs[0]
    own_pieces = refs[1 : 1 + pieces_n]
    oth_pieces = refs[1 + pieces_n : 1 + 2 * pieces_n]
    refs = refs[1 + 2 * pieces_n :]
    ctx_own, ctx_oth = refs[:ctx_n], refs[ctx_n : 2 * ctx_n]
    (x_ref, dout_ref, vec_ref,
     out_ref, gr_ref, hid_ref, gf_ref, low_ref, gp_ref, ga_ref, gc_own, gc_oth, ctx_ref, vg_ref,
     proj, inner, down, slope, sems) = refs[2 * ctx_n :]
    here = placed(meta)
    c = here["c"]
    step = pl.program_id(0)
    model = x_ref.shape[1]
    wide = hid_ref.shape[1]

    def copies(*numbers):
        found = []
        for rel, pieces in ((0, own_pieces), (1, oth_pieces)):
            target = wide_target(proj, inner, down, lax.rem(c + rel, 2))
            found += move(plan, here, pieces, target, sems, rel * plan.entries(), numbers)
        return found

    first, last = 0, len(plan.sections) - 1
    orders = [(first,), tuple(range(1, last)), (last,)]

    @pl.when(step == 0)
    def _():
        for numbers in orders:
            for copy in copies(*numbers):
                copy.start()
        vg_ref[...] = jnp.zeros_like(vg_ref)

    def arrived(which):
        @pl.when(step == 0)
        def _():
            for copy in copies(*orders[which]):
                copy.wait()

    vec = lambda n: vec_ref[n : n + 1, :]
    w_proj = lambda: proj[...].reshape(model, model)
    w_inner = lambda j: inner[:, :, model * j : model * j + model].reshape(model, model)
    span = CHIPS * model // wide
    w_down = lambda j: down[span * j : span * j + span].reshape(model, model)
    total = lambda value: jnp.sum(value, axis=0, keepdims=True)
    chunks = wide // model
    spans = [slice(at, at + SUB) for at in range(0, TILE, SUB)]
    columns = [slice(model * j, model * j + model) for j in range(chunks)]

    arrived(0)
    first = []
    for rows in spans:
        own = jnp.concatenate([ref[rows, :] for ref in ctx_own], axis=1)
        oth = jnp.concatenate([ref[rows, :] for ref in ctx_oth], axis=1)
        context = jnp.concatenate([jnp.where(c == 0, own, oth), jnp.where(c == 0, oth, own)], axis=1)
        ctx_ref[rows, :] = context
        n1, rate1 = centre(x_ref[rows, :].astype(F32) + (nn(context, w_proj()) + vec(2)))
        x1 = n1 * vec(3) + vec(4)
        low = x1.astype(BF)
        low_ref[rows, :] = low
        first.append((n1, rate1, x1, low))
    arrived(1)
    arrived(2)
    ffn = [None] * len(spans)
    for j, cols in enumerate(columns):
        for k, rows in enumerate(spans):
            pre = nn(first[k][3], w_inner(j)) + vec(8 + j)
            below = 0.5 + 0.5 * lax.erf(pre * 0.7071067811865476)
            slope[rows, cols] = below + pre * (jnp.exp(-0.5 * (pre * pre)) * 0.3989422804014327)
            hidden = (pre * below).astype(BF)
            hid_ref[rows, cols] = hidden
            more = nn(hidden, w_down(j))
            ffn[k] = more if ffn[k] is None else ffn[k] + more
    second = []
    for k, rows in enumerate(spans):
        n2, rate2 = centre(first[k][2] + (ffn[k] + vec(5)))
        out_ref[rows, :] = (n2 * vec(6) + vec(7)).astype(BF)
        grad = dout_ref[rows, :].astype(F32)
        gr2 = norm_back(grad * vec(6), n2, rate2)
        gf = gr2.astype(BF)
        gf_ref[rows, :] = gf
        vg_ref[6:7, :] += total(grad * n2)
        vg_ref[7:8, :] += total(grad)
        vg_ref[5:6, :] += total(gf.astype(F32))
        second.append([gr2, gf])
    for j, cols in enumerate(columns):
        for k, rows in enumerate(spans):
            gp = (nt(second[k][1], w_down(j)) * slope[rows, cols]).astype(BF)
            gp_ref[rows, cols] = gp
            vg_ref[8 + j : 9 + j, :] += total(gp.astype(F32))
            second[k][0] = second[k][0] + nt(gp, w_inner(j))
    for k, rows in enumerate(spans):
        n1, rate1, gx1 = first[k][0], first[k][1], second[k][0]
        gr1 = norm_back(gx1 * vec(3), n1, rate1)
        gr_ref[rows, :] = gr1
        ga = gr1.astype(BF)
        ga_ref[rows, :] = ga
        vg_ref[3:4, :] += total(gx1 * n1)
        vg_ref[4:5, :] += total(gx1)
        vg_ref[2:3, :] += total(ga.astype(F32))
        gc = cut(nt(ga, w_proj()))
        gc_own[rows, :] = jnp.where(c == 0, gc[0], gc[1]).astype(BF)
        gc_oth[rows, :] = jnp.where(c == 0, gc[1], gc[0]).astype(BF)


def feed_forward(plan, meta, own_pieces, oth_pieces, ctx, ctx_oth, x_own, d_own, vectors, wide):
    rows, model = x_own.shape
    half = model // 2
    tile = lambda n: pl.BlockSpec((TILE, n), lambda i, meta: (i, 0))
    full = lambda dims: pl.BlockSpec(dims, lambda i, meta: (0,) * len(dims))
    per = rows // 2 // TILE
    side = pl.BlockSpec((None, TILE, model), lambda i, meta: (lax.rem(i // per + meta[2], 2), lax.rem(i, per), 0))
    scratch = [
        pltpu.VMEM((CHIPS, model // CHIPS, model), BF),
        pltpu.VMEM((CHIPS, model // CHIPS, wide), BF),
        pltpu.VMEM((CHIPS, wide // CHIPS, model), BF),
        pltpu.VMEM((TILE, wide), F32),
        pltpu.SemaphoreType.DMA((2 * plan.entries(),)),
    ]
    outs = [(wide, BF), (model, BF), (model, BF), (wide, BF), (model, BF), (half, BF), (half, BF), (model, BF)]
    return pl.pallas_call(
        lambda *refs: ffn_kernel(plan, len(own_pieces), len(ctx), *refs),
        grid_spec=pltpu.PrefetchScalarGridSpec(
            num_scalar_prefetch=1,
            grid=(rows // TILE,),
            in_specs=[anywhere()] * (2 * len(own_pieces))
            + [tile(v.shape[1]) for v in ctx + ctx_oth]
            + [tile(model), tile(model), full(vectors.shape)],
            out_specs=[side] * 2 + [tile(w) for w, _ in outs] + [full((16, model))],
            scratch_shapes=scratch,
        ),
        out_shape=[shape((2, rows // 2, model), kind) for kind in (BF, F32)] + [shape((rows, w), kind) for w, kind in outs] + [shape((16, model), F32)],
        compiler_params=pltpu.CompilerParams(vmem_limit_bytes=VMEM_LIMIT),
        cost_estimate=cost(
            flops=4 * rows * model * (model + 2 * wide), bytes_accessed=rows * (8 * wide + 20 * model), transcendentals=2 * rows * wide
        ),
        name="feed_forward",
    )(meta, *own_pieces, *oth_pieces, *ctx, *ctx_oth, x_own, d_own, vectors)


def weight_grads_kernel(plan, pieces_n, *refs):
    meta, hid_ref, gp_ref, gf_ref, low_ref, ctx_ref, ga_ref = refs[:7]
    own_pieces = refs[7 : 7 + pieces_n]
    oth_pieces = refs[7 + pieces_n : 7 + 2 * pieces_n]
    proj, inner, down, sems = refs[7 + 2 * pieces_n :]
    here = placed(meta)
    c = here["c"]
    step = pl.program_id(0)
    model = gf_ref.shape[1]
    span = CHIPS * model // inner.shape[2]
    steps = inner.shape[2] // model

    @pl.when(step == 0)
    def _():
        proj[...] = tn(ctx_ref[...], ga_ref[...]).reshape(proj.shape).astype(BF)

    more_inner = tn(low_ref[...], gp_ref[...])
    inner[:, :, pl.ds(pl.multiple_of(step * model, 128), model)] = more_inner.reshape(CHIPS, -1, model).astype(BF)
    more_down = tn(hid_ref[...], gf_ref[...])
    down[pl.ds(step * span, span)] = more_down.reshape(span, -1, model).astype(BF)

    @pl.when(step == steps - 1)
    def _():
        copies = []
        for rel, pieces in ((0, own_pieces), (1, oth_pieces)):
            target = wide_target(proj, inner, down, lax.rem(c + rel, 2))
            copies += move(plan, here, pieces, target, sems, len(copies), back=True)
        run(copies)


def weight_grads(plan, meta, hid, gp, gf, low, context, ga):
    rows, model = gf.shape
    wide, half = hid.shape[1], model // 2
    pieces = plan.shapes(half)
    cols = pl.BlockSpec((rows, model), lambda i: (0, i))
    found = pl.pallas_call(
        lambda *refs: weight_grads_kernel(plan, len(pieces), *refs),
        grid=(wide // model,),
        in_specs=[smem(), cols, cols] + [whole((rows, model))] * 4,
        out_specs=[anywhere()] * (2 * len(pieces)),
        out_shape=pieces * 2,
        scratch_shapes=[
            pltpu.VMEM((CHIPS, model // CHIPS, model), BF),
            pltpu.VMEM((CHIPS, model // CHIPS, wide), BF),
            pltpu.VMEM((CHIPS, wide // CHIPS, model), BF),
            pltpu.SemaphoreType.DMA((2 * plan.entries(),)),
        ],
        compiler_params=pltpu.CompilerParams(vmem_limit_bytes=VMEM_LIMIT),
        cost_estimate=cost(
            flops=2 * rows * model * (model + 2 * wide), bytes_accessed=rows * (4 * wide + 8 * model), transcendentals=0
        ),
        name="weight_grads",
    )(meta, hid, gp, gf, low, context, ga)
    return found[: len(pieces)], found[len(pieces) :]


def gather_vectors(vectors, hidden, first, second, marks, hidden_marks):
    model = first.shape[1]
    one = nt((vectors[:, None, :] * marks[None]).reshape(-1, model).astype(BF), first)
    two = nt((hidden[:, None, :] * hidden_marks[None]).reshape(-1, model).astype(BF), second)
    laid = jnp.concatenate([one, two], axis=0).astype(BF)
    number = lax.broadcasted_iota(jnp.int32, (9 * CHIPS, 16 * CHIPS), 0)
    entry = lax.broadcasted_iota(jnp.int32, (9 * CHIPS, 16 * CHIPS), 1)
    picker = (entry == lax.rem(number, CHIPS) * 16 + number // CHIPS).astype(F32).astype(BF)
    return tn(picker, laid)


def qkv_grads_kernel(plan, pieces_n, pairs, number, last, *refs):
    meta, own_ref, oth_ref = refs[:3]
    grads = refs[3 : 3 + pairs]
    refs = refs[3 + pairs :]
    if last:
        (known_ref, vg_ref, first, second, marks, hidden_marks), refs = refs[:6], refs[6:]
    pieces, refs = refs[:pieces_n], refs[pieces_n:]
    if last:
        g_ref, sems, rows_ref, vec_ref, sums_ref = refs
    else:
        sums_ref, g_ref, sems = refs
    here = placed(meta)
    quarter, width = own_ref.shape[1], own_ref.shape[2] // 2
    sums_ref[...] = known_ref[...] if last else jnp.zeros_like(sums_ref)
    for p, source in enumerate(grads):
        total = None
        for rel, x_ref in ((0, own_ref), (1, oth_ref)):
            for n in range(2):
                at = 2 * n + lax.rem(here["c"] + rel, 2)
                more = tn(x_ref[n], source[pl.ds(pl.multiple_of(at * quarter, quarter), quarter), :])
                total = more if total is None else total + more
        g_ref[p] = total.reshape(g_ref.shape[1:]).astype(BF)
        sums_ref[number + p : number + p + 1, :] = jnp.sum(source[...].astype(F32), axis=0, keepdims=True)
    if last:
        even = here["c"] == 0
        vec_ref[...] = vg_ref[...]
        none = jnp.zeros((1, 128), F32)
        for p in range(number + pairs):
            for row, w in ((0, 0), (1, 2)):
                value = sums_ref[p : p + 1, 128 * w : 128 * w + 128]
                vec_ref[row : row + 1, 128 * p : 128 * p + 128] = jnp.where(even, value, none)
                at = width + 128 * p
                vec_ref[row : row + 1, at : at + 128] = jnp.where(even, none, value)
        found = gather_vectors(vec_ref[0:8, :], vec_ref[8:12, :], first[...], second[...], marks[...], hidden_marks[...])
        rows_ref[...] = found.reshape(rows_ref.shape).astype(BF)

    def target(section, chip, rows):
        if section == pairs:
            return rows_ref.at[chip, rows, :]
        return g_ref.at[section, chip, rows, :]

    run(move(plan, here, pieces, target, sems, 0, back=True))


def qkv_grads(plan, meta, x_own, x_oth, grads, number, sums=None, vg=None, tables=()):
    rows, model = 4 * x_own.shape[1], x_own.shape[2]
    width, depth = grads[0].shape[1], model // CHIPS
    last = vg is not None
    pieces = plan.shapes(width)
    more = [sums, vg, *tables] if last else []
    summed = shape((8, width), F32)
    found = pl.pallas_call(
        lambda *refs: qkv_grads_kernel(plan, len(pieces), len(grads), number, last, *refs),
        grid=(1,),
        in_specs=[smem(), whole(x_own.shape), whole(x_own.shape)]
        + [whole((rows, width))] * len(grads)
        + [whole(v.shape) for v in more],
        out_specs=[anywhere()] * len(pieces) + ([] if last else [whole(summed.shape)]),
        out_shape=pieces + ([] if last else [summed]),
        scratch_shapes=[
            pltpu.VMEM((len(grads), CHIPS, depth, width), BF),
            pltpu.SemaphoreType.DMA((plan.entries(),)),
        ]
        + ([pltpu.VMEM((CHIPS, 16, width), BF), pltpu.VMEM((16, model), F32), pltpu.VMEM((8, width), F32)] if last else []),
        compiler_params=pltpu.CompilerParams(vmem_limit_bytes=20 << 20),
        cost_estimate=cost(
            flops=2 * len(grads) * rows * model * width, bytes_accessed=2 * rows * (model + 3 * width), transcendentals=0
        ),
        name="qkv_grads",
    )(meta, x_own, x_oth, *grads, *more)
    return found if last else (found[:-1], found[-1])


def input_grads_kernel(meta, *refs):
    *grads, w_ref, own_ref, oth_ref = refs
    width = grads[0].shape[1]
    total = None
    for p, source in enumerate(grads):
        weight = w_ref[:, :, width * p : width * p + width].reshape(-1, width)
        more = nt(source[...], weight)
        total = more if total is None else total + more

    @pl.when(pl.program_id(0) == 0)
    def _():
        oth_ref[...] = total.astype(BF)

    @pl.when(pl.program_id(0) == 1)
    def _():
        own_ref[...] = total.astype(BF)


def input_grads(meta, grads, weights, given):
    rows, width = grads[0].shape
    model = weights.shape[0] * weights.shape[1]
    quarter = rows // 4
    half = lambda meta: 1 - meta[2] if given else meta[2]
    at = lambda i, meta: 2 * half(meta) + lax.rem(meta[0] + 1 + i, 2)
    return pl.pallas_call(
        input_grads_kernel,
        grid_spec=pltpu.PrefetchScalarGridSpec(
            num_scalar_prefetch=1,
            grid=(2,),
            in_specs=[pl.BlockSpec((quarter, width), lambda i, meta: (at(i, meta), 0))] * len(grads) + [whole(weights.shape)],
            out_specs=[whole((quarter, model))] * 2,
        ),
        out_shape=[shape((quarter, model), BF)] * 2,
        compiler_params=pltpu.CompilerParams(vmem_limit_bytes=14 << 20),
        cost_estimate=cost(
            flops=3 * rows * model * width, bytes_accessed=rows * (model + 3 * width), transcendentals=0
        ),
        name="input_grads",
    )(meta, *grads, weights)


def body(
    tokens,
    qkv_weight,
    query_bias,
    value_bias,
    proj_weight,
    proj_bias,
    attn_gain,
    attn_shift,
    inner_weight,
    inner_bias,
    down_weight,
    down_bias,
    ffn_gain,
    ffn_shift,
    seg_ids,
    rand_blocks,
    glob_blocks,
    d_out,
):
    dp, seq = lax.axis_index("dp"), lax.axis_index("seq")
    members = lax.axis_size("dp") * lax.axis_size("seq")
    near = lax.axis_size("dp") == 2 * ZS
    y, c = seq // 2, seq % 2
    even, low_y = c == 0, y == 0
    meta = jnp.stack([c, dp % 2, y, dp // 2]).astype(jnp.int32)
    model = tokens.shape[3]
    half = model // 2
    ffw = inner_weight.shape[1]
    share, share_f = qkv_weight.shape[0], down_weight.shape[0]
    groups = ffw // 2 // half
    depth, deep = model // CHIPS, ffw // CHIPS
    by_parity = lambda mine, other: (jnp.where(even, mine, other), jnp.where(even, other, mine))

    pair = lambda kept, came: jnp.where(low_y, jnp.stack([kept, came]), jnp.stack([came, kept]))

    def given_kept(value):
        return jnp.where(low_y, value[1], value[0]), jnp.where(low_y, value[0], value[1])

    vectors = (query_bias, value_bias, proj_bias, attn_gain, attn_shift, down_bias, ffn_gain, ffn_shift)
    sections_a, sections_b = [depth] * 3 + [16], [depth] * (1 + groups) + [deep]
    lengths_a, lengths_b = [share] * 3, [share] * (1 + groups) + [share_f]
    def documents(seg_ids, glob_blocks):
        segment = jnp.where(low_y, seg_ids[0, 0], seg_ids[1, 0])
        return segment, jnp.where(low_y, glob_blocks[0, 0], glob_blocks[1, 0]), *key_ranges(segment)

    blocks = rand_blocks[:, 0]
    x_given, x_kept = given_kept(tokens[:, 0])

    def pick_blocks(came):
        of_chip = by_parity(blocks, came)
        mine = jnp.where(low_y, *(jnp.concatenate([v[m] for v in of_chip]) for m in range(2)))
        return mine, jnp.where(low_y, *(jnp.concatenate([v[1 - m] for v in of_chip]) for m in range(2)))

    def attention(heads, number, qkv, table):
        return attend(meta, qkv, number, segment[None], table[heads], globs, lo, n)

    def attention_back(p, qkv, own, oth, ctx, ctx_oth, lse, table):
        part = p if p < 2 else 0
        return attend_back(meta, qkv, p, own, oth, ctx, ctx_oth, lse, part, segment[None], table[2 * p : 2 * p + 2], globs, lo, n)

    if near:
        plan_a, plan_b = Plan(sections_a, 80, plain=True), Plan(sections_b, CUT)
        back_b = Plan(sections_b, BACK_CUT, True)
        back_early, back_late = Plan([depth] * 2, depth, True), Plan([depth, 16], 32, True)
        mine, theirs = pack(meta, qkv_weight, proj_weight, inner_weight, down_weight)
        came = swap(theirs, "core")
        small = jnp.concatenate([jnp.pad(jnp.stack(vectors), ((0, 0), (0, 128 - share))),
                                 jnp.pad(inner_bias[None], ((0, 7), (0, 128 - share_f)))])
        blocks_came = swap(blocks, "core")
        chunk_a, chunk_b, chunk = lay(meta, mine, came, small, swap(small, "core"), lengths_a, lengths_b)
        chunk_a, chunk_b, chunk, seg_ids, glob_blocks, blocks_came = stage(
            chunk_a, chunk_b, chunk, seg_ids, glob_blocks, blocks_came
        )
        blocks_mine, blocks_given = pick_blocks(blocks_came)
        segment, globs, lo, n = documents(seg_ids, glob_blocks)

        za = shifts_z(chunk_a, 2, 3)
        both = shift_z(chunk, 1)
        x_came = swap(x_given, "y")
        blocks_came = swap(blocks_given, "y")
        chunk_a, chunk_b, x_came, blocks_came, both, *za = stage(chunk_a, chunk_b, x_came, blocks_came, both, *za)

        near_a = jnp.stack([chunk_a, both[: plan_a.rows]] + za)
        far_a = [swap(near_a, dim) for dim in ("x", "y", "xy")]
        x_own = pair(x_kept, x_came)
        x_oth = swap(x_own, "core")
        zb = [both[plan_a.rows :]] + shifts_z(chunk_b, 2) + shifts_z(after(chunk_b, x_oth), 3)
        tables = spread_tables(model, depth // 2, deep // 2, chunk_b)
        near_a, chunk_b, x_own, x_oth, *rest = stage(near_a, chunk_b, x_own, x_oth, *tables, *far_a, *zb)
        tables, far_a, zb = rest[:4], rest[4:7], rest[7:]
        pieces = [near_a] + far_a

        near_b = jnp.stack([chunk_b] + zb)
        a, b = split_rows(near_b, plan_b.cut)
        a_x, b_y, a_y, b_x = swap(a, "x"), swap(b, "y"), swap(a, "y"), swap(b, "x")
        near_oth = swap(near_b, "core")
        qkv, w_qkv, spread = project_qkv(plan_a, meta, pieces, x_own, x_oth, tables)
        table = jnp.where(c == y, blocks_mine, blocks_came)
        ctx_b, ctx_b_give, lse_b = attention(slice(4, 6), 2, qkv, table)
        d_given, d_kept = given_kept(after(d_out[:, 0], chunk_b))
        near_b, near_oth, a_x, b_y, a_y, b_x, qkv, ctx_b, ctx_b_give, d_given = stage(
            near_b, near_oth, a_x, b_y, a_y, b_x, qkv, ctx_b, ctx_b_give, d_given
        )

        a_xy, b_yx = swap(a_x, "y"), swap(b_y, "x")
        d_came = swap(d_given, "y")
        early = [a_x, a_y, b_y, b_x]
        early_oth = [swap(v, "core") for v in early]
        ctx_b_oth = swap(ctx_b_give, "core")
        ctx_a, ctx_a_give, lse_a = attention(slice(0, 4), 0, qkv, table)
        a_xy, b_yx, d_came, ctx_b_oth, ctx_a, ctx_a_give, *early_oth = stage(
            a_xy, b_yx, d_came, ctx_b_oth, ctx_a, ctx_a_give, *early_oth
        )
        own_b = [near_b] + early[:2] + [a_xy] + early[2:] + [b_yx]
        oth_b = [near_oth] + early_oth[:2] + [swap(a_xy, "core")] + early_oth[2:] + [swap(b_yx, "core")]
        ctx_a_oth = swap(ctx_a_give, "core")
        d_own = pair(d_kept, d_came).reshape(-1, model)
        found = feed_forward(plan_b, meta, own_b, oth_b, [ctx_a, ctx_b], [ctx_a_oth, ctx_b_oth], x_own.reshape(-1, model),
                             d_own, spread, ffw)
        out, gr, hid, gf, x1_low, gp, ga, gc_own, gc_oth, context, vg = found

        out_came, gc_came = swap(out[1], "y"), swap(gc_oth, "core")
        grads_own, grads_oth = weight_grads(back_b, meta, hid, gp, gf, x1_low, context, ga)
        out_came, gc_came, *rest = stage(out_came, gc_came, *grads_own, *grads_oth)
        a, a_far, b, b_far, a_oth, a_far_oth, b_oth, b_far_oth = rest
        layer_out = pair(out[0], out_came)[:, None]
        a_far, b_far = add(a_far, swap(a_far_oth, "core")), add(b_far, swap(b_far_oth, "core"))
        a_far, b_far, gc_came, a_oth, b_oth = stage(a_far, b_far, gc_came, a_oth, b_oth)

        a_came, b_came = swap(a_far, "y"), swap(b_far, "x")
        a_oth, b_oth = swap(a_oth, "core"), swap(b_oth, "core")
        back = lambda p, own, ctx, oth, lse: attention_back(p, qkv, own, gc_came, ctx, oth, lse, table)
        grad_0 = back(0, gc_own, ctx_a, ctx_a_give, lse_a[0:2])
        a_came, b_came, a_oth, b_oth, grad_0, gc_own = stage(a_came, b_came, a_oth, b_oth, grad_0, gc_own)
        a, b = add(a, a_oth, a_came), add(b, b_oth, b_came)
        a_came, b_came = swap(a[ZS:], "x"), swap(b[ZS:], "y")
        grad_1 = back(1, gc_own, ctx_a, ctx_a_give, lse_a[2:4])
        a, b, a_came, b_came, grad_1, gc_own = stage(a, b, a_came, b_came, grad_1, gc_own)
        total = jnp.concatenate([add(b[:ZS], b_came), add(a[:ZS], a_came)], axis=1)
        came_b = scatter_z(total, 1, 2, 3)
        (qa, qa_far, qb, qb_far), sums = qkv_grads(back_early, meta, x_own, x_oth, [grad_0, grad_1], 0)
        qa_came, qb_came = swap(qa_far, "y"), swap(qb_far, "x")
        grad_2 = back(2, after(gc_own, sums), ctx_b, ctx_b_give, lse_b)
        total, qa, qb, qa_came, qb_came, sums, grad_2, *came_b = stage(total, qa, qb, qa_came, qb_came, sums, grad_2, *came_b)
        own_given, oth_given = input_grads(meta, [grad_0, grad_1, grad_2], w_qkv, True)
        oth_given = swap(oth_given, "core")
        last = after(grad_2, own_given)
        ra, ra_far, rb, rb_far = qkv_grads(back_late, meta, x_own, x_oth, [last], 2, sums, vg, tables)
        ra_came, rb_came = swap(ra_far, "y"), swap(rb_far, "x")
        gx_given = add(gr[1], own_given, oth_given)
        gx_came = [swap(gx_given[: EARLY[0]], "y")]
        total_b = added(total[0], *came_b)
        ra, rb, ra_came, rb_came, gx_given, total_b, *gx_came = stage(
            ra, rb, ra_came, rb_came, gx_given, total_b, *gx_came
        )
        gx_came.append(swap(gx_given[EARLY[0] : EARLY[1]], "y"))
        qa = jnp.concatenate([add(qa, qa_came), add(ra, ra_came)], axis=1)
        qb = jnp.concatenate([add(qb, qb_came), add(rb, rb_came)], axis=1)
        qa_came, qb_came = swap(qa[ZS:], "x"), swap(qb[ZS:], "y")
        own_kept, oth_kept = input_grads(meta, [grad_0, grad_1, after(grad_2, qa)], w_qkv, False)
        qa, qb, qa_came, qb_came, own_kept, oth_kept, gx_given, *gx_came = stage(
            qa, qb, qa_came, qb_came, own_kept, oth_kept, gx_given, *gx_came
        )
        gx_came.append(swap(gx_given[EARLY[1] :], "y"))
        total = jnp.concatenate([add(qb[:ZS], qb_came), add(qa[:ZS], qa_came)], axis=1)
        came = scatter_z(total, 1, 2, 3)
        oth_kept = swap(oth_kept, "core")
        gx_kept = add(gr[0], own_kept, oth_kept)

        def finish(total, lengths):
            mine, theirs, at = [], [], 0
            for length in lengths:
                kept, given = by_parity(total[at : at + length], total[at + length : at + 2 * length])
                mine.append(kept)
                theirs.append(given)
                at += 2 * length
            mine = jnp.concatenate(mine, axis=0)
            came = swap(jnp.concatenate(theirs, axis=0).astype(BF), "core").astype(F32)
            halves, cuts, at = by_parity(mine, came), [], 0
            for length in lengths:
                cuts.append([v[at : at + length] for v in halves])
                at += length
            return cuts

        cuts_b = finish(after(total_b, total), lengths_b)
        total, *rest = stage(total, *came, *gx_came)
        came, gx_came = rest[:3], rest[3:]
        grad_input = pair(gx_kept, jnp.concatenate(gx_came))[:, None]
        total_a = added(total[0], *came)
        ends = (0, depth, depth + 32, 2 * depth + 32, 3 * depth)
        one, three, two, rest = (total_a[i:j] for i, j in zip(ends[:4], ends[1:]))
        total_a = jnp.concatenate([one, two, three, rest, total_a[3 * depth :]])
        cuts_a = finish(total_a, lengths_a)
        kept, given = by_parity(total_a[3 * depth :, :128], total_a[3 * depth :, 128:256])
        small = kept + swap(given, "core")
        small = jnp.concatenate([small[v, :share] for v in range(8)] + [small[8, :share_f]])
    else:
        plan_a, plan_b = Plan(sections_a, None), Plan(sections_b, None)
        everyone = lambda w: lax.all_gather(w, ("dp", "seq"), axis=0, tiled=True)
        full_qkv, full_proj, full_inner, full_down = map(everyone, (qkv_weight, proj_weight, inner_weight, down_weight))
        row = everyone(jnp.concatenate(list(vectors) + [inner_bias])[None])
        full_vectors = row[:, : 8 * share].reshape(members, 8, share).transpose(1, 0, 2).reshape(8, CHIPS, 2, -1)
        full_bias = row[:, 8 * share :].reshape(1, CHIPS, 2, -1)
        padded = lambda v: jnp.pad(v, ((0, 0),) * 3 + ((0, 128 - v.shape[3]),))
        rows = jnp.concatenate([padded(full_vectors), padded(full_bias)], axis=0)
        rows = jnp.pad(rows, ((0, 7), (0, 0), (0, 1), (0, 0))).transpose(1, 0, 2, 3).reshape(CHIPS, 16, 384)

        def packed(h):
            col = lambda w, at, width=half: w[:, at : at + width].reshape(CHIPS, -1, width)
            a = [
                jnp.concatenate([col(full_qkv, model * w + half * h + 128 * p, 128) for w in range(3)], axis=2)
                for p in range(3)
            ]
            b = [col(full_proj, half * h)] + [col(full_inner, ffw // 2 * h + half * g) for g in range(groups)]
            return jnp.concatenate(a + [rows], axis=1), jnp.concatenate(b + [col(full_down, half * h)], axis=1)

        segment, globs, lo, n = documents(seg_ids, glob_blocks)
        zero, one = packed(0), packed(1)
        pieces_a = [jnp.where(even, zero[0], one[0])]
        own_b, oth_b = [[v] for v in by_parity(zero[1], one[1])]
        tables = spread_tables(model, depth // 2, deep // 2)
        x_own = pair(x_kept, swap(x_given, "y"))
        x_oth = swap(x_own, "core")
        d_given, d_kept = given_kept(d_out[:, 0])
        d_own = pair(d_kept, swap(d_given, "y")).reshape(-1, model)
        blocks_mine, blocks_given = pick_blocks(swap(blocks, "core"))
        table = jnp.where(c == y, blocks_mine, swap(blocks_given, "y"))
        qkv, w_qkv, spread = project_qkv(plan_a, meta, pieces_a, x_own, x_oth, tables)
        ctx_a, ctx_a_give, lse_a = attention(slice(0, 4), 0, qkv, table)
        ctx_b, ctx_b_give, lse_b = attention(slice(4, 6), 2, qkv, table)
        ctx_oth = [swap(v, "core") for v in (ctx_a_give, ctx_b_give)]
        found = feed_forward(plan_b, meta, own_b, oth_b, [ctx_a, ctx_b], ctx_oth, x_own.reshape(-1, model), d_own, spread, ffw)
        out, gr, hid, gf, x1_low, gp, ga, gc_own, gc_oth, context, vg = found
        layer_out = pair(out[0], swap(out[1], "y"))[:, None]
        gc_came = swap(gc_oth, "core")
        grads_own, grads_oth = weight_grads(plan_b, meta, hid, gp, gf, x1_low, context, ga)
        ctxs = [(ctx_a, ctx_a_give, lse_a[2 * p : 2 * p + 2]) for p in range(2)] + [(ctx_b, ctx_b_give, lse_b)]
        grads = [attention_back(p, qkv, gc_own, gc_came, *ctxs[p], table) for p in range(3)]
        pieces = qkv_grads(plan_a, meta, x_own, x_oth, grads, 0, jnp.zeros((8, 3 * 128), F32), vg, tables)
        own_given, oth_given = input_grads(meta, grads, w_qkv, True)
        own_kept, oth_kept = input_grads(meta, grads, w_qkv, False)
        gx_came = swap(add(gr[1], own_given, swap(oth_given, "core")), "y")
        grad_input = pair(add(gr[0], own_kept, swap(oth_kept, "core")), gx_came)[:, None]
        scatter = lambda v: lax.psum_scatter(v.astype(F32), ("dp", "seq"), scatter_dimension=0, tiled=True)
        found = pieces[0][:, 3 * depth :].astype(F32)
        found = jnp.stack([found[:, :, :128], found[:, :, 128:256]], axis=1).transpose(2, 0, 1, 3)
        small = jnp.concatenate([found[v, :, :, : depth // 2].reshape(-1, 1) for v in range(8)], axis=1)
        small = jnp.concatenate([small.reshape(members, share, 8).transpose(0, 2, 1).reshape(members, -1),
                                 found[8, :, :, : deep // 2].reshape(members, share_f)], axis=1)
        small = scatter(small)[0]
        zero = jnp.zeros((model, half), BF)
        cuts_a, cuts_b = [], []
        for p in range(3):
            part = pieces[0][:, depth * p : depth * p + depth].reshape(-1, half)
            cuts_a.append([scatter(v) for v in by_parity(part, zero)])
        halves, at = by_parity(grads_own[0], grads_oth[0]), 0
        for length in sections_b:
            cuts_b.append([scatter(v[:, at : at + length].reshape(-1, half)) for v in halves])
            at += length

    cut_w = lambda h, p, w: cuts_a[p][h][:, 128 * w : 128 * w + 128]
    grad_qkv = jnp.concatenate([cut_w(h, p, w) for w in range(3) for h in range(2) for p in range(3)], axis=1)
    grad_proj = jnp.concatenate(cuts_b[0], axis=1)
    grad_inner = jnp.concatenate([cuts_b[1 + g][h] for h in range(2) for g in range(groups)], axis=1)
    grad_down = jnp.concatenate(cuts_b[1 + groups], axis=1)
    vector = [small[share * i : share * i + share] for i in range(8)]
    return (
        layer_out,
        grad_input,
        grad_qkv,
        vector[0],
        vector[1],
        grad_proj,
        vector[2],
        vector[3],
        vector[4],
        grad_inner,
        small[8 * share :],
        grad_down,
        vector[5],
        vector[6],
        vector[7],
    )


def solution(mesh):
    row, vec = P(("dp", "seq"), None), P(("dp", "seq"))
    wide = P(None, "dp", "seq", None)
    return jax.shard_map(
        body,
        mesh=mesh,
        in_specs=(wide, row, vec, vec, row, vec, vec, vec, row, vec, row, vec, vec, vec)
        + (P(None, "dp", None), P(None, "dp", "seq", None, None), P(None, "dp", None), wide),
        out_specs=(wide, wide, row, vec, vec, row, vec, vec, vec, row, vec, row, vec, vec, vec),
        check_vma=False,
    )
```

```python
import jax
import jax.numpy as jnp
from jax import lax
from jax.experimental import pallas as pl
from jax.experimental.pallas import tpu as pltpu
from jax.sharding import PartitionSpec as P

HD = 64
BLOCK = 64
EPSILON = 1e-06
BIG = float(2.0**100)
LOWEST = -3.0e38
TQ = 256
TK = 512
CHIPS = 16
SUB = 256
BF = jnp.bfloat16
F32 = jnp.float32
VMEM_LIMIT = 60 << 20
COST = 0.3
CUT = 320
BACK_CUT = 224
EARLY = 224


def nn(left, right):
    return lax.dot_general(left, right, (((1,), (0,)), ((), ())), preferred_element_type=F32)


def nt(left, right):
    return lax.dot_general(left, right, (((1,), (1,)), ((), ())), preferred_element_type=F32)


def tn(left, right):
    return lax.dot_general(left, right, (((0,), (0,)), ((), ())), preferred_element_type=F32)


def smem():
    return pl.BlockSpec(memory_space=pltpu.SMEM)


def anywhere():
    return pl.BlockSpec(memory_space=pl.ANY)


def cost(flops, bytes_accessed, transcendentals):
    part = lambda value: int(value * COST)
    return pl.CostEstimate(flops=part(flops), bytes_accessed=part(bytes_accessed), transcendentals=part(transcendentals))


def shape(dims, kind):
    return jax.ShapeDtypeStruct(dims, kind)


def after(value, *ready):
    if not ready:
        return value
    return lax.optimization_barrier((value,) + ready)[0]


def swap(value, dim):
    if dim == "x":
        return lax.ppermute(value, "dp", [(d, d ^ 1) for d in range(lax.axis_size("dp"))])
    if dim == "xy":
        pairs = [(4 * d + s, 4 * (d ^ 1) + (s ^ 2)) for d in range(lax.axis_size("dp")) for s in range(4)]
        return lax.ppermute(value, ("dp", "seq"), pairs)
    bit = 1 if dim == "core" else 2
    return lax.ppermute(value, "seq", [(s, s ^ bit) for s in range(4)])


def shift_z(value, by):
    size = lax.axis_size("dp") // 2
    return lax.ppermute(value, "dp", [(2 * z + x, (z + by) % size * 2 + x) for z in range(size) for x in range(2)])


ZS = 4


def stage(*values):
    return lax.optimization_barrier(values)


def shifts_z(chunk, *by):
    return [shift_z(chunk, k) for k in by]


def scatter_z(total, *by):
    return [shift_z(total[r], ZS - r) for r in by]


def split_rows(value, cut):
    return value[:, cut:], value[:, :cut]


def added(*values):
    return sum(v.astype(F32) for v in values)


def add(*values):
    return added(*values).astype(BF)


def chip_at(order, near, index, here):
    z = lax.rem(here["z"] - index % ZS + ZS, ZS)
    near = {order[0]: near[0], order[1]: near[1]}
    return z * 4 + lax.rem(here["x"] + near["x"], 2) * 2 + lax.rem(here["y"] + near["y"], 2)


def placed(meta):
    return {"c": meta[0], "x": meta[1], "y": meta[2], "z": meta[3]}


class Plan:
    def __init__(self, sections, cut, joined=False, plain=False):
        self.sections, self.cut, self.joined, self.plain = sections, cut, joined, plain
        self.rows = sum(sections)

    def pieces(self):
        if self.cut is None:
            return [(0, self.rows, None, [None] * CHIPS)]
        if self.plain:
            return [(0, self.rows, "xy", [sides] * ZS) for sides in ((0, 0), (1, 0), (0, 1), (1, 1))]
        found = []
        if not self.joined:
            found.append((0, self.rows, "xy", [(0, 0)] * ZS))
        for first, end, order in ((self.cut, self.rows, "xy"), (0, self.cut, "yx")):
            if self.joined:
                found += [(first, end, order, [(m // ZS, last) for m in range(2 * ZS)]) for last in range(2)]
            else:
                found += [(first, end, order, [sides] * ZS) for sides in ((1, 0), (0, 1), (1, 1))]
        return found

    def shapes(self, width):
        return [shape((len(sides), end - first, width), BF) for first, end, _, sides in self.pieces()]

    def walk(self, here):
        for piece, (first, end, order, sides) in enumerate(self.pieces()):
            for m, side in enumerate(sides):
                chip = m if side is None else chip_at(order, side, m, here)
                start = 0
                for number, length in enumerate(self.sections):
                    lo, hi = max(start, first), min(start + length, end)
                    if lo < hi:
                        yield piece, m, lo - first, hi - first, chip, number, lo - start
                    start += length

    def entries(self):
        return sum(1 for _ in self.walk({"c": 0, "x": 0, "y": 0, "z": 0}))


def move(plan, here, pieces, target, sems, base, numbers=None, back=False):
    copies = []
    for i, (p, m, lo, hi, chip, number, at) in enumerate(plan.walk(here)):
        if numbers is None or number in numbers:
            near, far = pieces[p].at[m, lo:hi, :], target(number, chip, slice(at, at + hi - lo))
            if back:
                near, far = far, near
            copies.append(pltpu.make_async_copy(near, far, sems.at[base + i]))
    return copies


def run(copies):
    for copy in copies:
        copy.start()
    for copy in copies:
        copy.wait()


def spread_vectors(rows, first, second, marks, hidden_marks):
    count = rows.shape[0]
    number = lax.broadcasted_iota(jnp.int32, (9 * CHIPS, count), 0)
    entry = lax.broadcasted_iota(jnp.int32, (9 * CHIPS, count), 1)
    picker = (entry == lax.rem(number, CHIPS) * 16 + number // CHIPS).astype(F32).astype(BF)
    picked = nn(picker, rows).astype(BF)
    model = first.shape[1]
    vectors = nn(picked[: 8 * CHIPS], first).reshape(8, CHIPS, model) * marks[None]
    hidden = nn(picked[8 * CHIPS :], second).reshape(4, 4, model) * hidden_marks[None]
    return jnp.sum(vectors, axis=1), jnp.sum(hidden, axis=1)


def spread_tables(model, share, share_f, *ready):
    lane, col = jnp.arange(384)[:, None], jnp.arange(model)[None, :]
    if ready:
        lane, col = after(lane, *ready), after(col, *ready)
    first = (lane == 128 * (col // share % 2) + col % share).astype(BF)
    second = (lane == 128 * (col // share_f % 2) + col % share_f).astype(BF)
    marks = (jnp.arange(CHIPS)[:, None] == col // (2 * share)).astype(F32)
    hidden_marks = (jnp.arange(4)[:, None] == col // (2 * share_f)).astype(F32)
    return first, second, marks, hidden_marks


def pack_kernel(meta, qkv_ref, proj_ref, inner_ref, down_ref, mine_ref, theirs_ref):
    model = proj_ref.shape[1]
    half, share = model // 2, proj_ref.shape[0]
    for rel, out in ((0, mine_ref), (1, theirs_ref)):
        h = lax.rem(meta[0] + rel, 2)
        lanes = lambda first, n: pl.ds(pl.multiple_of(first, 128), n)
        at = 0
        for p in range(half // 128):
            for w in range(3):
                out[at : at + share, 128 * w : 128 * w + 128] = qkv_ref[:, lanes(model * w + half * h + 128 * p, 128)]
            at += share
        out[at : at + share, :] = proj_ref[:, lanes(half * h, half)]
        at += share
        for g in range(inner_ref.shape[1] // 2 // half):
            out[at : at + share, :] = inner_ref[:, lanes(inner_ref.shape[1] // 2 * h + half * g, half)]
            at += share
        out[at : at + down_ref.shape[0], :] = down_ref[:, lanes(half * h, half)]


def pack(meta, qkv, proj, inner, down):
    half = proj.shape[1] // 2
    rows = proj.shape[0] * (half // 128 + 1 + inner.shape[1] // 2 // half) + down.shape[0]
    return pl.pallas_call(
        pack_kernel,
        in_specs=[smem()] + [pl.BlockSpec(memory_space=pltpu.VMEM)] * 4,
        out_specs=[pl.BlockSpec(memory_space=pltpu.VMEM)] * 2,
        out_shape=[shape((rows, half), BF)] * 2,
        cost_estimate=cost(flops=0, bytes_accessed=8 * rows * half, transcendentals=0),
        name="pack",
    )(meta, qkv, proj, inner, down)


def lay_kernel(lengths_a, lengths_b, meta, mine_ref, came_ref, small_ref, small_came, a_ref, b_ref, all_ref):
    even = meta[0] == 0
    order = lambda mine, came: (jnp.where(even, mine, came), jnp.where(even, came, mine))
    at = 0
    for lengths, out in ((lengths_a, a_ref), (lengths_b, b_ref)):
        to = 0
        for length in lengths:
            for part in order(mine_ref[at : at + length, :], came_ref[at : at + length, :]):
                out[to : to + length, :] = part
                to += length
            at += length
    small = jnp.concatenate(order(small_ref[...], small_came[...]) + (jnp.zeros(small_ref.shape, BF),), axis=1)
    a_ref[a_ref.shape[0] - small.shape[0] :, :] = small
    all_ref[: a_ref.shape[0], :] = a_ref[...]
    all_ref[a_ref.shape[0] :, :] = b_ref[...]


def lay(meta, mine, came, small, small_came, lengths_a, lengths_b):
    width = mine.shape[1]
    rows = 2 * sum(lengths_a) + small.shape[0], 2 * sum(lengths_b)
    return pl.pallas_call(
        lambda *refs: lay_kernel(lengths_a, lengths_b, *refs),
        in_specs=[smem()] + [pl.BlockSpec(memory_space=pltpu.VMEM)] * 4,
        out_specs=[pl.BlockSpec(memory_space=pltpu.VMEM)] * 3,
        out_shape=[shape((n, width), BF) for n in (*rows, sum(rows))],
        cost_estimate=cost(flops=0, bytes_accessed=8 * sum(rows) * width, transcendentals=0),
        name="lay",
    )(meta, mine, came, small, small_came)


def qkv_kernel(plan, pieces_n, *refs):
    meta = refs[0]
    pieces = refs[1 : 1 + pieces_n]
    own_ref, oth_ref, first, second, marks, hidden_marks, out_ref, w_ref, vec_ref, rows_ref, bias_ref, sems = refs[1 + pieces_n :]
    here = placed(meta)
    wide = out_ref.shape[1]
    third = wide // 3

    @pl.when(pl.program_id(0) == 0)
    def _():
        def target(number, chip, rows):
            if number == 3:
                return rows_ref.at[chip, rows, :]
            return w_ref.at[chip, rows, third * number : third * number + third]

        run(move(plan, here, pieces, target, sems, 0))
        rows = rows_ref[...].reshape(CHIPS * 16, 384)
        vectors, hidden = spread_vectors(rows, first[...], second[...], marks[...], hidden_marks[...])
        vec_ref[0:8, :] = vectors
        vec_ref[8:12, :] = hidden
        vec_ref[12:16, :] = jnp.zeros_like(hidden)
        mine = jnp.where(here["c"] == 0, vectors[:, :third], vectors[:, third:])
        bias_ref[...] = jnp.zeros_like(bias_ref)
        for p in range(3):
            for w, source in ((0, 0), (2, 1)):
                at = third * p + 128 * w
                bias_ref[0:1, at : at + 128] = mine[source : source + 1, 128 * p : 128 * p + 128]

    weight = w_ref[...].reshape(-1, wide)
    x = jnp.where(pl.program_id(0) < 2, own_ref[...], oth_ref[...])
    out_ref[...] = (nn(x, weight) + bias_ref[0:1, :]).astype(BF)


def project_qkv(plan, meta, pieces, x_own, x_oth, tables):
    _, tile, model = x_own.shape
    rows = 4 * tile
    width, depth = model // 2, model // CHIPS
    wide = 3 * width
    full = lambda dims: pl.BlockSpec(dims, lambda i, meta: (0,) * len(dims))
    return pl.pallas_call(
        lambda *refs: qkv_kernel(plan, len(pieces), *refs),
        grid_spec=pltpu.PrefetchScalarGridSpec(
            num_scalar_prefetch=1,
            grid=(4,),
            in_specs=[anywhere()] * len(pieces)
            + [pl.BlockSpec((None, tile, model), lambda i, meta: (jnp.minimum(i, 1), 0, 0))]
            + [pl.BlockSpec((None, tile, model), lambda i, meta: (jnp.maximum(i - 2, 0), 0, 0))]
            + [full(t.shape) for t in tables],
            out_specs=[
                pl.BlockSpec((tile, wide), lambda i, meta: (2 * lax.rem(i, 2) + lax.rem(meta[0] + i // 2, 2), 0)),
                full((CHIPS, depth, wide)),
                full((16, model)),
            ],
            scratch_shapes=[
                pltpu.VMEM((CHIPS, 16, width), BF),
                pltpu.VMEM((8, wide), F32),
                pltpu.SemaphoreType.DMA((plan.entries(),)),
            ],
        ),
        out_shape=[shape((rows, wide), BF), shape((CHIPS, depth, wide), BF), shape((16, model), F32)],
        compiler_params=pltpu.CompilerParams(vmem_limit_bytes=14 << 20),
        cost_estimate=pl.CostEstimate(
            flops=2 * rows * model * wide, bytes_accessed=2 * rows * (model + wide), transcendentals=0
        ),
        name="project_qkv",
    )(meta, *pieces, x_own, x_oth, *tables)


def fill_features(seg_ref, rand_ref, first_global, second_global, key_ref, query_ref):
    heads, _, length = key_ref.shape
    blocks = length // BLOCK
    at = lax.broadcasted_iota(jnp.int32, (blocks, length), 1) // BLOCK
    row = lax.broadcasted_iota(jnp.int32, (blocks, length), 0)
    seen = jnp.abs(at - row) <= 1
    for chosen in (first_global, second_global):
        seen = seen | (at == chosen) | (row == chosen)
    same = lax.broadcasted_iota(jnp.int32, (HD - blocks, length), 0) == seg_ref[...]
    for h in range(heads):
        picked = seen
        for r in range(rand_ref.shape[2]):
            picked = picked | (at == rand_ref[h, :, r : r + 1])
        key_ref[h, 0:blocks, :] = jnp.where(picked, 0.0, 1.0).astype(BF)
        key_ref[h, blocks:HD, :] = jnp.where(same, 0.0, 1.0).astype(BF)
    query_ref[0:blocks, :] = jnp.where(at == row, -BIG, 0.0).astype(BF)
    query_ref[blocks:HD, :] = jnp.where(same, -BIG, 0.0).astype(BF)


def of_pair(ref, p, w):
    return ref[:, 384 * p + 128 * w : 384 * p + 128 * w + 128]


def widen_pair(p, qkv_ref, key_feat, query_feat, key_wide, query_wide):
    scaled = of_pair(qkv_ref, p, 0) * BF(HD**-0.5)
    queries, keys = scaled.T, of_pair(qkv_ref, p, 1).T
    a, b = 2 * p, 2 * p + 1
    query_wide[a, 0:HD, :] = queries[0:HD]
    query_wide[a, HD:128, :] = query_feat[...]
    query_wide[b, 0:HD, :] = query_feat[...]
    query_wide[b, HD:128, :] = queries[HD:128]
    key_wide[a] = jnp.concatenate([keys[0:HD], key_feat[a]], axis=0).T
    key_wide[b] = jnp.concatenate([key_feat[b], keys[HD:128]], axis=0).T
    return keys


def over_keys(start, n, step, carry):
    carry = lax.fori_loop(0, n // 2, lambda j, carry: step(start + j * TK, j * TK, TK, carry), carry)
    done = n // 2 * TK
    return lax.fori_loop(0, lax.rem(n, 2), lambda j, carry: step(start + done, done, TK // 2, carry), carry)


def attend_kernel(meta, lo_ref, n_ref, glob_ref, qkv_ref, seg_ref, rand_ref, own_ref, oth_ref, lse_ref,
                  key_feat, query_feat, key_wide, query_wide, values, turned, store):
    heads, length = lse_ref.shape
    fill_features(seg_ref, rand_ref, glob_ref[0], glob_ref[1], key_feat, query_feat)
    for p in range(heads // 2):
        widen_pair(p, qkv_ref, key_feat, query_feat, key_wide, query_wide)
        values[128 * p : 128 * p + 128, :] = of_pair(qkv_ref, p, 2).T

    def tile(i, _):
        qs = pl.ds(pl.multiple_of(i * TQ, TQ), TQ)

        def scan(start, at, size, tops):
            ks = pl.ds(pl.multiple_of(start, 128), size)
            to = pl.ds(pl.multiple_of(at, TK), size)
            raised = []
            for h in range(heads):
                scores = nn(key_wide[h, ks, :], query_wide[h, :, qs])
                store[h, to, :] = scores
                raised.append(jnp.maximum(tops[h], jnp.max(scores.reshape(size // 8, 8, TQ), axis=0)))
            return tuple(raised)

        tops = over_keys(lo_ref[i], n_ref[i], scan, (jnp.full((8, TQ), LOWEST, F32),) * heads)
        tops = [jnp.max(top, axis=0, keepdims=True) for top in tops]

        def collect(start, at, size, carry):
            ks = pl.ds(pl.multiple_of(start, 128), size)
            to = pl.ds(pl.multiple_of(at, TK), size)
            new = []
            for h in range(heads):
                total, summed = carry[h]
                expo = jnp.exp(store[h, to, :] - tops[h])
                total = total + jnp.sum(expo.reshape(size // 8, 8, TQ), axis=0)
                summed = summed + nn(values[HD * h : HD * h + HD, ks], expo.astype(BF))
                new.append((total, summed))
            return tuple(new)

        none = (jnp.zeros((8, TQ), F32), jnp.zeros((HD, TQ), F32))
        found = over_keys(lo_ref[i], n_ref[i], collect, (none,) * heads)
        for h in range(heads):
            total, summed = found[h]
            total = jnp.sum(total, axis=0, keepdims=True)
            turned[HD * h : HD * h + HD, qs] = (summed / total).astype(BF)
            lse_ref[h : h + 1, qs] = tops[h] + jnp.log(total)
        return 0

    lax.fori_loop(0, length // TQ, tile, 0)
    quarter = length // 4
    even = meta[0] == 0
    for p in range(heads // 2):
        result = turned[128 * p : 128 * p + 128, :].T
        for n in range(2):
            one, two = (result[quarter * k : quarter * k + quarter] for k in (2 * n, 2 * n + 1))
            where = (slice(quarter * n, quarter * n + quarter), slice(128 * p, 128 * p + 128))
            own_ref[where] = jnp.where(even, one, two)
            oth_ref[where] = jnp.where(even, two, one)


def whole(dims):
    return pl.BlockSpec(dims, lambda *_: (0,) * len(dims))


def attend(meta, qkv, number, seg_row, table, globs, lo, n):
    length = qkv.shape[0]
    heads, blocks = table.shape[:2]
    wide = heads * HD
    return pl.pallas_call(
        attend_kernel,
        grid=(1,),
        in_specs=[smem()] * 4
        + [pl.BlockSpec((length, 3 * wide), lambda i: (0, number)), whole((1, length)), whole((heads, blocks, 3))],
        out_specs=[whole((length // 2, wide))] * 2 + [whole((heads, length))],
        out_shape=[shape((length // 2, wide), BF)] * 2 + [shape((heads, length), F32)],
        scratch_shapes=[
            pltpu.VMEM((heads, HD, length), BF),
            pltpu.VMEM((HD, length), BF),
            pltpu.VMEM((heads, length, 128), BF),
            pltpu.VMEM((heads, 128, length), BF),
            pltpu.VMEM((wide, length), BF),
            pltpu.VMEM((wide, length), BF),
            pltpu.VMEM((heads, length, TQ), F32),
        ],
        compiler_params=pltpu.CompilerParams(vmem_limit_bytes=28 << 20),
        cost_estimate=pl.CostEstimate(
            flops=heads * length * length * 700, bytes_accessed=10 * length * wide, transcendentals=heads * length * length // 2
        ),
        name="attend",
    )(meta, lo, n, globs, qkv, seg_row, table)


def attend_back_kernel(meta, lo_ref, n_ref, glob_ref, qkv_ref, own_ref, oth_ref, ctx_own, ctx_oth, lse_ref, seg_ref,
                       rand_ref, out_ref, key_feat, query_feat, key_wide, query_wide, value_one,
                       grad_turned, keys_turned, inner_ref, dkt, dvt, dqt, grads):
    heads, length = lse_ref.shape
    quarter = length // 4
    fill_features(seg_ref, rand_ref, glob_ref[0], glob_ref[1], key_feat, query_feat)
    for rel, source, ctx in ((0, own_ref, ctx_own), (1, oth_ref, ctx_oth)):
        for n in range(2):
            at = 2 * n + lax.rem(meta[0] + rel, 2)
            rows = pl.ds(pl.multiple_of(at * quarter, quarter), quarter)
            grads[0, rows, :] = source[quarter * n : quarter * n + quarter, :]
            grads[1, rows, :] = ctx[quarter * n : quarter * n + quarter, :]
    low = lax.broadcasted_iota(jnp.int32, (length, 128), 1) < HD
    zero = jnp.zeros((length, 128), BF)
    for p in range(heads // 2):
        cols = slice(128 * p, 128 * p + 128)
        keys = widen_pair(p, qkv_ref, key_feat, query_feat, key_wide, query_wide)
        keys_turned[cols, :] = keys
        grad, value = grads[0, :, cols], of_pair(qkv_ref, p, 2)
        for e in range(2):
            keep = low if e == 0 else ~low
            value_one[2 * p + e] = jnp.where(keep, value, zero)
        turned = grad.T
        grad_turned[cols, :] = turned
        product = turned.astype(F32) * grads[1, :, cols].T.astype(F32)
        for e in range(2):
            h = 2 * p + e
            inner_ref[h : h + 1, :] = jnp.sum(product[HD * e : HD * e + HD], axis=0, keepdims=True)
    dkt[...] = jnp.zeros_like(dkt)
    dvt[...] = jnp.zeros_like(dvt)

    def tile(i, _):
        qs = pl.ds(pl.multiple_of(i * TQ, TQ), TQ)

        def body(start, at, size, carry):
            ks = pl.ds(pl.multiple_of(start, 128), size)
            new = []
            scores = [nn(key_wide[h, ks, :], query_wide[h, :, qs]) for h in range(heads)]
            grad_probs = [nn(value_one[h, ks, :], grad_turned[128 * (h // 2) : 128 * (h // 2) + 128, qs]) for h in range(heads)]
            probs = [jnp.exp(scores[h] - lse_ref[h : h + 1, qs]) for h in range(heads)]
            low = [prob.astype(BF) for prob in probs]
            for h in range(heads):
                rows = slice(HD * h, HD * h + HD)
                mine = slice(HD * (h % 2), HD * (h % 2) + HD)
                dvt[rows, ks] += nt(grad_turned[rows, qs], low[h])
            grad_scores = [(probs[h] * (grad_probs[h] - inner_ref[h : h + 1, qs])).astype(BF) for h in range(heads)]
            for h in range(heads):
                rows = slice(HD * h, HD * h + HD)
                mine = slice(HD * (h % 2), HD * (h % 2) + HD)
                new.append(carry[h] + nn(keys_turned[rows, ks], grad_scores[h]))
            for h in range(heads):
                rows = slice(HD * h, HD * h + HD)
                mine = slice(HD * (h % 2), HD * (h % 2) + HD)
                dkt[rows, ks] += nt(query_wide[h, mine, qs], grad_scores[h])
            return tuple(new)

        found = over_keys(lo_ref[i], n_ref[i], body, (jnp.zeros((HD, TQ), F32),) * heads)
        for h in range(heads):
            dqt[HD * h : HD * h + HD, qs] = (found[h] * HD**-0.5).astype(BF)
        return 0

    lax.fori_loop(0, length // TQ, tile, 0)
    for p in range(heads // 2):
        cols = slice(128 * p, 128 * p + 128)
        for w, value in enumerate((dqt[cols, :], dkt[cols, :].astype(BF), dvt[cols, :].astype(BF))):
            out_ref[:, 384 * p + 128 * w : 384 * p + 128 * w + 128] = value.T


def attend_back(meta, qkv, number, own, oth, ctx, ctx_oth, lse, part, seg_row, table, globs, lo, n):
    length = qkv.shape[0]
    heads, blocks = table.shape[:2]
    wide = heads * HD
    group = lambda w, i=number: pl.BlockSpec((length, w), lambda _: (0, i))
    half = pl.BlockSpec((length // 2, wide), lambda _: (0, number))
    return pl.pallas_call(
        attend_back_kernel,
        grid=(1,),
        in_specs=[smem()] * 4
        + [group(3 * wide), half, half]
        + [pl.BlockSpec((length // 2, wide), lambda _: (0, part))] * 2
        + [whole((heads, length)), whole((1, length)), whole((heads, blocks, 3))],
        out_specs=whole((length, 3 * wide)),
        out_shape=shape((length, 3 * wide), BF),
        scratch_shapes=[
            pltpu.VMEM((heads, HD, length), BF),
            pltpu.VMEM((HD, length), BF),
            pltpu.VMEM((heads, length, 128), BF),
            pltpu.VMEM((heads, 128, length), BF),
            pltpu.VMEM((heads, length, 128), BF),
            pltpu.VMEM((wide, length), BF),
            pltpu.VMEM((wide, length), BF),
            pltpu.VMEM((heads, length), F32),
            pltpu.VMEM((wide, length), F32),
            pltpu.VMEM((wide, length), F32),
            pltpu.VMEM((wide, length), BF),
            pltpu.VMEM((2, length, wide), BF),
        ],
        compiler_params=pltpu.CompilerParams(vmem_limit_bytes=17 << 20),
        cost_estimate=cost(
            flops=heads * length * length * 1500, bytes_accessed=20 * length * wide, transcendentals=heads * length * length // 2
        ),
        name="attend_back",
    )(meta, lo, n, globs, qkv, own, oth, ctx, ctx_oth, lse, seg_row, table)


def key_ranges(segment):
    length = segment.shape[0]
    first, last = segment[::TQ], segment[TQ - 1 :: TQ]
    lo = jnp.sum(segment[None, :] < first[:, None], axis=1, dtype=jnp.int32) // 128 * 128
    hi = jnp.sum(segment[None, :] <= last[:, None], axis=1, dtype=jnp.int32)
    n = (hi - lo + TK // 2 - 1) // (TK // 2)
    return jnp.minimum(lo, length - n * (TK // 2)), n


def centre(value):
    centred = value - jnp.mean(value, axis=1, keepdims=True)
    rate = lax.rsqrt(jnp.mean(centred * centred, axis=1, keepdims=True) + EPSILON)
    return centred * rate, rate


def norm_back(grad, normed, rate):
    return rate * (
        grad
        - jnp.mean(grad, axis=1, keepdims=True)
        - normed * jnp.mean(grad * normed, axis=1, keepdims=True)
    )


def cut(value):
    half = value.shape[1] // 2
    return value[:, :half], value[:, half:]


def wide_target(proj, inner, down, half):
    width = proj.shape[2] // 2
    groups = inner.shape[2] // 2 // width

    def target(number, chip, rows):
        if number == 0:
            return proj.at[chip, rows, pl.ds(pl.multiple_of(half * width, 128), width)]
        if number <= groups:
            first = half * (groups * width) + width * (number - 1)
            return inner.at[chip, rows, pl.ds(pl.multiple_of(first, 128), width)]
        return down.at[chip, rows, pl.ds(pl.multiple_of(half * width, 128), width)]

    return target


def ffn_kernel(plan, pieces_n, ctx_n, *refs):
    meta = refs[0]
    own_pieces = refs[1 : 1 + pieces_n]
    oth_pieces = refs[1 + pieces_n : 1 + 2 * pieces_n]
    refs = refs[1 + 2 * pieces_n :]
    ctx_own, ctx_oth = refs[:ctx_n], refs[ctx_n : 2 * ctx_n]
    (x_ref, d_came, d_kept, vec_ref,
     given_ref, out_ref, gr_ref, hid_ref, gf_ref, low_ref, gp_ref, ga_ref, gc_own, gc_oth, ctx_ref, vg_ref,
     proj, inner, down, slope, sems) = refs[2 * ctx_n :]
    here = placed(meta)
    c = here["c"]
    step = pl.program_id(0)
    model = x_ref.shape[1]
    wide = hid_ref.shape[1]

    def copies(*numbers):
        found = []
        for rel, pieces in ((0, own_pieces), (1, oth_pieces)):
            target = wide_target(proj, inner, down, lax.rem(c + rel, 2))
            found += move(plan, here, pieces, target, sems, rel * plan.entries(), numbers)
        return found

    first, last = 0, len(plan.sections) - 1
    orders = [(first,), tuple(range(1, last)), (last,)]

    @pl.when(step == 0)
    def _():
        for numbers in orders:
            for copy in copies(*numbers):
                copy.start()
        vg_ref[...] = jnp.zeros_like(vg_ref)

    def arrived(which):
        @pl.when(step == 0)
        def _():
            for copy in copies(*orders[which]):
                copy.wait()

    vec = lambda n: vec_ref[n : n + 1, :]
    w_proj = lambda: proj[...].reshape(model, model)
    w_inner = lambda j: inner[:, :, model * j : model * j + model].reshape(model, model)
    span = CHIPS * model // wide
    w_down = lambda j: down[span * j : span * j + span].reshape(model, model)
    total = lambda value: jnp.sum(value, axis=0, keepdims=True)
    chunks = wide // model
    spans = [slice(at, at + SUB) for at in range(0, x_ref.shape[0], SUB)]
    columns = [slice(model * j, model * j + model) for j in range(chunks)]

    arrived(0)
    first = []
    for rows in spans:
        own = jnp.concatenate([ref[rows, :] for ref in ctx_own], axis=1)
        oth = jnp.concatenate([ref[rows, :] for ref in ctx_oth], axis=1)
        context = jnp.concatenate([jnp.where(c == 0, own, oth), jnp.where(c == 0, oth, own)], axis=1)
        ctx_ref[rows, :] = context
        n1, rate1 = centre(x_ref[rows, :].astype(F32) + (nn(context, w_proj()) + vec(2)))
        x1 = n1 * vec(3) + vec(4)
        low = x1.astype(BF)
        low_ref[rows, :] = low
        first.append((n1, rate1, x1, low))
    arrived(1)
    arrived(2)
    ffn = [None] * len(spans)
    for j, cols in enumerate(columns):
        for k, rows in enumerate(spans):
            pre = nn(first[k][3], w_inner(j)) + vec(8 + j)
            below = 0.5 + 0.5 * lax.erf(pre * 0.7071067811865476)
            slope[rows, cols] = below + pre * (jnp.exp(-0.5 * (pre * pre)) * 0.3989422804014327)
            hidden = (pre * below).astype(BF)
            hid_ref[rows, cols] = hidden
            more = nn(hidden, w_down(j))
            ffn[k] = more if ffn[k] is None else ffn[k] + more
    second = []
    for k, rows in enumerate(spans):
        n2, rate2 = centre(first[k][2] + (ffn[k] + vec(5)))
        out_ref[rows, :] = (n2 * vec(6) + vec(7)).astype(BF)
        grad = jnp.where(step == 0, d_came[rows, :], d_kept[rows, :]).astype(F32)
        gr2 = norm_back(grad * vec(6), n2, rate2)
        gf = gr2.astype(BF)
        gf_ref[rows, :] = gf
        vg_ref[6:7, :] += total(grad * n2)
        vg_ref[7:8, :] += total(grad)
        vg_ref[5:6, :] += total(gf.astype(F32))
        second.append([gr2, gf])
    for j, cols in enumerate(columns):
        for k, rows in enumerate(spans):
            gp = (nt(second[k][1], w_down(j)) * slope[rows, cols]).astype(BF)
            gp_ref[rows, cols] = gp
            vg_ref[8 + j : 9 + j, :] += total(gp.astype(F32))
            second[k][0] = second[k][0] + nt(gp, w_inner(j))
    for k, rows in enumerate(spans):
        n1, rate1, gx1 = first[k][0], first[k][1], second[k][0]
        gr1 = norm_back(gx1 * vec(3), n1, rate1)
        gr_ref[rows, :] = gr1
        ga = gr1.astype(BF)
        ga_ref[rows, :] = ga
        vg_ref[3:4, :] += total(gx1 * n1)
        vg_ref[4:5, :] += total(gx1)
        vg_ref[2:3, :] += total(ga.astype(F32))
        gc = cut(nt(ga, w_proj()))
        gc_own[rows, :] = jnp.where(c == 0, gc[0], gc[1]).astype(BF)
        gc_oth[rows, :] = jnp.where(c == 0, gc[1], gc[0]).astype(BF)

    @pl.when(step == 0)
    def _():
        given_ref[...] = out_ref[...]


def feed_forward(plan, meta, own_pieces, oth_pieces, ctx, ctx_oth, x_own, d_came, d_out, vectors, wide):
    rows, model = x_own.shape
    half, tall = model // 2, rows // 2
    tile = lambda n: pl.BlockSpec((tall, n), lambda i, meta: (lax.rem(i + 1 + meta[2], 2), 0))
    full = lambda dims: pl.BlockSpec(dims, lambda i, meta: (0,) * len(dims))
    scratch = [
        pltpu.VMEM((CHIPS, model // CHIPS, model), BF),
        pltpu.VMEM((CHIPS, model // CHIPS, wide), BF),
        pltpu.VMEM((CHIPS, wide // CHIPS, model), BF),
        pltpu.VMEM((tall, wide), F32),
        pltpu.SemaphoreType.DMA((2 * plan.entries(),)),
    ]
    outs = [(wide, BF), (model, BF), (model, BF), (wide, BF), (model, BF), (half, BF), (half, BF), (model, BF)]
    return pl.pallas_call(
        lambda *refs: ffn_kernel(plan, len(own_pieces), len(ctx), *refs),
        grid_spec=pltpu.PrefetchScalarGridSpec(
            num_scalar_prefetch=1,
            grid=(2,),
            in_specs=[anywhere()] * (2 * len(own_pieces))
            + [tile(v.shape[1]) for v in ctx + ctx_oth]
            + [tile(model), full((tall, model)), pl.BlockSpec((None, tall, model), lambda i, meta: (meta[2], 0, 0))]
            + [full(vectors.shape)],
            out_specs=[full((tall, model))] * 2
            + [pl.BlockSpec((None, tall, model), lambda i, meta: (i, 0, 0))]
            + [tile(w) for w, _ in outs]
            + [full((16, model))],
            scratch_shapes=scratch,
        ),
        out_shape=[shape((tall, model), BF)] * 2
        + [shape((2, tall, model), F32)]
        + [shape((rows, w), kind) for w, kind in outs]
        + [shape((16, model), F32)],
        compiler_params=pltpu.CompilerParams(vmem_limit_bytes=VMEM_LIMIT),
        cost_estimate=cost(
            flops=4 * rows * model * (model + 2 * wide), bytes_accessed=rows * (8 * wide + 20 * model), transcendentals=2 * rows * wide
        ),
        name="feed_forward",
    )(meta, *own_pieces, *oth_pieces, *ctx, *ctx_oth, x_own, d_came, d_out, vectors)


def weight_grads_kernel(plan, pieces_n, *refs):
    meta, hid_ref, gp_ref, gf_ref, low_ref, ctx_ref, ga_ref = refs[:7]
    own_pieces = refs[7 : 7 + pieces_n]
    oth_pieces = refs[7 + pieces_n : 7 + 2 * pieces_n]
    proj, inner, down, sems = refs[7 + 2 * pieces_n :]
    here = placed(meta)
    c = here["c"]
    step = pl.program_id(0)
    model = gf_ref.shape[1]
    span = CHIPS * model // inner.shape[2]
    steps = inner.shape[2] // model

    @pl.when(step == 0)
    def _():
        proj[...] = tn(ctx_ref[...], ga_ref[...]).reshape(proj.shape).astype(BF)

    more_inner = tn(low_ref[...], gp_ref[...])
    inner[:, :, pl.ds(pl.multiple_of(step * model, 128), model)] = more_inner.reshape(CHIPS, -1, model).astype(BF)
    more_down = tn(hid_ref[...], gf_ref[...])
    down[pl.ds(step * span, span)] = more_down.reshape(span, -1, model).astype(BF)

    @pl.when(step == steps - 1)
    def _():
        copies = []
        for rel, pieces in ((0, own_pieces), (1, oth_pieces)):
            target = wide_target(proj, inner, down, lax.rem(c + rel, 2))
            copies += move(plan, here, pieces, target, sems, len(copies), back=True)
        run(copies)


def weight_grads(plan, meta, hid, gp, gf, low, context, ga):
    rows, model = gf.shape
    wide, half = hid.shape[1], model // 2
    pieces = plan.shapes(half)
    cols = pl.BlockSpec((rows, model), lambda i: (0, i))
    found = pl.pallas_call(
        lambda *refs: weight_grads_kernel(plan, len(pieces), *refs),
        grid=(wide // model,),
        in_specs=[smem(), cols, cols] + [whole((rows, model))] * 4,
        out_specs=[anywhere()] * (2 * len(pieces)),
        out_shape=pieces * 2,
        scratch_shapes=[
            pltpu.VMEM((CHIPS, model // CHIPS, model), BF),
            pltpu.VMEM((CHIPS, model // CHIPS, wide), BF),
            pltpu.VMEM((CHIPS, wide // CHIPS, model), BF),
            pltpu.SemaphoreType.DMA((2 * plan.entries(),)),
        ],
        compiler_params=pltpu.CompilerParams(vmem_limit_bytes=VMEM_LIMIT),
        cost_estimate=cost(
            flops=2 * rows * model * (model + 2 * wide), bytes_accessed=rows * (4 * wide + 8 * model), transcendentals=0
        ),
        name="weight_grads",
    )(meta, hid, gp, gf, low, context, ga)
    return found[: len(pieces)], found[len(pieces) :]


def gather_vectors(vectors, hidden, first, second, marks, hidden_marks):
    model = first.shape[1]
    one = nt((vectors[:, None, :] * marks[None]).reshape(-1, model).astype(BF), first)
    two = nt((hidden[:, None, :] * hidden_marks[None]).reshape(-1, model).astype(BF), second)
    laid = jnp.concatenate([one, two], axis=0).astype(BF)
    number = lax.broadcasted_iota(jnp.int32, (9 * CHIPS, 16 * CHIPS), 0)
    entry = lax.broadcasted_iota(jnp.int32, (9 * CHIPS, 16 * CHIPS), 1)
    picker = (entry == lax.rem(number, CHIPS) * 16 + number // CHIPS).astype(F32).astype(BF)
    return tn(picker, laid)


def qkv_grads_kernel(plan, pieces_n, pairs, number, last, *refs):
    meta, own_ref, oth_ref = refs[:3]
    grads = refs[3 : 3 + pairs]
    refs = refs[3 + pairs :]
    if last:
        (known_ref, vg_ref, first, second, marks, hidden_marks), refs = refs[:6], refs[6:]
    pieces, refs = refs[:pieces_n], refs[pieces_n:]
    if last:
        g_ref, sems, rows_ref, vec_ref, sums_ref = refs
    else:
        sums_ref, g_ref, sems = refs
    here = placed(meta)
    quarter, width = own_ref.shape[1], own_ref.shape[2] // 2
    sums_ref[...] = known_ref[...] if last else jnp.zeros_like(sums_ref)
    for p, source in enumerate(grads):
        total = None
        for rel, x_ref in ((0, own_ref), (1, oth_ref)):
            for n in range(2):
                at = 2 * n + lax.rem(here["c"] + rel, 2)
                more = tn(x_ref[n], source[pl.ds(pl.multiple_of(at * quarter, quarter), quarter), :])
                total = more if total is None else total + more
        g_ref[p] = total.reshape(g_ref.shape[1:]).astype(BF)
        sums_ref[number + p : number + p + 1, :] = jnp.sum(source[...].astype(F32), axis=0, keepdims=True)
    if last:
        even = here["c"] == 0
        vec_ref[...] = vg_ref[...]
        none = jnp.zeros((1, 128), F32)
        for p in range(number + pairs):
            for row, w in ((0, 0), (1, 2)):
                value = sums_ref[p : p + 1, 128 * w : 128 * w + 128]
                vec_ref[row : row + 1, 128 * p : 128 * p + 128] = jnp.where(even, value, none)
                at = width + 128 * p
                vec_ref[row : row + 1, at : at + 128] = jnp.where(even, none, value)
        found = gather_vectors(vec_ref[0:8, :], vec_ref[8:12, :], first[...], second[...], marks[...], hidden_marks[...])
        rows_ref[...] = found.reshape(rows_ref.shape).astype(BF)

    def target(section, chip, rows):
        if section == pairs:
            return rows_ref.at[chip, rows, :]
        return g_ref.at[section, chip, rows, :]

    run(move(plan, here, pieces, target, sems, 0, back=True))


def qkv_grads(plan, meta, x_own, x_oth, grads, number, sums=None, vg=None, tables=()):
    rows, model = 4 * x_own.shape[1], x_own.shape[2]
    width, depth = grads[0].shape[1], model // CHIPS
    last = vg is not None
    pieces = plan.shapes(width)
    more = [sums, vg, *tables] if last else []
    summed = shape((8, width), F32)
    found = pl.pallas_call(
        lambda *refs: qkv_grads_kernel(plan, len(pieces), len(grads), number, last, *refs),
        grid=(1,),
        in_specs=[smem(), whole(x_own.shape), whole(x_own.shape)]
        + [whole((rows, width))] * len(grads)
        + [whole(v.shape) for v in more],
        out_specs=[anywhere()] * len(pieces) + ([] if last else [whole(summed.shape)]),
        out_shape=pieces + ([] if last else [summed]),
        scratch_shapes=[
            pltpu.VMEM((len(grads), CHIPS, depth, width), BF),
            pltpu.SemaphoreType.DMA((plan.entries(),)),
        ]
        + ([pltpu.VMEM((CHIPS, 16, width), BF), pltpu.VMEM((16, model), F32), pltpu.VMEM((8, width), F32)] if last else []),
        compiler_params=pltpu.CompilerParams(vmem_limit_bytes=20 << 20),
        cost_estimate=cost(
            flops=2 * len(grads) * rows * model * width, bytes_accessed=2 * rows * (model + 3 * width), transcendentals=0
        ),
        name="qkv_grads",
    )(meta, x_own, x_oth, *grads, *more)
    return found if last else (found[:-1], found[-1])


def input_grads_kernel(meta, *refs):
    *grads, w_ref, own_ref, oth_ref = refs
    width = grads[0].shape[1]
    total = None
    for p, source in enumerate(grads):
        weight = w_ref[:, :, width * p : width * p + width].reshape(-1, width)
        more = nt(source[...], weight)
        total = more if total is None else total + more

    @pl.when(pl.program_id(0) == 0)
    def _():
        oth_ref[...] = total.astype(BF)

    @pl.when(pl.program_id(0) == 1)
    def _():
        own_ref[...] = total.astype(BF)


def input_grads(meta, grads, weights, given):
    rows, width = grads[0].shape
    model = weights.shape[0] * weights.shape[1]
    quarter = rows // 4
    half = lambda meta: 1 - meta[2] if given else meta[2]
    at = lambda i, meta: 2 * half(meta) + lax.rem(meta[0] + 1 + i, 2)
    return pl.pallas_call(
        input_grads_kernel,
        grid_spec=pltpu.PrefetchScalarGridSpec(
            num_scalar_prefetch=1,
            grid=(2,),
            in_specs=[pl.BlockSpec((quarter, width), lambda i, meta: (at(i, meta), 0))] * len(grads) + [whole(weights.shape)],
            out_specs=[whole((quarter, model))] * 2,
        ),
        out_shape=[shape((quarter, model), BF)] * 2,
        compiler_params=pltpu.CompilerParams(vmem_limit_bytes=14 << 20),
        cost_estimate=cost(
            flops=3 * rows * model * width, bytes_accessed=rows * (model + 3 * width), transcendentals=0
        ),
        name="input_grads",
    )(meta, *grads, weights)


def body(
    tokens,
    qkv_weight,
    query_bias,
    value_bias,
    proj_weight,
    proj_bias,
    attn_gain,
    attn_shift,
    inner_weight,
    inner_bias,
    down_weight,
    down_bias,
    ffn_gain,
    ffn_shift,
    seg_ids,
    rand_blocks,
    glob_blocks,
    d_out,
):
    dp, seq = lax.axis_index("dp"), lax.axis_index("seq")
    members = lax.axis_size("dp") * lax.axis_size("seq")
    near = lax.axis_size("dp") == 2 * ZS
    y, c = seq // 2, seq % 2
    even, low_y = c == 0, y == 0
    meta = jnp.stack([c, dp % 2, y, dp // 2]).astype(jnp.int32)
    model = tokens.shape[3]
    half = model // 2
    ffw = inner_weight.shape[1]
    share, share_f = qkv_weight.shape[0], down_weight.shape[0]
    groups = ffw // 2 // half
    depth, deep = model // CHIPS, ffw // CHIPS
    by_parity = lambda mine, other: (jnp.where(even, mine, other), jnp.where(even, other, mine))

    pair = lambda kept, came: jnp.where(low_y, jnp.stack([kept, came]), jnp.stack([came, kept]))

    def given_kept(value):
        return jnp.where(low_y, value[1], value[0]), jnp.where(low_y, value[0], value[1])

    vectors = (query_bias, value_bias, proj_bias, attn_gain, attn_shift, down_bias, ffn_gain, ffn_shift)
    sections_a, sections_b = [depth] * 3 + [16], [depth] * (1 + groups) + [deep]
    lengths_a, lengths_b = [share] * 3, [share] * (1 + groups) + [share_f]
    def documents(seg_ids, glob_blocks):
        segment = jnp.where(low_y, seg_ids[0, 0], seg_ids[1, 0])
        return segment, jnp.where(low_y, glob_blocks[0, 0], glob_blocks[1, 0]), *key_ranges(segment)

    blocks = rand_blocks[:, 0]
    x_given, x_kept = given_kept(tokens[:, 0])

    def pick_blocks(came):
        of_chip = by_parity(blocks, came)
        mine = jnp.where(low_y, *(jnp.concatenate([v[m] for v in of_chip]) for m in range(2)))
        return mine, jnp.where(low_y, *(jnp.concatenate([v[1 - m] for v in of_chip]) for m in range(2)))

    def attention(heads, number, qkv, table):
        return attend(meta, qkv, number, segment[None], table[heads], globs, lo, n)

    def attention_back(p, qkv, own, oth, ctx, ctx_oth, lse, table):
        part = p if p < 2 else 0
        return attend_back(meta, qkv, p, own, oth, ctx, ctx_oth, lse, part, segment[None], table[2 * p : 2 * p + 2], globs, lo, n)

    if near:
        plan_a, plan_b = Plan(sections_a, 80, plain=True), Plan(sections_b, CUT)
        back_b = Plan(sections_b, BACK_CUT, True)
        back_early, back_late = Plan([depth] * 2, depth, True), Plan([depth, 16], 32, True)
        mine, theirs = pack(meta, qkv_weight, proj_weight, inner_weight, down_weight)
        came = swap(theirs, "core")
        mine, inner_bias, blocks, *vectors = stage(mine, inner_bias, blocks, *vectors)
        small = jnp.concatenate([jnp.pad(jnp.stack(vectors), ((0, 0), (0, 128 - share))),
                                 jnp.pad(inner_bias[None], ((0, 7), (0, 128 - share_f)))])
        blocks_came = swap(blocks, "core")
        chunk_a, chunk_b, chunk = lay(meta, mine, came, small, swap(small, "core"), lengths_a, lengths_b)
        chunk_a, chunk_b, chunk, seg_ids, glob_blocks, blocks_came = stage(
            chunk_a, chunk_b, chunk, seg_ids, glob_blocks, blocks_came
        )
        blocks_mine, blocks_given = pick_blocks(blocks_came)
        segment, globs, lo, n = documents(seg_ids, glob_blocks)

        za = shifts_z(chunk_a, 2, 3)
        both = shift_z(chunk, 1)
        x_came = swap(x_given, "y")
        blocks_came = swap(blocks_given, "y")
        chunk_a, chunk_b, x_came, blocks_came, both, *za = stage(chunk_a, chunk_b, x_came, blocks_came, both, *za)

        near_a = jnp.stack([chunk_a, both[: plan_a.rows]] + za)
        far_a = [swap(near_a, dim) for dim in ("x", "y", "xy")]
        x_own = pair(x_kept, after(x_came, near_a))
        x_oth = swap(x_own, "core")
        zb = [both[plan_a.rows :]] + shifts_z(chunk_b, 2) + shifts_z(after(chunk_b, x_oth), 3)
        tables = spread_tables(model, depth // 2, deep // 2, chunk_b)
        near_a, chunk_b, x_own, x_oth, *rest = stage(near_a, chunk_b, x_own, x_oth, *tables, *far_a, *zb)
        tables, far_a, zb = rest[:4], rest[4:7], rest[7:]
        pieces = [near_a] + far_a

        near_b = jnp.stack([chunk_b] + zb)
        a, b = split_rows(near_b, plan_b.cut)
        a_x, b_y, a_y, b_x = swap(a, "x"), swap(b, "y"), swap(a, "y"), swap(b, "x")
        near_oth = swap(near_b, "core")
        qkv, w_qkv, spread = project_qkv(plan_a, meta, pieces, x_own, x_oth, tables)
        table = jnp.where(c == y, blocks_mine, blocks_came)
        ctx_b, ctx_b_give, lse_b = attention(slice(4, 6), 2, qkv, table)
        d_given, _ = given_kept(after(d_out[:, 0], chunk_b))
        near_b, near_oth, a_x, b_y, a_y, b_x, qkv, ctx_b, ctx_b_give, d_given = stage(
            near_b, near_oth, a_x, b_y, a_y, b_x, qkv, ctx_b, ctx_b_give, d_given
        )

        a_xy, b_yx = swap(a_x, "y"), swap(b_y, "x")
        d_came = swap(d_given, "y")
        early = [a_x, a_y, b_y, b_x]
        early_oth = [swap(v, "core") for v in early]
        ctx_b_oth = swap(ctx_b_give, "core")
        ctx_a, ctx_a_give, lse_a = attention(slice(0, 4), 0, qkv, table)
        a_xy, b_yx, d_came, ctx_b_oth, ctx_a, ctx_a_give, *early_oth = stage(
            a_xy, b_yx, d_came, ctx_b_oth, ctx_a, ctx_a_give, *early_oth
        )
        own_b = [near_b] + early[:2] + [a_xy] + early[2:] + [b_yx]
        oth_b = [near_oth] + early_oth[:2] + [swap(a_xy, "core")] + early_oth[2:] + [swap(b_yx, "core")]
        ctx_a_oth = swap(ctx_a_give, "core")
        found = feed_forward(plan_b, meta, own_b, oth_b, [ctx_a, ctx_b], [ctx_a_oth, ctx_b_oth], x_own.reshape(-1, model),
                             d_came, d_out[:, 0], spread, ffw)
        out_given, out_kept, gr, hid, gf, x1_low, gp, ga, gc_own, gc_oth, context, vg = found

        out_came, gc_came = swap(out_given, "y"), swap(gc_oth, "core")
        grads_own, grads_oth = weight_grads(back_b, meta, hid, gp, gf, x1_low, context, ga)
        out_came, gc_came, *rest = stage(out_came, gc_came, *grads_own, *grads_oth)
        a, a_far, b, b_far, a_oth, a_far_oth, b_oth, b_far_oth = rest
        a_far, b_far = add(a_far, swap(a_far_oth, "core")), add(b_far, swap(b_far_oth, "core"))
        a_far, b_far, gc_came, a_oth, b_oth = stage(a_far, b_far, gc_came, a_oth, b_oth)

        a_came, b_came = swap(a_far, "y"), swap(b_far, "x")
        a_oth, b_oth = swap(a_oth, "core"), swap(b_oth, "core")
        back = lambda p, own, ctx, oth, lse: attention_back(p, qkv, own, gc_came, ctx, oth, lse, table)
        grad_0 = back(0, gc_own, ctx_a, ctx_a_give, lse_a[0:2])
        grad_1 = back(1, after(gc_own, grad_0), ctx_a, ctx_a_give, lse_a[2:4])
        layer_out = pair(out_kept, after(out_came, grad_1))[:, None]
        a_came, b_came, a_oth, b_oth, grad_0, grad_1, gc_own, layer_out = stage(
            a_came, b_came, a_oth, b_oth, grad_0, grad_1, gc_own, layer_out
        )
        a, b = add(a, a_oth, a_came), add(b, b_oth, b_came)
        a_came, b_came = swap(a[ZS:], "x"), swap(b[ZS:], "y")
        (qa, qa_far, qb, qb_far), sums = qkv_grads(back_early, meta, x_own, x_oth, [grad_0, grad_1], 0)
        qa_came, qb_came = swap(qa_far, "y"), swap(qb_far, "x")
        grad_2 = back(2, after(gc_own, sums), ctx_b, ctx_b_give, lse_b)
        a, b, a_came, b_came, qa, qb, qa_came, qb_came, sums, grad_2 = stage(
            a, b, a_came, b_came, qa, qb, qa_came, qb_came, sums, grad_2
        )
        total = jnp.concatenate([add(b[:ZS], b_came), add(a[:ZS], a_came)], axis=1)
        came_b = scatter_z(total, 1)
        ra, ra_far, rb, rb_far = qkv_grads(back_late, meta, x_own, x_oth, [grad_2], 2, sums, vg, tables)
        ra_came, rb_came = swap(ra_far, "y"), swap(rb_far, "x")
        own_given, oth_given = input_grads(meta, [grad_0, grad_1, after(grad_2, ra)], w_qkv, True)
        total, ra, rb, ra_came, rb_came, own_given, oth_given, *came_b = stage(
            total, ra, rb, ra_came, rb_came, own_given, oth_given, *came_b
        )
        came_b += scatter_z(total, 2)
        qa = jnp.concatenate([add(qa, qa_came), add(ra, ra_came)], axis=1)
        qb = jnp.concatenate([add(qb, qb_came), add(rb, rb_came)], axis=1)
        qa_came, qb_came = swap(qa[ZS:], "x"), swap(qb[ZS:], "y")
        gx_given = add(gr[0], own_given, swap(oth_given, "core"))
        gx_came = [swap(gx_given[:EARLY], "y")]
        own_kept, oth_kept = input_grads(meta, [grad_0, grad_1, after(grad_2, qa)], w_qkv, False)
        qa, qb, qa_came, qb_came, own_kept, oth_kept, gx_given, total, *rest = stage(
            qa, qb, qa_came, qb_came, own_kept, oth_kept, gx_given, total, *came_b, *gx_came
        )
        came_b, gx_came = rest[:2] + scatter_z(total, 3), [rest[2], swap(gx_given[EARLY:], "y")]
        total_b = total[0]
        total = jnp.concatenate([add(qb[:ZS], qb_came), add(qa[:ZS], qa_came)], axis=1)
        came = scatter_z(total, 1, 2, 3)
        oth_kept = swap(oth_kept, "core")
        gx_kept = add(gr[1], own_kept, oth_kept)

        def finish(total, lengths):
            mine, theirs, at = [], [], 0
            for length in lengths:
                kept, given = by_parity(total[at : at + length], total[at + length : at + 2 * length])
                mine.append(kept)
                theirs.append(given)
                at += 2 * length
            mine = jnp.concatenate(mine, axis=0)
            came = swap(jnp.concatenate(theirs, axis=0).astype(BF), "core").astype(F32)
            halves, cuts, at = by_parity(mine, came), [], 0
            for length in lengths:
                cuts.append([v[at : at + length] for v in halves])
                at += length
            return cuts

        total, total_b, *rest = stage(total, total_b, *came, *came_b, *gx_came)
        came, came_b, gx_came = rest[:3], rest[3:6], rest[6:]
        cuts_b = finish(added(total_b, *came_b), lengths_b)
        grad_input = pair(gx_kept, jnp.concatenate(gx_came))[:, None]
        total_a = added(total[0], *came)
        ends = (0, depth, depth + 32, 2 * depth + 32, 3 * depth)
        one, three, two, rest = (total_a[i:j] for i, j in zip(ends[:4], ends[1:]))
        total_a = jnp.concatenate([one, two, three, rest, total_a[3 * depth :]])
        cuts_a = finish(total_a, lengths_a)
        kept, given = by_parity(total_a[3 * depth :, :128], total_a[3 * depth :, 128:256])
        small = kept + swap(given, "core")
        small = jnp.concatenate([small[v, :share] for v in range(8)] + [small[8, :share_f]])
    else:
        plan_a, plan_b = Plan(sections_a, None), Plan(sections_b, None)
        everyone = lambda w: lax.all_gather(w, ("dp", "seq"), axis=0, tiled=True)
        full_qkv, full_proj, full_inner, full_down = map(everyone, (qkv_weight, proj_weight, inner_weight, down_weight))
        row = everyone(jnp.concatenate(list(vectors) + [inner_bias])[None])
        full_vectors = row[:, : 8 * share].reshape(members, 8, share).transpose(1, 0, 2).reshape(8, CHIPS, 2, -1)
        full_bias = row[:, 8 * share :].reshape(1, CHIPS, 2, -1)
        padded = lambda v: jnp.pad(v, ((0, 0),) * 3 + ((0, 128 - v.shape[3]),))
        rows = jnp.concatenate([padded(full_vectors), padded(full_bias)], axis=0)
        rows = jnp.pad(rows, ((0, 7), (0, 0), (0, 1), (0, 0))).transpose(1, 0, 2, 3).reshape(CHIPS, 16, 384)

        def packed(h):
            col = lambda w, at, width=half: w[:, at : at + width].reshape(CHIPS, -1, width)
            a = [
                jnp.concatenate([col(full_qkv, model * w + half * h + 128 * p, 128) for w in range(3)], axis=2)
                for p in range(3)
            ]
            b = [col(full_proj, half * h)] + [col(full_inner, ffw // 2 * h + half * g) for g in range(groups)]
            return jnp.concatenate(a + [rows], axis=1), jnp.concatenate(b + [col(full_down, half * h)], axis=1)

        segment, globs, lo, n = documents(seg_ids, glob_blocks)
        zero, one = packed(0), packed(1)
        pieces_a = [jnp.where(even, zero[0], one[0])]
        own_b, oth_b = [[v] for v in by_parity(zero[1], one[1])]
        tables = spread_tables(model, depth // 2, deep // 2)
        x_own = pair(x_kept, swap(x_given, "y"))
        x_oth = swap(x_own, "core")
        d_came = swap(given_kept(d_out[:, 0])[0], "y")
        blocks_mine, blocks_given = pick_blocks(swap(blocks, "core"))
        table = jnp.where(c == y, blocks_mine, swap(blocks_given, "y"))
        qkv, w_qkv, spread = project_qkv(plan_a, meta, pieces_a, x_own, x_oth, tables)
        ctx_a, ctx_a_give, lse_a = attention(slice(0, 4), 0, qkv, table)
        ctx_b, ctx_b_give, lse_b = attention(slice(4, 6), 2, qkv, table)
        ctx_oth = [swap(v, "core") for v in (ctx_a_give, ctx_b_give)]
        found = feed_forward(plan_b, meta, own_b, oth_b, [ctx_a, ctx_b], ctx_oth, x_own.reshape(-1, model), d_came, d_out[:, 0], spread, ffw)
        out_given, out_kept, gr, hid, gf, x1_low, gp, ga, gc_own, gc_oth, context, vg = found
        layer_out = pair(out_kept, swap(out_given, "y"))[:, None]
        gc_came = swap(gc_oth, "core")
        grads_own, grads_oth = weight_grads(plan_b, meta, hid, gp, gf, x1_low, context, ga)
        ctxs = [(ctx_a, ctx_a_give, lse_a[2 * p : 2 * p + 2]) for p in range(2)] + [(ctx_b, ctx_b_give, lse_b)]
        grads = [attention_back(p, qkv, gc_own, gc_came, *ctxs[p], table) for p in range(3)]
        pieces = qkv_grads(plan_a, meta, x_own, x_oth, grads, 0, jnp.zeros((8, 3 * 128), F32), vg, tables)
        own_given, oth_given = input_grads(meta, grads, w_qkv, True)
        own_kept, oth_kept = input_grads(meta, grads, w_qkv, False)
        gx_came = swap(add(gr[0], own_given, swap(oth_given, "core")), "y")
        grad_input = pair(add(gr[1], own_kept, swap(oth_kept, "core")), gx_came)[:, None]
        scatter = lambda v: lax.psum_scatter(v.astype(F32), ("dp", "seq"), scatter_dimension=0, tiled=True)
        found = pieces[0][:, 3 * depth :].astype(F32)
        found = jnp.stack([found[:, :, :128], found[:, :, 128:256]], axis=1).transpose(2, 0, 1, 3)
        small = jnp.concatenate([found[v, :, :, : depth // 2].reshape(-1, 1) for v in range(8)], axis=1)
        small = jnp.concatenate([small.reshape(members, share, 8).transpose(0, 2, 1).reshape(members, -1),
                                 found[8, :, :, : deep // 2].reshape(members, share_f)], axis=1)
        small = scatter(small)[0]
        zero = jnp.zeros((model, half), BF)
        cuts_a, cuts_b = [], []
        for p in range(3):
            part = pieces[0][:, depth * p : depth * p + depth].reshape(-1, half)
            cuts_a.append([scatter(v) for v in by_parity(part, zero)])
        halves, at = by_parity(grads_own[0], grads_oth[0]), 0
        for length in sections_b:
            cuts_b.append([scatter(v[:, at : at + length].reshape(-1, half)) for v in halves])
            at += length

    cut_w = lambda h, p, w: cuts_a[p][h][:, 128 * w : 128 * w + 128]
    grad_qkv = jnp.concatenate([cut_w(h, p, w) for w in range(3) for h in range(2) for p in range(3)], axis=1)
    grad_proj = jnp.concatenate(cuts_b[0], axis=1)
    grad_inner = jnp.concatenate([cuts_b[1 + g][h] for h in range(2) for g in range(groups)], axis=1)
    grad_down = jnp.concatenate(cuts_b[1 + groups], axis=1)
    vector = [small[share * i : share * i + share] for i in range(8)]
    return (
        layer_out,
        grad_input,
        grad_qkv,
        vector[0],
        vector[1],
        grad_proj,
        vector[2],
        vector[3],
        vector[4],
        grad_inner,
        small[8 * share :],
        grad_down,
        vector[5],
        vector[6],
        vector[7],
    )


def solution(mesh):
    row, vec = P(("dp", "seq"), None), P(("dp", "seq"))
    wide = P(None, "dp", "seq", None)
    return jax.shard_map(
        body,
        mesh=mesh,
        in_specs=(wide, row, vec, vec, row, vec, vec, vec, row, vec, row, vec, vec, vec)
        + (P(None, "dp", None), P(None, "dp", "seq", None, None), P(None, "dp", None), wide),
        out_specs=(wide, wide, row, vec, vec, row, vec, vec, vec, row, vec, row, vec, vec, vec),
        check_vma=False,
    )
```
